32 devices in a mesh: groups: 2 (over x), tok: 16 (over z, y, core).
Axes of the slice: x: 2, y: 2, z: 4, core: 2. Of those that a mesh axis runs over, the one named last changes fastest.
Arguments:
- queries: bfloat16 [4096, 2048], P(('groups', 'tok')), parts along dimension 0, may hold values from -6 to 6
- key_matrix: bfloat16 [4096, 512], P(('groups', 'tok')), parts along dimension 0, may hold values from -6 to 6
- value_matrix: bfloat16 [4096, 512], P(('groups', 'tok')), parts along dimension 0, may hold values from -6 to 6
- attention_output: bfloat16 [4096, 2048], P(('groups', 'tok')), parts along dimension 0, may hold values from -3 to 3
- output_gradient: bfloat16 [4096, 2048], P(('groups', 'tok')), parts along dimension 0, may hold values from -48 to 48
- log_sum_norm: float32 [16, 4096], P(None, ('groups', 'tok')), parts along dimension 1, may hold values from 6 to 8
- doc_ids: int32 [4096], P(('groups', 'tok')), parts along dimension 0, may hold values from 0 to 7, never falling along the last dimension, each value on 1 to 1024 neighbouring positions
Outputs:
- query_grad: bfloat16 [4096, 2048], P(('groups', 'tok')), parts along dimension 0
- key_grad: bfloat16 [4096, 512], P(('groups', 'tok')), parts along dimension 0
- value_grad: bfloat16 [4096, 512], P(('groups', 'tok')), parts along dimension 0
The draws below stay inside these ranges and needn't reach their ends.
There are 2 independent parts, one for each index of `groups`. The reference program is written for one: setup_inputs(seed, part) draws one part's arguments, and reference() takes and returns one part's arrays. A program takes and returns all parts, laid end to end along the dimension named above; each array names one. Nothing has to cross between parts.
Inputs may be any that keep to these rules, and one draw needn't show every extreme that they name: `doc_ids`: document ids never fall along the slab; each document has 1 to 1024 tokens and one has exactly 1024.
All inputs are finite; a program needn't handle non-finite values.
Results may differ from the reference program's by a relative error of at most 0.0051.
Values may be sent and summed in bfloat16 or wider, within the bound.
No kernel may reach another device: no remote copies, remote signals or barrier semaphores. Data moves between devices by JAX's collectives and lax.ppermute only.
A program may use at most 128 MiB of HBM per device.

```python
import math
import jax
import jax.numpy as jnp
import numpy as np
from jax import lax

DEVICE_TOKENS = 128
WINDOW = 4096
QUERY_HEADS = 16
KEY_VALUE_HEADS = 4
HEAD_SIZE = 128
DOCS = 8
SLAB_TOKENS = 2048
DOC_MOST = 1024


def steps_of(own_key, extent, split, least, high):
    def one(axis_at, parts):
        steps = jax.random.uniform(jax.random.fold_in(jax.random.fold_in(own_key, 6), axis_at), (parts,), jnp.float32, least / len(split), high / len(split))
        return jnp.repeat(jnp.exp(steps), extent[axis_at] // parts).reshape((-1,) + (1,) * (len(extent) - axis_at - 1))

    loudness = one(*split[0])
    for cut in split[1:]:
        loudness = loudness * one(*cut)
    return loudness


def profile(amount, total, limit, slope):
    loads = [(1 << 20) // math.isqrt(grade ** slope) + 1 for grade in range(2, amount + 1)]
    surplus, counts = total - limit - (amount - 1), [1] * (amount - 1)
    while surplus > 0:
        candidates = [i for i in range(amount - 1) if counts[i] < limit]
        pool, left = sum([loads[i] for i in candidates]), surplus
        for i in candidates:
            extra = min(limit - counts[i], max(1, left * loads[i] // pool), surplus)
            counts[i] = counts[i] + extra
            surplus = surplus - extra
    return np.array([limit] + counts)


def uneven(own_key, amount, total, limit, lean):
    if amount == 2:
        one = jax.random.randint(own_key, (), max(1, total - limit), min(limit, total - 1) + 1)
        return jnp.stack([one, total - one])
    tallies = jnp.asarray(profile(amount, total, limit, lean), jnp.int32)
    pairs = (amount - 1) // 2
    giver, sink = tallies[1:1 + 2 * pairs:2], tallies[2:2 + 2 * pairs:2]
    slack = jnp.minimum(giver - 1, limit - sink)
    passed = jax.random.randint(jax.random.fold_in(own_key, 1), (pairs,), 0, 1 << 20) % (slack + 1)
    tallies = tallies.at[1:1 + 2 * pairs:2].set(giver - passed).at[2:2 + 2 * pairs:2].set(sink + passed)
    return tallies[jax.random.permutation(jax.random.fold_in(own_key, 2), amount)]


def normal_values(key, extent, deviation, most, split=(), kind=jnp.bfloat16):
    result = jax.random.normal(key, extent, jnp.float32) * deviation
    if len(split) > 0:
        result = steps_of(key, extent, split, -0.22, 0.18) * result
    return jnp.clip(result, min=-most, max=most).astype(kind)


def setup_inputs(seed: int = 0, part: int = 0) -> dict:
    streams_of = jax.random.split(jax.random.key(seed), 8)
    own_keys = jax.random.split(jax.random.fold_in(streams_of[7], part), 8)
    queries = normal_values(own_keys[0], (SLAB_TOKENS, QUERY_HEADS * HEAD_SIZE), 1.0, 6.0, ((0, 16),))
    key_matrix = normal_values(own_keys[1], (SLAB_TOKENS, KEY_VALUE_HEADS * HEAD_SIZE), 1.0, 6.0, ((0, 16),))
    value_matrix = normal_values(own_keys[2], (SLAB_TOKENS, KEY_VALUE_HEADS * HEAD_SIZE), 1.0, 6.0, ((0, 16),))
    attention_output = normal_values(own_keys[3], (SLAB_TOKENS, QUERY_HEADS * HEAD_SIZE), 0.5, 3.0, ((0, 16),))
    output_gradient = normal_values(own_keys[4], (SLAB_TOKENS, QUERY_HEADS * HEAD_SIZE), 8.0, 48.0, ((0, 16),))
    log_sum_norm = jnp.clip(6.0 + 2.0 * jax.random.uniform(own_keys[5], (QUERY_HEADS, SLAB_TOKENS), jnp.float32) ** steps_of(own_keys[5], (QUERY_HEADS, SLAB_TOKENS), ((1, 16),), -0.2, 0.2), 6.0, 8.0)
    doc_ids = jnp.searchsorted(jnp.cumsum(uneven(own_keys[6], DOCS, SLAB_TOKENS, DOC_MOST, 2)), jnp.arange(SLAB_TOKENS), side="right").astype(jnp.int32)
    return dict(queries=queries, key_matrix=key_matrix, value_matrix=value_matrix, attention_output=attention_output, output_gradient=output_gradient, log_sum_norm=log_sum_norm, doc_ids=doc_ids)


def reference(queries, key_matrix, value_matrix, attention_output, output_gradient, log_sum_norm, doc_ids):
    group_width = QUERY_HEADS // KEY_VALUE_HEADS
    score_scale = HEAD_SIZE ** -0.5
    key_value_width = KEY_VALUE_HEADS * HEAD_SIZE
    reachable_rows = WINDOW + DEVICE_TOKENS
    padded_key_rows = jnp.concatenate([jnp.zeros((WINDOW, key_value_width), jnp.bfloat16), key_matrix], 0)
    padded_value_rows = jnp.concatenate([jnp.zeros((WINDOW, key_value_width), jnp.bfloat16), value_matrix], 0)
    docs_padded = jnp.concatenate([-jnp.ones((WINDOW,), jnp.int32), doc_ids.astype(jnp.int32)], 0)
    block_count = SLAB_TOKENS // DEVICE_TOKENS

    def block_turn(carried, block_index):
        key_total, value_total = carried
        leading_row = (block_index * DEVICE_TOKENS).astype(jnp.int32)
        query_per_head = lax.dynamic_slice_in_dim(queries, leading_row, DEVICE_TOKENS, 0).astype(jnp.float32).reshape(DEVICE_TOKENS, KEY_VALUE_HEADS, group_width, HEAD_SIZE)
        gradient_per_head = lax.dynamic_slice_in_dim(output_gradient, leading_row, DEVICE_TOKENS, 0).astype(jnp.float32).reshape(DEVICE_TOKENS, KEY_VALUE_HEADS, group_width, HEAD_SIZE)
        output_per_head = lax.dynamic_slice_in_dim(attention_output, leading_row, DEVICE_TOKENS, 0).astype(jnp.float32).reshape(DEVICE_TOKENS, KEY_VALUE_HEADS, group_width, HEAD_SIZE)
        norm_per_head = lax.dynamic_slice_in_dim(log_sum_norm, leading_row, DEVICE_TOKENS, 1).reshape(KEY_VALUE_HEADS, group_width, DEVICE_TOKENS)[..., None]
        key_per_head = lax.dynamic_slice_in_dim(padded_key_rows, leading_row, reachable_rows, 0).astype(jnp.float32).reshape(reachable_rows, KEY_VALUE_HEADS, HEAD_SIZE)
        value_per_head = lax.dynamic_slice_in_dim(padded_value_rows, leading_row, reachable_rows, 0).astype(jnp.float32).reshape(reachable_rows, KEY_VALUE_HEADS, HEAD_SIZE)
        key_docs = lax.dynamic_slice_in_dim(docs_padded, leading_row, reachable_rows, 0)
        query_docs = lax.dynamic_slice_in_dim(doc_ids.astype(jnp.int32), leading_row, DEVICE_TOKENS, 0)
        query_pos = leading_row + jnp.arange(DEVICE_TOKENS, dtype=jnp.int32)
        key_pos = leading_row - WINDOW + jnp.arange(reachable_rows, dtype=jnp.int32)
        gap_rows = query_pos[:, None] - key_pos[None, :]
        live_mask = (gap_rows >= 0) & (gap_rows < WINDOW) & (key_pos[None, :] >= 0) & (query_docs[:, None] == key_docs[None, :])
        delta_per_row = jnp.sum(gradient_per_head * output_per_head, -1).transpose(1, 2, 0)[..., None]
        scores = jnp.einsum('tgrd,kgd->grtk', query_per_head, key_per_head)
        attend = jnp.where(live_mask, jnp.exp(scores * score_scale - norm_per_head), jnp.float32(0.0))
        dprob = jnp.einsum('tgrd,kgd->grtk', gradient_per_head, value_per_head)
        dscore = (attend * (dprob - delta_per_row) * score_scale).astype(jnp.bfloat16).astype(jnp.float32)
        attend_low = attend.astype(jnp.bfloat16).astype(jnp.float32)
        value_part = jnp.einsum('grtk,tgrd->kgd', attend_low, gradient_per_head).reshape(reachable_rows, key_value_width)
        key_part = jnp.einsum('grtk,tgrd->kgd', dscore, query_per_head).reshape(reachable_rows, key_value_width)
        query_part = jnp.einsum('grtk,kgd->tgrd', dscore, key_per_head).reshape(DEVICE_TOKENS, QUERY_HEADS * HEAD_SIZE)
        key_total = lax.dynamic_update_slice_in_dim(key_total, lax.dynamic_slice_in_dim(key_total, leading_row, reachable_rows, 0) + key_part, leading_row, 0)
        value_total = lax.dynamic_update_slice_in_dim(value_total, lax.dynamic_slice_in_dim(value_total, leading_row, reachable_rows, 0) + value_part, leading_row, 0)
        return (key_total, value_total), query_part.astype(jnp.bfloat16)

    start_totals = (jnp.zeros((SLAB_TOKENS + WINDOW, key_value_width), jnp.float32), jnp.zeros((SLAB_TOKENS + WINDOW, key_value_width), jnp.float32))
    totals, query_blocks = lax.scan(block_turn, start_totals, jnp.arange(block_count, dtype=jnp.int32))
    query_grad = query_blocks.reshape(SLAB_TOKENS, QUERY_HEADS * HEAD_SIZE)
    key_grad = totals[0][WINDOW:].astype(jnp.bfloat16)
    value_grad = totals[1][WINDOW:].astype(jnp.bfloat16)
    return (query_grad, key_grad, value_grad)
```

```python
import functools
import math

import jax
import jax.numpy as jnp
from jax import lax
from jax.experimental import pallas as pl
from jax.experimental.pallas import tpu as pltpu
from jax.sharding import PartitionSpec as P

WINDOW = 4096
QUERY_HEADS = 16
KEY_VALUE_HEADS = 4
HEAD_SIZE = 128
GROUP = QUERY_HEADS // KEY_VALUE_HEADS
SCALE = HEAD_SIZE ** (-0.5)
LOG2E = math.log2(math.e)
EXTRA = 8
F32 = jnp.float32
BF16 = jnp.bfloat16

VMEM = pl.BlockSpec(memory_space=pltpu.VMEM)
SMEM = pl.BlockSpec(memory_space=pltpu.SMEM)


def dot(a, b, dims):
    return lax.dot_general(a, b, (dims, ((), ())), preferred_element_type=F32)


def call(kernel, ins, outs, scratch=(), flops=0, name=None):
    size = sum(math.prod(o.shape) * o.dtype.itemsize for o in outs)
    size += sum(math.prod(x.shape) * x.dtype.itemsize for x in ins)
    return pl.pallas_call(
        kernel,
        out_shape=outs,
        in_specs=[SMEM] + [VMEM] * (len(ins) - 1),
        out_specs=[VMEM] * len(outs),
        scratch_shapes=list(scratch),
        cost_estimate=pl.CostEstimate(flops=flops, bytes_accessed=size, transcendentals=0),
        compiler_params=pltpu.CompilerParams(vmem_limit_bytes=48 << 20),
        name=name,
    )(*ins)


def pack_keys(rows, place, key_ref, value_ref, doc_ref, *outs):
    docs = jnp.broadcast_to((doc_ref[...] + 1).astype(F32), (EXTRA, rows)).astype(BF16)
    for s, out in enumerate(outs):
        cut = pl.ds(pl.multiple_of((place[1] ^ s) * HEAD_SIZE, HEAD_SIZE), HEAD_SIZE)
        out[0:rows, 0:HEAD_SIZE] = key_ref[:, cut]
        out[0:rows, HEAD_SIZE:] = value_ref[:, cut]
        out[rows:, 0:rows] = docs


def pack_queries(rows, place, query_ref, grad_ref, output_ref, norm_ref, *rest):
    outs, stats = rest[:-1], rest[-1]
    lane = lax.broadcasted_iota(jnp.int32, (rows, HEAD_SIZE), 1)
    columns = jnp.zeros((rows, HEAD_SIZE), F32)
    for h in range(QUERY_HEADS):
        cut = slice(h * HEAD_SIZE, (h + 1) * HEAD_SIZE)
        product = grad_ref[:, cut].astype(F32) * output_ref[:, cut].astype(F32)
        columns = jnp.where(lane == h, jnp.sum(product, 1, keepdims=True), columns)
    delta = columns.T
    for g in range(KEY_VALUE_HEADS):
        stats[g, 0:GROUP, :] = norm_ref[g * GROUP : (g + 1) * GROUP, :]
        stats[g, GROUP : 2 * GROUP, :] = delta[g * GROUP : (g + 1) * GROUP, :]
    width = GROUP * HEAD_SIZE
    for s, out in enumerate(outs):
        g = place[1] ^ s
        cut = pl.ds(pl.multiple_of(g * width, width), width)
        out[0:rows, 0:width] = query_ref[:, cut]
        out[0:rows, width:] = grad_ref[:, cut]
        left = stats[g]
        for part in range(3):
            term = left.astype(BF16)
            out[rows:, part * rows : (part + 1) * rows] = term
            left = left - term.astype(F32)


def join(rows, place, *refs):
    pieces, out = refs[:-1], refs[-1]
    block = rows + EXTRA
    for s, piece in enumerate(pieces):
        out[place[1] ^ s] = piece[...]


def attend(rows, offsets, reach, first, last, place, *refs):
    parts = KEY_VALUE_HEADS
    queries, refs = refs[:parts], refs[parts:]
    own, refs = refs[0], refs[1:]
    keys, refs = refs[: len(offsets)], refs[len(offsets) :]
    if not first:
        dq_in, refs = refs[0], refs[1:]
    if last:
        dq_out, refs = refs[:parts], refs[parts:]
    else:
        dq_out, refs = refs[0], refs[1:]
    kv_out, refs = refs[: len(offsets)], refs[len(offsets) :]
    stack_q, stack_g, stats, dq, dkv = refs
    row, me = place[0], place[1]
    width = GROUP * HEAD_SIZE
    span = parts * rows
    for s in range(parts):
        for h in range(GROUP):
            cut = slice(h * HEAD_SIZE, (h + 1) * HEAD_SIZE)
            stack_q[s, h * rows : (h + 1) * rows, :] = queries[s][0:rows, cut]
            cut = slice(width + h * HEAD_SIZE, width + (h + 1) * HEAD_SIZE)
            stack_g[s, h * rows : (h + 1) * rows, :] = queries[s][0:rows, cut]
        total = queries[s][rows:, 0:rows].astype(F32)
        total = total + queries[s][rows:, rows : 2 * rows].astype(F32)
        total = total + queries[s][rows:, 2 * rows : 3 * rows].astype(F32)
        stats[s] = total
    if first:
        dq[...] = jnp.zeros_like(dq)
    else:
        dq[...] = dq_in[...]
    for at, offset in enumerate(offsets):
        dkv[...] = jnp.zeros_like(dkv)

        def key_block(b, carry, at=at, offset=offset):
            key_rows = keys[at][b]
            key = key_rows[0:rows, 0:HEAD_SIZE]
            value = key_rows[0:rows, HEAD_SIZE:]
            key_docs = jnp.broadcast_to(key_rows[rows : rows + 1, 0:rows].astype(F32), (rows, rows)).T
            for s in range(parts):
                a = me ^ s
                near = offset * span + (a - b) * rows
                live = (near + rows - 1 >= 0) & (near - rows + 1 < reach) & (row >= offset)

                @pl.when(live)
                def _():
                    docs = own[a, rows : rows + 1, 0:rows].astype(F32)
                    gap = (
                        near
                        + lax.broadcasted_iota(jnp.int32, (rows, rows), 1)
                        - lax.broadcasted_iota(jnp.int32, (rows, rows), 0)
                    )
                    mask = key_docs == docs
                    if offset == 0:
                        mask = mask & (gap >= 0)
                    if (offset + 1) * span > WINDOW:
                        mask = mask & (gap < WINDOW)
                    query = stack_q[s]
                    grad = stack_g[s]
                    scores = dot(key, query, ((1,), (1,)))
                    dprob = dot(value, grad, ((1,), (1,)))
                    probs, dscores = [], []
                    for h in range(GROUP):
                        cut = slice(h * rows, (h + 1) * rows)
                        norm = stats[s, h : h + 1, :] * LOG2E
                        delta = stats[s, GROUP + h : GROUP + h + 1, :]
                        prob = jnp.exp2(scores[:, cut] * (SCALE * LOG2E) - norm)
                        prob = jnp.where(mask, prob, 0.0)
                        probs.append(prob.astype(BF16))
                        dscores.append((prob * (dprob[:, cut] - delta) * SCALE).astype(BF16))
                    prob = jnp.concatenate(probs, 1)
                    dscore = jnp.concatenate(dscores, 1)
                    dkv[b, :, 0:HEAD_SIZE] += dot(dscore, query, ((1,), (0,)))
                    dkv[b, :, HEAD_SIZE:] += dot(prob, grad, ((1,), (0,)))
                    dq[s] += dot(dscore, key, ((0,), (0,)))

            return carry

        lax.fori_loop(0, parts, key_block, 0)
        kv_out[at][...] = dkv[...].astype(kv_out[at].dtype)
    if last:
        for s in range(parts):
            for h in range(GROUP):
                cut = slice(h * HEAD_SIZE, (h + 1) * HEAD_SIZE)
                dq_out[s][:, cut] = dq[s, h * rows : (h + 1) * rows, :].astype(BF16)
    else:
        dq_out[...] = dq[...]


def add_terms(place, *refs):
    parts = KEY_VALUE_HEADS
    terms, outs = refs[:-parts], refs[-parts:]
    for s, out in enumerate(outs):
        b = place[1] ^ s
        total = terms[0][b]
        for term in terms[1:]:
            total = total + term[b].astype(F32)
        out[...] = total.astype(BF16)


def spread(place, *refs):
    parts = KEY_VALUE_HEADS
    pieces, outs = refs[:parts], refs[parts:]
    width = pieces[0].shape[1] // len(outs)
    for s, piece in enumerate(pieces):
        cut = pl.ds(pl.multiple_of((place[1] ^ s) * width, width), width)
        for k, out in enumerate(outs):
            out[:, cut] = piece[:, k * width : (k + 1) * width]


def local(
    queries, key_matrix, value_matrix, attention_output, output_gradient, log_sum_norm, doc_ids
):
    parts = KEY_VALUE_HEADS
    rows = queries.shape[0]
    count = lax.axis_size("tok")
    span = parts * rows
    reach = min(WINDOW, count * rows // 2)
    behind = min(-(-(reach - 1) // span), count // parts - 1)
    device = lax.axis_index("tok")
    place = jnp.stack([device // parts, device % parts]).astype(jnp.int32)
    width = GROUP * HEAD_SIZE
    shape = jax.ShapeDtypeStruct

    def across(value, s):
        return lax.ppermute(value, "tok", [(t, t ^ s) for t in range(count)])

    def along(value, steps):
        pairs = [(t, t + steps * parts) for t in range(count)]
        return lax.ppermute(value, "tok", [(a, b) for a, b in pairs if 0 <= b < count])

    def exchange(pieces):
        return [pieces[0]] + [across(pieces[s], s) for s in range(1, parts)]

    block = rows + EXTRA
    pieces = call(
        functools.partial(pack_keys, rows),
        (place, key_matrix, value_matrix, doc_ids.reshape(1, rows)),
        [shape((block, 2 * HEAD_SIZE), BF16)] * parts,
        name="pack_keys",
    )
    pieces = exchange(pieces)
    (own,) = call(
        functools.partial(join, rows),
        (place, *pieces),
        [shape((parts, block, 2 * HEAD_SIZE), BF16)],
        name="join",
    )
    query_pieces = call(
        functools.partial(pack_queries, rows),
        (place, queries, output_gradient, attention_output, log_sum_norm),
        [shape((block, 2 * width), BF16)] * parts,
        scratch=[pltpu.VMEM((parts, 2 * GROUP, rows), F32)],
        name="pack_queries",
    )
    query_pieces = exchange(query_pieces)
    windows = [own]
    for _ in range(behind):
        windows.append(along(windows[-1], 1))

    kv_shape = (parts, rows, 2 * HEAD_SIZE)
    stages = [tuple(range(min(2, behind + 1)))] + [(d,) for d in range(2, behind + 1)]
    dq, terms = None, []
    for k, offsets in enumerate(stages):
        first, last = k == 0, k == len(stages) - 1
        ins = [place, *query_pieces, own, *[windows[d] for d in offsets]]
        if not first:
            ins.append(dq)
        if last:
            outs = [shape((rows, width), BF16)] * parts
        else:
            outs = [shape((parts, GROUP * rows, HEAD_SIZE), F32)]
        outs = outs + [shape(kv_shape, F32 if d == 0 else BF16) for d in offsets]
        got = call(
            functools.partial(attend, rows, offsets, reach, first, last),
            ins,
            outs,
            scratch=[
                pltpu.VMEM((parts, GROUP * rows, HEAD_SIZE), BF16),
                pltpu.VMEM((parts, GROUP * rows, HEAD_SIZE), BF16),
                pltpu.VMEM((parts, 2 * GROUP, rows), F32),
                pltpu.VMEM((parts, GROUP * rows, HEAD_SIZE), F32),
                pltpu.VMEM(kv_shape, F32),
            ],
            flops=10 * len(offsets) * span * span * GROUP * HEAD_SIZE,
            name="attend_" + "_".join(map(str, offsets)),
        )
        dq = got[:parts] if last else got[0]
        for d, term in zip(offsets, got[-len(offsets) :]):
            terms.append(term if d == 0 else along(term, -d))

    (query_grad,) = call(
        spread, (place, *exchange(dq)), [shape((rows, parts * width), BF16)], name="spread_queries"
    )
    pieces = call(
        add_terms, (place, *terms), [shape((rows, 2 * HEAD_SIZE), BF16)] * parts, name="add_terms"
    )
    key_grad, value_grad = call(
        spread,
        (place, *exchange(pieces)),
        [shape((rows, parts * HEAD_SIZE), BF16)] * 2,
        name="spread_keys",
    )
    return query_grad, key_grad, value_grad


def solution(mesh):
    axes = ("groups", "tok")
    return jax.shard_map(
        local,
        mesh=mesh,
        in_specs=(
            P(axes, None),
            P(axes, None),
            P(axes, None),
            P(axes, None),
            P(axes, None),
            P(None, axes),
            P(axes),
        ),
        out_specs=(P(axes, None), P(axes, None), P(axes, None)),
        check_vma=False,
    )
```

```python
import functools
import math

import jax
import jax.numpy as jnp
from jax import lax
from jax.experimental import pallas as pl
from jax.experimental.pallas import tpu as pltpu
from jax.sharding import PartitionSpec as P

WINDOW = 4096
QUERY_HEADS = 16
KEY_VALUE_HEADS = 4
HEAD_SIZE = 128
GROUP = QUERY_HEADS // KEY_VALUE_HEADS
SCALE = HEAD_SIZE ** (-0.5)
LOG2E = math.log2(math.e)
EXTRA = 8
F32 = jnp.float32
BF16 = jnp.bfloat16

VMEM = pl.BlockSpec(memory_space=pltpu.VMEM)
SMEM = pl.BlockSpec(memory_space=pltpu.SMEM)


def dot(a, b, dims):
    return lax.dot_general(a, b, (dims, ((), ())), preferred_element_type=F32)


HBM = pl.BlockSpec(memory_space=pltpu.MemorySpace.HBM)
ANY = pl.BlockSpec(memory_space=pl.ANY)


def call(kernel, ins, outs, scratch=(), flops=0, name=None, specs=None):
    size = sum(math.prod(o.shape) * o.dtype.itemsize for o in outs)
    size += sum(math.prod(x.shape) * x.dtype.itemsize for x in ins)
    return pl.pallas_call(
        kernel,
        out_shape=outs,
        in_specs=[SMEM] + (specs or [VMEM] * (len(ins) - 1)),
        out_specs=[VMEM] * len(outs),
        scratch_shapes=list(scratch),
        cost_estimate=pl.CostEstimate(flops=flops, bytes_accessed=size, transcendentals=0),
        compiler_params=pltpu.CompilerParams(vmem_limit_bytes=48 << 20),
        name=name,
    )(*ins)


def head_columns(g):
    return pl.ds(pl.multiple_of(g * HEAD_SIZE, HEAD_SIZE), HEAD_SIZE)


def pack_keys(rows, place, key_ref, value_ref, doc_ref, *rest):
    outs, sems = rest[:-1], rest[-1]
    copies = []
    for s, out in enumerate(outs):
        cut = head_columns(place[1] ^ s)
        for k, source in enumerate((key_ref, value_ref)):
            target = out.at[k * rows : (k + 1) * rows, :]
            copies.append(pltpu.make_async_copy(source.at[:, cut], target, sems.at[s, k]))
    for copy in copies:
        copy.start()
    docs = jnp.broadcast_to((doc_ref[...] + 1).astype(F32), (EXTRA, rows)).astype(BF16)
    for out in outs:
        out[2 * rows :, 0:rows] = docs
    for copy in copies:
        copy.wait()


def pack_queries(rows, place, query_ref, grad_ref, output_ref, norm_ref, *rest):
    outs, (grads, outputs, stats, sems, more_sems) = rest[:-5], rest[-5:]
    first = pltpu.make_async_copy(grad_ref, grads, more_sems.at[0])
    second = pltpu.make_async_copy(output_ref, outputs, more_sems.at[1])
    first.start()
    second.start()
    copies = []
    for s, out in enumerate(outs):
        for h in range(GROUP):
            cut = head_columns((place[1] ^ s) * GROUP + h)
            for k, source in enumerate((query_ref, grad_ref)):
                at = (k * GROUP + h) * rows
                target = out.at[at : at + rows, :]
                copies.append(pltpu.make_async_copy(source.at[:, cut], target, sems.at[s, k, h]))
    for copy in copies:
        copy.start()
    first.wait()
    second.wait()
    lane = lax.broadcasted_iota(jnp.int32, (rows, HEAD_SIZE), 1)
    columns = jnp.zeros((rows, HEAD_SIZE), F32)
    for h in range(QUERY_HEADS):
        cut = slice(h * HEAD_SIZE, (h + 1) * HEAD_SIZE)
        product = grads[:, cut].astype(F32) * outputs[:, cut].astype(F32)
        columns = jnp.where(lane == h, jnp.sum(product, 1, keepdims=True), columns)
    delta = columns.T
    for g in range(KEY_VALUE_HEADS):
        stats[g, 0:GROUP, :] = norm_ref[g * GROUP : (g + 1) * GROUP, :]
        stats[g, GROUP : 2 * GROUP, :] = delta[g * GROUP : (g + 1) * GROUP, :]
    for s, out in enumerate(outs):
        left = stats[place[1] ^ s]
        for part in range(3):
            term = left.astype(BF16)
            at = 2 * GROUP * rows + part * EXTRA
            out[at : at + EXTRA, 0:rows] = term
            left = left - term.astype(F32)
    for copy in copies:
        copy.wait()


def join(rows, place, *refs):
    parts = KEY_VALUE_HEADS
    pieces, out = refs[:parts], refs[-1]
    span = parts * rows
    for s, piece in enumerate(pieces):
        a = place[1] ^ s
        for k in range(2):
            at = pl.multiple_of(k * span + a * rows, rows)
            out[pl.ds(at, rows), :] = piece[k * rows : (k + 1) * rows, :]
        at = pl.multiple_of(2 * span + a * EXTRA, EXTRA)
        out[pl.ds(at, EXTRA), :] = piece[2 * rows :, :]


def attend_scratch(rows):
    parts = KEY_VALUE_HEADS
    return [
        pltpu.VMEM((parts, HEAD_SIZE, GROUP * rows), F32),
        pltpu.VMEM((2 * parts * rows, HEAD_SIZE), F32),
        pltpu.VMEM((HEAD_SIZE, parts * rows), BF16),
        pltpu.VMEM((parts * rows, rows), F32),
        pltpu.SMEM((2 * parts,), F32),
    ]


def attend(rows, offsets, reach, first, last, place, *refs):
    parts = KEY_VALUE_HEADS
    queries, refs = refs[:parts], refs[parts:]
    own, refs = refs[0], refs[1:]
    keys, refs = refs[: len(offsets)], refs[len(offsets) :]
    if not first:
        dq_in, refs = refs[0], refs[1:]
    if last:
        dq_out, refs = refs[:parts], refs[parts:]
    else:
        dq_out, refs = refs[0], refs[1:]
    kv_out, refs = refs[: len(offsets)], refs[len(offsets) :]
    dq, dkv, key_t, docs_t, docs_s = refs
    row, me = place[0], place[1]
    width = GROUP * rows
    span = parts * rows
    for a in range(parts):
        docs = own[2 * span + a * EXTRA : 2 * span + a * EXTRA + 1, 0:rows].astype(F32)
        docs_s[a] = jnp.min(docs)
    dq[...] = jnp.zeros_like(dq)
    for at, offset in enumerate(offsets):
        dkv[...] = jnp.zeros_like(dkv)
        key_ref = keys[at]
        for b in range(parts):
            cut = slice(b * rows, (b + 1) * rows)
            key_t[:, cut] = key_ref[cut, :].T
            docs = key_ref[2 * span + b * EXTRA : 2 * span + b * EXTRA + 1, 0:rows].astype(F32)
            docs_t[cut, :] = jnp.broadcast_to(docs, (rows, rows)).T
            if b == parts - 1:
                docs_s[parts] = jnp.max(docs)
        for s in range(parts):
            a = me ^ s
            near = offset * span + a * rows
            live = (near - span + 1 < reach) & (row >= offset) & (docs_s[a] <= docs_s[parts])

            @pl.when(live)
            def _(s=s, a=a, near=near, key_ref=key_ref, offset=offset):
                docs = own[pl.ds(pl.multiple_of(2 * span + a * EXTRA, EXTRA), EXTRA), :]
                docs = docs.astype(F32)[0:1, 0:rows]
                query = queries[s][0:width, :]
                grad = queries[s][width : 2 * width, :]
                stats = queries[s][2 * width :, :].astype(F32)
                stats = stats[0:EXTRA] + stats[EXTRA : 2 * EXTRA] + stats[2 * EXTRA :]
                gap = (
                    near
                    + lax.broadcasted_iota(jnp.int32, (span, rows), 1)
                    - lax.broadcasted_iota(jnp.int32, (span, rows), 0)
                )
                mask = docs_t[...] == docs
                if offset == 0:
                    mask = mask & (gap >= 0)
                if (offset + 1) * span > WINDOW:
                    mask = mask & (gap < WINDOW)
                scores = dot(key_ref[0:span, :], query, ((1,), (1,)))
                dprob = dot(key_ref[span : 2 * span, :], grad, ((1,), (1,)))
                probs, dscores = [], []
                for h in range(GROUP):
                    cut = slice(h * rows, (h + 1) * rows)
                    norm = stats[h : h + 1, :] * LOG2E
                    delta = stats[GROUP + h : GROUP + h + 1, :]
                    prob = jnp.exp2(scores[:, cut] * (SCALE * LOG2E) - norm)
                    prob = jnp.where(mask, prob, 0.0)
                    probs.append(prob.astype(BF16))
                    dscores.append((prob * (dprob[:, cut] - delta) * SCALE).astype(BF16))
                prob = jnp.concatenate(probs, 1)
                dscore = jnp.concatenate(dscores, 1)
                dkv[0:span, :] += dot(dscore, query, ((1,), (0,)))
                dkv[span:, :] += dot(prob, grad, ((1,), (0,)))
                dq[s] += dot(key_t[...], dscore, ((1,), (0,)))

        kv_out[at][...] = dkv[...].astype(kv_out[at].dtype)
    for s in range(parts):
        total = dq[s] if first else dq[s] + dq_in[s]
        if last:
            dq_out[s][...] = total.astype(BF16)
        else:
            dq_out[s] = total


def add_terms(rows, count, place, *refs):
    parts = KEY_VALUE_HEADS
    terms, outs = refs[:count], refs[-parts:]
    for s, out in enumerate(outs):
        for k in range(2):
            at = pl.multiple_of((k * parts + (place[1] ^ s)) * rows, rows)
            total = terms[0][pl.ds(at, rows), :]
            for term in terms[1:]:
                total = total + term[pl.ds(at, rows), :].astype(F32)
            out[k * rows : (k + 1) * rows, :] = total.astype(BF16)


def spread_queries(rows, place, *refs):
    pieces, out = refs[:-1], refs[-1]
    for s, piece in enumerate(pieces):
        for h in range(GROUP):
            cut = head_columns((place[1] ^ s) * GROUP + h)
            out[:, cut] = piece[:, h * rows : (h + 1) * rows].T


def spread_keys(rows, place, *refs):
    pieces, outs = refs[:-2], refs[-2:]
    for s, piece in enumerate(pieces):
        for k, out in enumerate(outs):
            out[:, head_columns(place[1] ^ s)] = piece[k * rows : (k + 1) * rows, :]


def local(
    queries, key_matrix, value_matrix, attention_output, output_gradient, log_sum_norm, doc_ids
):
    parts = KEY_VALUE_HEADS
    rows = queries.shape[0]
    count = lax.axis_size("tok")
    span = parts * rows
    reach = min(WINDOW, count * rows // 2)
    behind = min(-(-(reach - 1) // span), count // parts - 1)
    device = lax.axis_index("tok")
    place = jnp.stack([device // parts, device % parts]).astype(jnp.int32)
    width = GROUP * rows
    shape = jax.ShapeDtypeStruct

    def across(value, s):
        return lax.ppermute(value, "tok", [(t, t ^ s) for t in range(count)])

    def along(value, steps):
        pairs = [(t, t + steps * parts) for t in range(count)]
        return lax.ppermute(value, "tok", [(a, b) for a, b in pairs if 0 <= b < count])

    def exchange(pieces):
        return [pieces[0]] + [across(pieces[s], s) for s in range(1, parts)]

    pieces = call(
        functools.partial(pack_keys, rows),
        (place, key_matrix, value_matrix, doc_ids.reshape(1, rows)),
        [shape((2 * rows + EXTRA, HEAD_SIZE), BF16)] * parts,
        scratch=[pltpu.SemaphoreType.DMA((parts, 2))],
        specs=[HBM, HBM, VMEM],
        name="pack_keys",
    )
    pieces = exchange(pieces)
    query_pieces = call(
        functools.partial(pack_queries, rows),
        (place, queries, output_gradient, attention_output, log_sum_norm),
        [shape((2 * width + 3 * EXTRA, HEAD_SIZE), BF16)] * parts,
        scratch=[
            pltpu.VMEM(queries.shape, BF16),
            pltpu.VMEM(queries.shape, BF16),
            pltpu.VMEM((parts, 2 * GROUP, rows), F32),
            pltpu.SemaphoreType.DMA((parts, 2, GROUP)),
            pltpu.SemaphoreType.DMA((2,)),
        ],
        specs=[HBM, HBM, HBM, VMEM],
        name="pack_queries",
    )
    (own,) = call(
        functools.partial(join, rows),
        (place, *pieces, query_pieces[0]),
        [shape((parts * (2 * rows + EXTRA), HEAD_SIZE), BF16)],
        specs=[VMEM] * parts + [ANY],
        name="join",
    )
    query_pieces = exchange(query_pieces)
    windows = [own]
    for _ in range(behind):
        windows.append(along(windows[-1], 1))

    kv_shape = (2 * span, HEAD_SIZE)
    stages = [tuple(range(min(2, behind + 1)))] + [(d,) for d in range(2, behind + 1)]
    dq, terms = None, []
    for k, offsets in enumerate(stages):
        first, last = k == 0, k == len(stages) - 1
        ins = [place, *query_pieces, own, *[windows[d] for d in offsets]]
        if not first:
            ins.append(dq)
        if last:
            outs = [shape((HEAD_SIZE, width), BF16)] * parts
        else:
            outs = [shape((parts, HEAD_SIZE, width), F32)]
        outs = outs + [shape(kv_shape, F32 if d == 0 else BF16) for d in offsets]
        got = call(
            functools.partial(attend, rows, offsets, reach, first, last),
            ins,
            outs,
            scratch=attend_scratch(rows),
            flops=10 * len(offsets) * span * span * GROUP * HEAD_SIZE,
            name="attend_" + "_".join(map(str, offsets)),
        )
        dq = got[:parts] if last else got[0]
        for d, term in zip(offsets, got[-len(offsets) :]):
            terms.append(term if d == 0 else along(term, -d))

    (query_grad,) = call(
        functools.partial(spread_queries, rows),
        (place, *exchange(dq)),
        [shape((rows, parts * GROUP * HEAD_SIZE), BF16)],
        name="spread_queries",
    )
    pieces = call(
        functools.partial(add_terms, rows, len(terms)),
        (place, *terms, query_grad),
        [shape((2 * rows, HEAD_SIZE), BF16)] * parts,
        specs=[VMEM] * len(terms) + [ANY],
        name="add_terms",
    )
    key_grad, value_grad = call(
        functools.partial(spread_keys, rows),
        (place, *exchange(pieces)),
        [shape((rows, parts * HEAD_SIZE), BF16)] * 2,
        name="spread_keys",
    )
    return query_grad, key_grad, value_grad


def solution(mesh):
    axes = ("groups", "tok")
    return jax.shard_map(
        local,
        mesh=mesh,
        in_specs=(
            P(axes, None),
            P(axes, None),
            P(axes, None),
            P(axes, None),
            P(axes, None),
            P(None, axes),
            P(axes),
        ),
        out_specs=(P(axes, None), P(axes, None), P(axes, None)),
        check_vma=False,
    )
```

```python
import functools
import math

import jax
import jax.numpy as jnp
from jax import lax
from jax.experimental import pallas as pl
from jax.experimental.pallas import tpu as pltpu
from jax.sharding import PartitionSpec as P

WINDOW = 4096
QUERY_HEADS = 16
KEY_VALUE_HEADS = 4
HEAD_SIZE = 128
GROUP = QUERY_HEADS // KEY_VALUE_HEADS
SCALE = HEAD_SIZE ** (-0.5)
LOG2E = math.log2(math.e)
EXTRA = 8
F32 = jnp.float32
BF16 = jnp.bfloat16

VMEM = pl.BlockSpec(memory_space=pltpu.VMEM)
SMEM = pl.BlockSpec(memory_space=pltpu.SMEM)


def dot(a, b, dims):
    return lax.dot_general(a, b, (dims, ((), ())), preferred_element_type=F32)


HBM = pl.BlockSpec(memory_space=pltpu.MemorySpace.HBM)
TOKEN = jax.ShapeDtypeStruct((8, 128), F32)


def call(kernel, ins, outs, scratch=(), flops=0, name=None, specs=None, out_specs=None):
    specs = specs or [VMEM] * (len(ins) - 1)
    ins = [ins[0]] + [
        pltpu.with_memory_space_constraint(x, pltpu.MemorySpace.HBM) if spec is HBM else x
        for x, spec in zip(ins[1:], specs)
    ]
    size = sum(math.prod(o.shape) * o.dtype.itemsize for o in outs)
    size += sum(math.prod(x.shape) * x.dtype.itemsize for x in ins)
    return pl.pallas_call(
        kernel,
        out_shape=outs,
        in_specs=[SMEM] + specs,
        out_specs=out_specs or [VMEM] * len(outs),
        scratch_shapes=list(scratch),
        cost_estimate=pl.CostEstimate(flops=flops, bytes_accessed=size, transcendentals=0),
        compiler_params=pltpu.CompilerParams(vmem_limit_bytes=48 << 20),
        name=name,
    )(*ins)


def head_columns(g):
    return pl.ds(pl.multiple_of(g * HEAD_SIZE, HEAD_SIZE), HEAD_SIZE)


def pack_keys(rows, place, key_ref, value_ref, doc_ref, *rest):
    outs, (ids, doc_sem, sems) = rest[:-3], rest[-3:]
    first = pltpu.make_async_copy(doc_ref, ids, doc_sem)
    first.start()
    copies = []
    for s, out in enumerate(outs):
        cut = head_columns(place[1] ^ s)
        for k, source in enumerate((key_ref, value_ref)):
            target = out.at[k * rows : (k + 1) * rows, :]
            copies.append(pltpu.make_async_copy(source.at[:, cut], target, sems.at[s, k]))
    for copy in copies:
        copy.start()
    first.wait()
    docs = jnp.broadcast_to((ids[...] + 1).astype(F32), (EXTRA, rows)).astype(BF16)
    for out in outs:
        out[2 * rows :, 0:rows] = docs
    for copy in copies:
        copy.wait()


def pack_queries(rows, place, query_ref, grad_ref, output_ref, norm_ref, *rest):
    outs, (token, grads, outputs, stats, sems, more_sems) = rest[:-6], rest[-6:]
    first = pltpu.make_async_copy(grad_ref, grads, more_sems.at[0])
    second = pltpu.make_async_copy(output_ref, outputs, more_sems.at[1])
    first.start()
    second.start()
    copies = []
    for s, out in enumerate(outs):
        for h in range(GROUP):
            cut = head_columns((place[1] ^ s) * GROUP + h)
            for k, source in enumerate((query_ref, grad_ref)):
                at = (k * GROUP + h) * rows
                target = out.at[at : at + rows, :]
                copies.append(pltpu.make_async_copy(source.at[:, cut], target, sems.at[s, k, h]))
    for copy in copies:
        copy.start()
    first.wait()
    second.wait()
    lane = lax.broadcasted_iota(jnp.int32, (rows, HEAD_SIZE), 1)
    columns = jnp.zeros((rows, HEAD_SIZE), F32)
    for h in range(QUERY_HEADS):
        cut = slice(h * HEAD_SIZE, (h + 1) * HEAD_SIZE)
        product = grads[:, cut].astype(F32) * outputs[:, cut].astype(F32)
        columns = jnp.where(lane == h, jnp.sum(product, 1, keepdims=True), columns)
    delta = columns.T
    for g in range(KEY_VALUE_HEADS):
        stats[g, 0:GROUP, :] = norm_ref[g * GROUP : (g + 1) * GROUP, :]
        stats[g, GROUP : 2 * GROUP, :] = delta[g * GROUP : (g + 1) * GROUP, :]
    for s, out in enumerate(outs):
        left = stats[place[1] ^ s]
        for part in range(3):
            term = left.astype(BF16)
            at = 2 * GROUP * rows + part * EXTRA
            out[at : at + EXTRA, 0:rows] = term
            left = left - term.astype(F32)
    for copy in copies:
        copy.wait()
    token[...] = jnp.zeros_like(token)


def join(rows, place, *refs):
    parts = KEY_VALUE_HEADS
    pieces, out = refs[:parts], refs[-1]
    span = parts * rows
    for s, piece in enumerate(pieces):
        a = place[1] ^ s
        for k in range(2):
            at = pl.multiple_of(k * span + a * rows, rows)
            out[pl.ds(at, rows), :] = piece[k * rows : (k + 1) * rows, :]
        at = pl.multiple_of(2 * span + a * EXTRA, EXTRA)
        out[pl.ds(at, EXTRA), :] = piece[2 * rows :, :]


def attend_scratch(rows):
    parts = KEY_VALUE_HEADS
    return [
        pltpu.VMEM((parts, HEAD_SIZE, GROUP * rows), F32),
        pltpu.VMEM((2 * parts * rows, HEAD_SIZE), F32),
        pltpu.VMEM((HEAD_SIZE, parts * rows), BF16),
        pltpu.VMEM((parts * rows, rows), F32),
        pltpu.SMEM((2 * parts,), F32),
    ]


def attend(rows, offsets, reach, first, last, place, *refs):
    parts = KEY_VALUE_HEADS
    queries, refs = refs[:parts], refs[parts:]
    own, refs = refs[0], refs[1:]
    keys, refs = refs[: len(offsets)], refs[len(offsets) :]
    if not first:
        dq_in, refs = refs[0], refs[1:]
    if last:
        dq_out, refs = refs[:parts], refs[parts:]
    else:
        dq_out, refs = refs[0], refs[1:]
    kv_out, refs = refs[: len(offsets)], refs[len(offsets) :]
    dq, dkv, key_t, docs_t, docs_s = refs
    row, me = place[0], place[1]
    width = GROUP * rows
    span = parts * rows
    for a in range(parts):
        docs = own[2 * span + a * EXTRA : 2 * span + a * EXTRA + 1, 0:rows].astype(F32)
        docs_s[a] = jnp.min(docs)
    dq[...] = jnp.zeros_like(dq)
    for at, offset in enumerate(offsets):
        dkv[...] = jnp.zeros_like(dkv)
        key_ref = keys[at]
        for b in range(parts):
            cut = slice(b * rows, (b + 1) * rows)
            key_t[:, cut] = key_ref[cut, :].T
            docs = key_ref[2 * span + b * EXTRA : 2 * span + b * EXTRA + 1, 0:rows].astype(F32)
            docs_t[cut, :] = jnp.broadcast_to(docs, (rows, rows)).T
            if b == parts - 1:
                docs_s[parts] = jnp.max(docs)
        for s in range(parts):
            a = me ^ s
            near = offset * span + a * rows
            live = (near - span + 1 < reach) & (row >= offset) & (docs_s[a] <= docs_s[parts])

            @pl.when(live)
            def _(s=s, a=a, near=near, key_ref=key_ref, offset=offset):
                docs = own[pl.ds(pl.multiple_of(2 * span + a * EXTRA, EXTRA), EXTRA), :]
                docs = docs.astype(F32)[0:1, 0:rows]
                query = queries[s][0:width, :]
                grad = queries[s][width : 2 * width, :]
                stats = queries[s][2 * width :, :].astype(F32)
                stats = stats[0:EXTRA] + stats[EXTRA : 2 * EXTRA] + stats[2 * EXTRA :]
                gap = (
                    near
                    + lax.broadcasted_iota(jnp.int32, (span, rows), 1)
                    - lax.broadcasted_iota(jnp.int32, (span, rows), 0)
                )
                mask = docs_t[...] == docs
                if offset == 0:
                    mask = mask & (gap >= 0)
                if (offset + 1) * span > WINDOW:
                    mask = mask & (gap < WINDOW)
                scores = dot(key_ref[0:span, :], query, ((1,), (1,)))
                dprob = dot(key_ref[span : 2 * span, :], grad, ((1,), (1,)))
                probs, dscores = [], []
                for h in range(GROUP):
                    cut = slice(h * rows, (h + 1) * rows)
                    norm = stats[h : h + 1, :] * LOG2E
                    delta = stats[GROUP + h : GROUP + h + 1, :]
                    prob = jnp.exp2(scores[:, cut] * (SCALE * LOG2E) - norm)
                    prob = jnp.where(mask, prob, 0.0)
                    probs.append(prob.astype(BF16))
                    dscores.append((prob * (dprob[:, cut] - delta) * SCALE).astype(BF16))
                prob = jnp.concatenate(probs, 1)
                dscore = jnp.concatenate(dscores, 1)
                dkv[0:span, :] += dot(dscore, query, ((1,), (0,)))
                dkv[span:, :] += dot(prob, grad, ((1,), (0,)))
                dq[s] += dot(key_t[...], dscore, ((1,), (0,)))

        kv_out[at][...] = dkv[...].astype(kv_out[at].dtype)
    for s in range(parts):
        total = dq[s] if first else dq[s] + dq_in[s]
        if last:
            dq_out[s][...] = total.astype(BF16)
        else:
            dq_out[s] = total


def add_terms(rows, count, place, *refs):
    parts = KEY_VALUE_HEADS
    terms, outs = refs[:count], refs[-parts:]
    for s, out in enumerate(outs):
        for k in range(2):
            at = pl.multiple_of((k * parts + (place[1] ^ s)) * rows, rows)
            total = terms[0][pl.ds(at, rows), :]
            for term in terms[1:]:
                total = total + term[pl.ds(at, rows), :].astype(F32)
            out[k * rows : (k + 1) * rows, :] = total.astype(BF16)


def spread_queries(rows, place, *refs):
    pieces, (out, token, turned, sems) = refs[:-4], refs[-4:]
    width = GROUP * HEAD_SIZE
    copies = []
    for s, piece in enumerate(pieces):
        for h in range(GROUP):
            cut = slice(h * HEAD_SIZE, (h + 1) * HEAD_SIZE)
            turned[s, :, cut] = piece[:, h * rows : (h + 1) * rows].T
        cut = pl.ds(pl.multiple_of((place[1] ^ s) * width, width), width)
        copies.append(pltpu.make_async_copy(turned.at[s], out.at[:, cut], sems.at[s]))
        copies[-1].start()
    token[...] = jnp.zeros_like(token)
    for copy in copies:
        copy.wait()


def spread_keys(rows, place, *refs):
    pieces, outs, sems = refs[:-3], refs[-3:-1], refs[-1]
    copies = []
    for s, piece in enumerate(pieces):
        for k, out in enumerate(outs):
            source = piece.at[k * rows : (k + 1) * rows, :]
            target = out.at[:, head_columns(place[1] ^ s)]
            copies.append(pltpu.make_async_copy(source, target, sems.at[s, k]))
            copies[-1].start()
    for copy in copies:
        copy.wait()


def local(
    queries, key_matrix, value_matrix, attention_output, output_gradient, log_sum_norm, doc_ids
):
    parts = KEY_VALUE_HEADS
    rows = queries.shape[0]
    count = lax.axis_size("tok")
    span = parts * rows
    reach = min(WINDOW, count * rows // 2)
    behind = min(-(-(reach - 1) // span), count // parts - 1)
    device = lax.axis_index("tok")
    place = jnp.stack([device // parts, device % parts]).astype(jnp.int32)
    width = GROUP * rows
    shape = jax.ShapeDtypeStruct

    def across(value, s):
        return lax.ppermute(value, "tok", [(t, t ^ s) for t in range(count)])

    def along(value, steps):
        return lax.ppermute(
            value, "tok", [(t, (t + steps * parts) % count) for t in range(count)]
        )

    def exchange(pieces):
        return [pieces[0]] + [across(pieces[s], s) for s in range(1, parts)]

    pieces = call(
        functools.partial(pack_keys, rows),
        (place, key_matrix, value_matrix, doc_ids.reshape(1, rows)),
        [shape((2 * rows + EXTRA, HEAD_SIZE), BF16)] * parts,
        scratch=[
            pltpu.VMEM((1, rows), jnp.int32),
            pltpu.SemaphoreType.DMA(()),
            pltpu.SemaphoreType.DMA((parts, 2)),
        ],
        specs=[HBM, HBM, HBM],
        name="pack_keys",
    )
    pieces = exchange(pieces)
    *query_pieces, token = call(
        functools.partial(pack_queries, rows),
        (place, queries, output_gradient, attention_output, log_sum_norm),
        [shape((2 * width + 3 * EXTRA, HEAD_SIZE), BF16)] * parts + [TOKEN],
        scratch=[
            pltpu.VMEM(queries.shape, BF16),
            pltpu.VMEM(queries.shape, BF16),
            pltpu.VMEM((parts, 2 * GROUP, rows), F32),
            pltpu.SemaphoreType.DMA((parts, 2, GROUP)),
            pltpu.SemaphoreType.DMA((2,)),
        ],
        specs=[HBM, HBM, HBM, VMEM],
        name="pack_queries",
    )
    (own,) = call(
        functools.partial(join, rows),
        (place, *pieces, token),
        [shape((parts * (2 * rows + EXTRA), HEAD_SIZE), BF16)],
        name="join",
    )
    query_pieces = exchange(query_pieces)
    windows = [own]
    for _ in range(behind):
        windows.append(along(windows[-1], 1))

    kv_shape = (2 * span, HEAD_SIZE)
    stages = [tuple(range(min(2, behind + 1)))] + [(d,) for d in range(2, behind + 1)]
    dq, terms = None, []
    for k, offsets in enumerate(stages):
        first, last = k == 0, k == len(stages) - 1
        ins = [place, *query_pieces, own, *[windows[d] for d in offsets]]
        if not first:
            ins.append(dq)
        if last:
            outs = [shape((HEAD_SIZE, width), BF16)] * parts
        else:
            outs = [shape((parts, HEAD_SIZE, width), F32)]
        outs = outs + [shape(kv_shape, F32 if d == 0 else BF16) for d in offsets]
        got = call(
            functools.partial(attend, rows, offsets, reach, first, last),
            ins,
            outs,
            scratch=attend_scratch(rows),
            flops=10 * len(offsets) * span * span * GROUP * HEAD_SIZE,
            name="attend_" + "_".join(map(str, offsets)),
        )
        dq = got[:parts] if last else got[0]
        for d, term in zip(offsets, got[-len(offsets) :]):
            terms.append(term if d == 0 else along(term, -d))

    query_grad, token = call(
        functools.partial(spread_queries, rows),
        (place, *exchange(dq)),
        [shape((rows, parts * GROUP * HEAD_SIZE), BF16), TOKEN],
        scratch=[
            pltpu.VMEM((parts, rows, GROUP * HEAD_SIZE), BF16),
            pltpu.SemaphoreType.DMA((parts,)),
        ],
        out_specs=[HBM, VMEM],
        name="spread_queries",
    )
    pieces = call(
        functools.partial(add_terms, rows, len(terms)),
        (place, *terms, token),
        [shape((2 * rows, HEAD_SIZE), BF16)] * parts,
        name="add_terms",
    )
    key_grad, value_grad = call(
        functools.partial(spread_keys, rows),
        (place, *exchange(pieces)),
        [shape((rows, parts * HEAD_SIZE), BF16)] * 2,
        scratch=[pltpu.SemaphoreType.DMA((parts, 2))],
        out_specs=[HBM, HBM],
        name="spread_keys",
    )
    return query_grad, key_grad, value_grad


def solution(mesh):
    axes = ("groups", "tok")
    return jax.shard_map(
        local,
        mesh=mesh,
        in_specs=(
            P(axes, None),
            P(axes, None),
            P(axes, None),
            P(axes, None),
            P(axes, None),
            P(None, axes),
            P(axes),
        ),
        out_specs=(P(axes, None), P(axes, None), P(axes, None)),
        check_vma=False,
    )
```

```python
import functools
import math

import jax
import jax.numpy as jnp
from jax import lax
from jax.experimental import pallas as pl
from jax.experimental.pallas import tpu as pltpu
from jax.sharding import PartitionSpec as P

WINDOW = 4096
QUERY_HEADS = 16
KEY_VALUE_HEADS = 4
HEAD_SIZE = 128
GROUP = QUERY_HEADS // KEY_VALUE_HEADS
SCALE = HEAD_SIZE ** (-0.5)
LOG2E = math.log2(math.e)
EXTRA = 8
F32 = jnp.float32
BF16 = jnp.bfloat16

VMEM = pl.BlockSpec(memory_space=pltpu.VMEM)
SMEM = pl.BlockSpec(memory_space=pltpu.SMEM)


def dot(a, b, dims):
    return lax.dot_general(a, b, (dims, ((), ())), preferred_element_type=F32)


HBM = pl.BlockSpec(memory_space=pltpu.MemorySpace.HBM)
TOKEN = jax.ShapeDtypeStruct((8, 128), F32)


def call(kernel, ins, outs, scratch=(), flops=0, specs=None, out_specs=None):
    specs = specs or [VMEM] * (len(ins) - 1)
    ins = [ins[0]] + [
        pltpu.with_memory_space_constraint(x, pltpu.MemorySpace.HBM) if spec is HBM else x
        for x, spec in zip(ins[1:], specs)
    ]
    size = sum(math.prod(o.shape) * o.dtype.itemsize for o in outs)
    size += sum(math.prod(x.shape) * x.dtype.itemsize for x in ins)
    return pl.pallas_call(
        kernel,
        out_shape=outs,
        in_specs=[SMEM] + specs,
        out_specs=out_specs or [VMEM] * len(outs),
        scratch_shapes=list(scratch),
        cost_estimate=pl.CostEstimate(flops=flops, bytes_accessed=size, transcendentals=0),
        compiler_params=pltpu.CompilerParams(vmem_limit_bytes=48 << 20),
    )(*ins)


def head_columns(g):
    return pl.ds(pl.multiple_of(g * HEAD_SIZE, HEAD_SIZE), HEAD_SIZE)


def pack_keys(rows, place, key_ref, value_ref, doc_ref, *rest):
    outs, (ids, doc_sem, sems) = rest[:-3], rest[-3:]
    first = pltpu.make_async_copy(doc_ref, ids, doc_sem)
    first.start()
    copies = []
    for s, out in enumerate(outs):
        cut = head_columns(place[1] ^ s)
        for k, source in enumerate((key_ref, value_ref)):
            target = out.at[k * rows : (k + 1) * rows, :]
            copies.append(pltpu.make_async_copy(source.at[:, cut], target, sems.at[s, k]))
    for copy in copies:
        copy.start()
    first.wait()
    docs = jnp.broadcast_to((ids[...] + 1).astype(F32), (EXTRA, rows)).astype(BF16)
    for out in outs:
        out[2 * rows :, 0:rows] = docs
    for copy in copies:
        copy.wait()


def pack_queries(rows, place, query_ref, grad_ref, output_ref, norm_ref, *rest):
    outs, (token, grads, outputs, stats, sems, more_sems) = rest[:-6], rest[-6:]
    first = pltpu.make_async_copy(grad_ref, grads, more_sems.at[0])
    second = pltpu.make_async_copy(output_ref, outputs, more_sems.at[1])
    first.start()
    second.start()
    copies = []
    for s, out in enumerate(outs):
        for h in range(GROUP):
            cut = head_columns((place[1] ^ s) * GROUP + h)
            for k, source in enumerate((query_ref, grad_ref)):
                at = (k * GROUP + h) * rows
                target = out.at[at : at + rows, :]
                copies.append(pltpu.make_async_copy(source.at[:, cut], target, sems.at[s, k, h]))
    for copy in copies:
        copy.start()
    first.wait()
    second.wait()
    lane = lax.broadcasted_iota(jnp.int32, (rows, HEAD_SIZE), 1)
    columns = jnp.zeros((rows, HEAD_SIZE), F32)
    for h in range(QUERY_HEADS):
        cut = slice(h * HEAD_SIZE, (h + 1) * HEAD_SIZE)
        product = grads[:, cut].astype(F32) * outputs[:, cut].astype(F32)
        columns = jnp.where(lane == h, jnp.sum(product, 1, keepdims=True), columns)
    delta = columns.T
    for g in range(KEY_VALUE_HEADS):
        stats[g, 0:GROUP, :] = norm_ref[g * GROUP : (g + 1) * GROUP, :]
        stats[g, GROUP : 2 * GROUP, :] = delta[g * GROUP : (g + 1) * GROUP, :]
    for s, out in enumerate(outs):
        left = stats[place[1] ^ s]
        for part in range(3):
            term = left.astype(BF16)
            at = 2 * GROUP * rows + part * EXTRA
            out[at : at + EXTRA, 0:rows] = term
            left = left - term.astype(F32)
    for copy in copies:
        copy.wait()
    token[...] = jnp.zeros_like(token)


def join(rows, place, *refs):
    parts = KEY_VALUE_HEADS
    pieces, out = refs[:parts], refs[-1]
    span = parts * rows
    for s, piece in enumerate(pieces):
        a = place[1] ^ s
        for k in range(2):
            at = pl.multiple_of(k * span + a * rows, rows)
            out[pl.ds(at, rows), :] = piece[k * rows : (k + 1) * rows, :]
        at = pl.multiple_of(2 * span + a * EXTRA, EXTRA)
        out[pl.ds(at, EXTRA), :] = piece[2 * rows :, :]


def attend_scratch(rows):
    parts = KEY_VALUE_HEADS
    return [
        pltpu.VMEM((parts, HEAD_SIZE, GROUP * rows), F32),
        pltpu.VMEM((2 * parts * rows, HEAD_SIZE), F32),
        pltpu.VMEM((HEAD_SIZE, parts * rows), BF16),
        pltpu.VMEM((parts * rows, rows), F32),
        pltpu.SMEM((2 * parts,), F32),
    ]


def attend(rows, offset, reach, first, last, place, *refs):
    parts = KEY_VALUE_HEADS
    queries, refs = refs[:parts], refs[parts:]
    own, key_ref, refs = refs[0], refs[1], refs[2:]
    if not first:
        dq_in, refs = refs[0], refs[1:]
    if last:
        dq_out, refs = refs[:parts], refs[parts:]
    else:
        dq_out, refs = refs[0], refs[1:]
    kv_out, dq, dkv, key_t, docs_t, docs_s = refs
    row, me = place[0], place[1]
    width = GROUP * rows
    span = parts * rows
    for a in range(parts):
        docs = own[2 * span + a * EXTRA : 2 * span + a * EXTRA + 1, 0:rows].astype(F32)
        docs_s[a] = jnp.min(docs)
    dq[...] = jnp.zeros_like(dq)
    dkv[...] = jnp.zeros_like(dkv)
    for b in range(parts):
        cut = slice(b * rows, (b + 1) * rows)
        key_t[:, cut] = key_ref[cut, :].T
        docs = key_ref[2 * span + b * EXTRA : 2 * span + b * EXTRA + 1, 0:rows].astype(F32)
        docs_t[cut, :] = jnp.broadcast_to(docs, (rows, rows)).T
        if b == parts - 1:
            docs_s[parts] = jnp.max(docs)
    for s in range(parts):
        a = me ^ s
        near = offset * span + a * rows
        live = (near - span + 1 < reach) & (row >= offset) & (docs_s[a] <= docs_s[parts])

        @pl.when(live)
        def _(s=s, a=a, near=near):
            docs = own[pl.ds(pl.multiple_of(2 * span + a * EXTRA, EXTRA), EXTRA), :]
            docs = docs.astype(F32)[0:1, 0:rows]
            query = queries[s][0:width, :]
            grad = queries[s][width : 2 * width, :]
            stats = queries[s][2 * width :, :].astype(F32)
            stats = stats[0:EXTRA] + stats[EXTRA : 2 * EXTRA] + stats[2 * EXTRA :]
            gap = (
                near
                + lax.broadcasted_iota(jnp.int32, (span, rows), 1)
                - lax.broadcasted_iota(jnp.int32, (span, rows), 0)
            )
            mask = docs_t[...] == docs
            if offset == 0:
                mask = mask & (gap >= 0)
            if (offset + 1) * span > WINDOW:
                mask = mask & (gap < WINDOW)
            scores = dot(key_ref[0:span, :], query, ((1,), (1,)))
            dprob = dot(key_ref[span : 2 * span, :], grad, ((1,), (1,)))
            probs, dscores = [], []
            for h in range(GROUP):
                cut = slice(h * rows, (h + 1) * rows)
                norm = stats[h : h + 1, :] * LOG2E
                delta = stats[GROUP + h : GROUP + h + 1, :]
                prob = jnp.exp2(scores[:, cut] * (SCALE * LOG2E) - norm)
                prob = jnp.where(mask, prob, 0.0)
                probs.append(prob.astype(BF16))
                dscores.append((prob * (dprob[:, cut] - delta) * SCALE).astype(BF16))
            prob = jnp.concatenate(probs, 1)
            dscore = jnp.concatenate(dscores, 1)
            dkv[0:span, :] += dot(dscore, query, ((1,), (0,)))
            dkv[span:, :] += dot(prob, grad, ((1,), (0,)))
            dq[s] += dot(key_t[...], dscore, ((1,), (0,)))

    kv_out[...] = dkv[...].astype(kv_out.dtype)
    for s in range(parts):
        total = dq[s] if first else dq[s] + dq_in[s]
        if last:
            dq_out[s][...] = total.astype(BF16)
        else:
            dq_out[s] = total


def add_terms(place, arrived, term, out):
    out[...] = (arrived[...].astype(F32) + term[...]).astype(BF16)


def cut_terms(rows, count, place, *refs):
    parts = KEY_VALUE_HEADS
    terms, outs = refs[:count], refs[-parts:]
    for s, out in enumerate(outs):
        for k in range(2):
            at = pl.multiple_of((k * parts + (place[1] ^ s)) * rows, rows)
            total = sum(term[pl.ds(at, rows), :].astype(F32) for term in terms)
            out[k * rows : (k + 1) * rows, :] = total.astype(BF16)


def spread_queries(rows, place, *refs):
    pieces, (out, token, turned, sems) = refs[:-4], refs[-4:]
    width = GROUP * HEAD_SIZE
    copies = []
    for s, piece in enumerate(pieces):
        for h in range(GROUP):
            cut = slice(h * HEAD_SIZE, (h + 1) * HEAD_SIZE)
            turned[s, :, cut] = piece[:, h * rows : (h + 1) * rows].T
        cut = pl.ds(pl.multiple_of((place[1] ^ s) * width, width), width)
        copies.append(pltpu.make_async_copy(turned.at[s], out.at[:, cut], sems.at[s]))
        copies[-1].start()
    token[...] = jnp.zeros_like(token)
    for copy in copies:
        copy.wait()


def spread_keys(rows, sources, place, *refs):
    parts = KEY_VALUE_HEADS
    pieces, (key_out, value_out, total, sems) = refs[:-5], refs[-4:]
    copies = []
    for s in range(parts):
        term = pieces[s][...].astype(F32)
        for k in range(1, sources):
            term = term + pieces[k * parts + s][...].astype(F32)
        total[s] = term.astype(BF16)
        for k, out in enumerate((key_out, value_out)):
            source = total.at[s, k * rows : (k + 1) * rows, :]
            target = out.at[:, head_columns(place[1] ^ s)]
            copies.append(pltpu.make_async_copy(source, target, sems.at[s, k]))
            copies[-1].start()
    for copy in copies:
        copy.wait()


def local(
    queries, key_matrix, value_matrix, attention_output, output_gradient, log_sum_norm, doc_ids
):
    parts = KEY_VALUE_HEADS
    rows = queries.shape[0]
    count = lax.axis_size("tok")
    span = parts * rows
    reach = min(WINDOW, count * rows // 2)
    behind = min(-(-(reach - 1) // span), count // parts - 1)
    device = lax.axis_index("tok")
    place = jnp.stack([device // parts, device % parts]).astype(jnp.int32)
    width = GROUP * rows
    shape = jax.ShapeDtypeStruct

    def move(value, steps, s=0):
        pairs = [(t, ((t + steps * parts) % count) ^ s) for t in range(count)]
        return lax.ppermute(value, "tok", pairs)

    def exchange(pieces):
        return [pieces[0]] + [move(pieces[s], 0, s) for s in range(1, parts)]

    pieces = call(
        functools.partial(pack_keys, rows),
        (place, key_matrix, value_matrix, doc_ids.reshape(1, rows)),
        [shape((2 * rows + EXTRA, HEAD_SIZE), BF16)] * parts,
        scratch=[
            pltpu.VMEM((1, rows), jnp.int32),
            pltpu.SemaphoreType.DMA(()),
            pltpu.SemaphoreType.DMA((parts, 2)),
        ],
        specs=[HBM, HBM, HBM],
    )
    pieces = exchange(pieces)
    *query_pieces, token = call(
        functools.partial(pack_queries, rows),
        (place, queries, output_gradient, attention_output, log_sum_norm),
        [shape((2 * width + 3 * EXTRA, HEAD_SIZE), BF16)] * parts + [TOKEN],
        scratch=[
            pltpu.VMEM(queries.shape, BF16),
            pltpu.VMEM(queries.shape, BF16),
            pltpu.VMEM((parts, 2 * GROUP, rows), F32),
            pltpu.SemaphoreType.DMA((parts, 2, GROUP)),
            pltpu.SemaphoreType.DMA((2,)),
        ],
        specs=[HBM, HBM, HBM, VMEM],
    )
    (own,) = call(
        functools.partial(join, rows),
        (place, *pieces, token),
        [shape((parts * (2 * rows + EXTRA), HEAD_SIZE), BF16)],
    )
    query_pieces = exchange(query_pieces)
    windows = [own]
    for _ in range(behind):
        windows.append(move(windows[-1], 1))

    kv_shape = (2 * span, HEAD_SIZE)
    stages = [0] + list(range(behind, 0, -1))
    dq, own_term, sent = None, None, None
    for k, offset in enumerate(stages):
        first, last = k == 0, k == len(stages) - 1
        ins = [place, *query_pieces, own, windows[offset]]
        if not first:
            ins.append(dq)
        if last:
            outs = [shape((HEAD_SIZE, width), BF16)] * parts
        else:
            outs = [shape((parts, HEAD_SIZE, width), F32)]
        outs = outs + [shape(kv_shape, BF16 if offset == behind > 0 else F32)]
        got = call(
            functools.partial(attend, rows, offset, reach, first, last),
            ins,
            outs,
            scratch=attend_scratch(rows),
            flops=10 * span * span * GROUP * HEAD_SIZE,
        )
        dq, term = (got[:parts] if last else got[0]), got[-1]
        piece_shapes = [shape((2 * rows, HEAD_SIZE), BF16)] * parts
        if offset == 0:
            own_term = term
        elif offset == 1:
            terms = (term,) if sent is None else (sent, term)
            got = call(
                functools.partial(cut_terms, rows, len(terms)), (place, *terms), piece_shapes
            )
            sent = [move(piece, -1, s) for s, piece in enumerate(got)]
        elif sent is None:
            sent = move(term, -1)
        else:
            (term,) = call(add_terms, (place, sent, term), [shape(kv_shape, BF16)])
            sent = move(term, -1)

    dq_pieces = exchange(dq)
    own_pieces = call(
        functools.partial(cut_terms, rows, 1),
        (place, own_term, *([] if sent is None else got[:1])),
        piece_shapes,
    )
    own_pieces = exchange(own_pieces)
    query_grad, token = call(
        functools.partial(spread_queries, rows),
        (place, *dq_pieces),
        [shape((rows, parts * GROUP * HEAD_SIZE), BF16), TOKEN],
        scratch=[
            pltpu.VMEM((parts, rows, GROUP * HEAD_SIZE), BF16),
            pltpu.SemaphoreType.DMA((parts,)),
        ],
        out_specs=[HBM, VMEM],
    )
    pieces = own_pieces + (sent or [])
    key_grad, value_grad = call(
        functools.partial(spread_keys, rows, len(pieces) // parts),
        (place, *pieces, token),
        [shape((rows, parts * HEAD_SIZE), BF16)] * 2,
        scratch=[
            pltpu.VMEM((parts, 2 * rows, HEAD_SIZE), BF16),
            pltpu.SemaphoreType.DMA((parts, 2)),
        ],
        out_specs=[HBM, HBM],
    )
    return query_grad, key_grad, value_grad


def solution(mesh):
    axes = ("groups", "tok")
    return jax.shard_map(
        local,
        mesh=mesh,
        in_specs=(
            P(axes, None),
            P(axes, None),
            P(axes, None),
            P(axes, None),
            P(axes, None),
            P(None, axes),
            P(axes),
        ),
        out_specs=(P(axes, None), P(axes, None), P(axes, None)),
        check_vma=False,
    )
```

```python
import functools
import math

import jax
import jax.numpy as jnp
from jax import lax
from jax.experimental import pallas as pl
from jax.experimental.pallas import tpu as pltpu
from jax.sharding import PartitionSpec as P

WINDOW = 4096
QUERY_HEADS = 16
KEY_VALUE_HEADS = 4
HEAD_SIZE = 128
GROUP = QUERY_HEADS // KEY_VALUE_HEADS
SCALE = HEAD_SIZE ** (-0.5)
LOG2E = math.log2(math.e)
EXTRA = 8
F32 = jnp.float32
BF16 = jnp.bfloat16

VMEM = pl.BlockSpec(memory_space=pltpu.VMEM)
SMEM = pl.BlockSpec(memory_space=pltpu.SMEM)


def dot(a, b, dims):
    return lax.dot_general(a, b, (dims, ((), ())), preferred_element_type=F32)


HBM = pl.BlockSpec(memory_space=pltpu.MemorySpace.HBM)
TOKEN = jax.ShapeDtypeStruct((8, 128), F32)


def call(kernel, ins, outs, scratch=(), flops=0, specs=None, out_specs=None):
    specs = specs or [VMEM] * (len(ins) - 1)
    ins = [ins[0]] + [
        pltpu.with_memory_space_constraint(x, pltpu.MemorySpace.HBM) if spec is HBM else x
        for x, spec in zip(ins[1:], specs)
    ]
    size = sum(math.prod(o.shape) * o.dtype.itemsize for o in outs)
    size += sum(math.prod(x.shape) * x.dtype.itemsize for x in ins)
    return pl.pallas_call(
        kernel,
        out_shape=outs,
        in_specs=[SMEM] + specs,
        out_specs=out_specs or [VMEM] * len(outs),
        scratch_shapes=list(scratch),
        cost_estimate=pl.CostEstimate(flops=flops, bytes_accessed=size, transcendentals=0),
        compiler_params=pltpu.CompilerParams(vmem_limit_bytes=48 << 20),
    )(*ins)


def head_columns(g):
    return pl.ds(pl.multiple_of(g * HEAD_SIZE, HEAD_SIZE), HEAD_SIZE)


def pack_keys(rows, place, key_ref, value_ref, doc_ref, *rest):
    outs, (ids, doc_sem, sems) = rest[:-3], rest[-3:]
    first = pltpu.make_async_copy(doc_ref, ids, doc_sem)
    first.start()
    copies = []
    for s, out in enumerate(outs):
        cut = head_columns(place[1] ^ s)
        for k, source in enumerate((key_ref, value_ref)):
            target = out.at[k * rows : (k + 1) * rows, :]
            copies.append(pltpu.make_async_copy(source.at[:, cut], target, sems.at[s, k]))
    for copy in copies:
        copy.start()
    first.wait()
    docs = jnp.broadcast_to((ids[...] + 1).astype(F32), (EXTRA, rows)).astype(BF16)
    for out in outs:
        out[2 * rows :, 0:rows] = docs
    for copy in copies:
        copy.wait()


def pack_queries(rows, place, query_ref, grad_ref, output_ref, norm_ref, *rest):
    outs, (token, grads, outputs, stats, sems, more_sems) = rest[:-6], rest[-6:]
    first = pltpu.make_async_copy(grad_ref, grads, more_sems.at[0])
    second = pltpu.make_async_copy(output_ref, outputs, more_sems.at[1])
    first.start()
    second.start()
    copies = []
    for s, out in enumerate(outs):
        for h in range(GROUP):
            cut = head_columns((place[1] ^ s) * GROUP + h)
            for k, source in enumerate((query_ref, grad_ref)):
                at = (k * GROUP + h) * rows
                target = out.at[at : at + rows, :]
                copies.append(pltpu.make_async_copy(source.at[:, cut], target, sems.at[s, k, h]))
    for copy in copies:
        copy.start()
    first.wait()
    second.wait()
    lane = lax.broadcasted_iota(jnp.int32, (rows, HEAD_SIZE), 1)
    columns = jnp.zeros((rows, HEAD_SIZE), F32)
    for h in range(QUERY_HEADS):
        cut = slice(h * HEAD_SIZE, (h + 1) * HEAD_SIZE)
        product = grads[:, cut].astype(F32) * outputs[:, cut].astype(F32)
        columns = jnp.where(lane == h, jnp.sum(product, 1, keepdims=True), columns)
    delta = columns.T
    for g in range(KEY_VALUE_HEADS):
        stats[g, 0:GROUP, :] = norm_ref[g * GROUP : (g + 1) * GROUP, :]
        stats[g, GROUP : 2 * GROUP, :] = delta[g * GROUP : (g + 1) * GROUP, :]
    for s, out in enumerate(outs):
        left = stats[place[1] ^ s]
        for part in range(3):
            term = left.astype(BF16)
            at = 2 * GROUP * rows + part * EXTRA
            out[at : at + EXTRA, 0:rows] = term
            left = left - term.astype(F32)
    for copy in copies:
        copy.wait()
    token[...] = jnp.zeros_like(token)


def join(rows, place, *refs):
    parts = KEY_VALUE_HEADS
    pieces, out = refs[:parts], refs[-1]
    span = parts * rows
    for s, piece in enumerate(pieces):
        a = place[1] ^ s
        for k in range(2):
            at = pl.multiple_of(k * span + a * rows, rows)
            out[pl.ds(at, rows), :] = piece[k * rows : (k + 1) * rows, :]
        at = pl.multiple_of(2 * span + a * EXTRA, EXTRA)
        out[pl.ds(at, EXTRA), :] = piece[2 * rows :, :]


def attend_scratch(rows):
    parts = KEY_VALUE_HEADS
    return [
        pltpu.VMEM((parts, HEAD_SIZE, GROUP * rows), F32),
        pltpu.VMEM((2 * parts * rows, HEAD_SIZE), F32),
        pltpu.VMEM((HEAD_SIZE, parts * rows), BF16),
        pltpu.VMEM((parts * rows, rows), F32),
        pltpu.SMEM((2 * parts,), F32),
    ]


def attend(rows, offset, reach, first, last, place, *refs):
    parts = KEY_VALUE_HEADS
    queries, refs = refs[:parts], refs[parts:]
    own, key_ref, refs = refs[0], refs[1], refs[2:]
    if not first:
        dq_in, refs = refs[0], refs[1:]
    if last:
        dq_out, refs = refs[:parts], refs[parts:]
    else:
        dq_out, refs = refs[0], refs[1:]
    kv_out, dq, dkv, key_t, docs_t, docs_s = refs
    row, me = place[0], place[1]
    width = GROUP * rows
    span = parts * rows
    for a in range(parts):
        docs = own[2 * span + a * EXTRA : 2 * span + a * EXTRA + 1, 0:rows].astype(F32)
        docs_s[a] = jnp.min(docs)
    dq[...] = jnp.zeros_like(dq)
    dkv[...] = jnp.zeros_like(dkv)
    for b in range(parts):
        cut = slice(b * rows, (b + 1) * rows)
        key_t[:, cut] = key_ref[cut, :].T
        docs = key_ref[2 * span + b * EXTRA : 2 * span + b * EXTRA + 1, 0:rows].astype(F32)
        docs_t[cut, :] = jnp.broadcast_to(docs, (rows, rows)).T
        if (b + 1) % (parts // 2) == 0:
            docs_s[parts + b // (parts // 2)] = jnp.max(docs)
    half = span // 2
    for s in range(parts):
        a = me ^ s
        near = offset * span + a * rows
        low = (near - half + 1 < reach) & (row >= offset) & (docs_s[a] <= docs_s[parts])
        high = (near - span + 1 < reach) & (row >= offset) & (docs_s[a] <= docs_s[parts + 1])
        if offset == 0:
            high = high & (a * rows + rows > half)

        def block(start, stop, s=s, a=a, near=near):
            docs = own[pl.ds(pl.multiple_of(2 * span + a * EXTRA, EXTRA), EXTRA), :]
            docs = docs.astype(F32)[0:1, 0:rows]
            query = queries[s][0:width, :]
            grad = queries[s][width : 2 * width, :]
            stats = queries[s][2 * width :, :].astype(F32)
            stats = stats[0:EXTRA] + stats[EXTRA : 2 * EXTRA] + stats[2 * EXTRA :]
            gap = (
                near
                - start
                + lax.broadcasted_iota(jnp.int32, (stop - start, rows), 1)
                - lax.broadcasted_iota(jnp.int32, (stop - start, rows), 0)
            )
            mask = docs_t[start:stop, :] == docs
            if offset == 0:
                mask = mask & (gap >= 0)
            if (offset + 1) * span > WINDOW:
                mask = mask & (gap < WINDOW)
            scores = dot(key_ref[start:stop, :], query, ((1,), (1,)))
            dprob = dot(key_ref[span + start : span + stop, :], grad, ((1,), (1,)))
            probs, dscores = [], []
            for h in range(GROUP):
                cut = slice(h * rows, (h + 1) * rows)
                norm = stats[h : h + 1, :] * LOG2E
                delta = stats[GROUP + h : GROUP + h + 1, :]
                prob = jnp.exp2(scores[:, cut] * (SCALE * LOG2E) - norm)
                prob = jnp.where(mask, prob, 0.0)
                probs.append(prob.astype(BF16))
                dscores.append((prob * (dprob[:, cut] - delta) * SCALE).astype(BF16))
            prob = jnp.concatenate(probs, 1)
            dscore = jnp.concatenate(dscores, 1)
            dkv[start:stop, :] += dot(dscore, query, ((1,), (0,)))
            dkv[span + start : span + stop, :] += dot(prob, grad, ((1,), (0,)))
            dq[s] += dot(key_t[:, start:stop], dscore, ((1,), (0,)))

        pl.when(low & high)(functools.partial(block, 0, span))
        pl.when(high & ~low)(functools.partial(block, half, span))
        if offset == 0:
            pl.when(low & ~high)(functools.partial(block, 0, half))

    kv_out[...] = dkv[...].astype(kv_out.dtype)
    for s in range(parts):
        total = dq[s] if first else dq[s] + dq_in[s]
        if last:
            dq_out[s][...] = total.astype(BF16)
        else:
            dq_out[s] = total


def add_terms(place, arrived, term, out):
    out[...] = (arrived[...].astype(F32) + term[...]).astype(BF16)


def cut_terms(rows, count, place, *refs):
    parts = KEY_VALUE_HEADS
    terms, outs = refs[:count], refs[-parts:]
    for s, out in enumerate(outs):
        for k in range(2):
            at = pl.multiple_of((k * parts + (place[1] ^ s)) * rows, rows)
            total = sum(term[pl.ds(at, rows), :].astype(F32) for term in terms)
            out[k * rows : (k + 1) * rows, :] = total.astype(BF16)


def spread_queries(rows, place, *refs):
    pieces, (out, token, turned, sems) = refs[:-4], refs[-4:]
    width = GROUP * HEAD_SIZE
    copies = []
    for s, piece in enumerate(pieces):
        for h in range(GROUP):
            cut = slice(h * HEAD_SIZE, (h + 1) * HEAD_SIZE)
            turned[s, :, cut] = piece[:, h * rows : (h + 1) * rows].T
        cut = pl.ds(pl.multiple_of((place[1] ^ s) * width, width), width)
        copies.append(pltpu.make_async_copy(turned.at[s], out.at[:, cut], sems.at[s]))
        copies[-1].start()
    token[...] = jnp.zeros_like(token)
    for copy in copies:
        copy.wait()


def spread_keys(rows, sources, place, *refs):
    parts = KEY_VALUE_HEADS
    pieces, (key_out, value_out, total, sems) = refs[:-5], refs[-4:]
    copies = []
    for s in range(parts):
        term = pieces[s][...].astype(F32)
        for k in range(1, sources):
            term = term + pieces[k * parts + s][...].astype(F32)
        total[s] = term.astype(BF16)
        for k, out in enumerate((key_out, value_out)):
            source = total.at[s, k * rows : (k + 1) * rows, :]
            target = out.at[:, head_columns(place[1] ^ s)]
            copies.append(pltpu.make_async_copy(source, target, sems.at[s, k]))
            copies[-1].start()
    for copy in copies:
        copy.wait()


def local(
    queries, key_matrix, value_matrix, attention_output, output_gradient, log_sum_norm, doc_ids
):
    parts = KEY_VALUE_HEADS
    rows = queries.shape[0]
    count = lax.axis_size("tok")
    span = parts * rows
    reach = min(WINDOW, count * rows // 2)
    behind = min(-(-(reach - 1) // span), count // parts - 1)
    device = lax.axis_index("tok")
    place = jnp.stack([device // parts, device % parts]).astype(jnp.int32)
    width = GROUP * rows
    shape = jax.ShapeDtypeStruct

    def move(value, steps, s=0, low=0):
        def target(t):
            row, me = divmod(t, parts)
            if row >= low:
                row = low + (row - low + steps) % (count // parts - low)
            return (row * parts + me) ^ s

        return lax.ppermute(value, "tok", [(t, target(t)) for t in range(count)])

    def exchange(pieces):
        return [pieces[0]] + [move(pieces[s], 0, s) for s in range(1, parts)]

    pieces = call(
        functools.partial(pack_keys, rows),
        (place, key_matrix, value_matrix, doc_ids.reshape(1, rows)),
        [shape((2 * rows + EXTRA, HEAD_SIZE), BF16)] * parts,
        scratch=[
            pltpu.VMEM((1, rows), jnp.int32),
            pltpu.SemaphoreType.DMA(()),
            pltpu.SemaphoreType.DMA((parts, 2)),
        ],
        specs=[HBM, HBM, HBM],
    )
    pieces = exchange(pieces)
    *query_pieces, token = call(
        functools.partial(pack_queries, rows),
        (place, queries, output_gradient, attention_output, log_sum_norm),
        [shape((2 * width + 3 * EXTRA, HEAD_SIZE), BF16)] * parts + [TOKEN],
        scratch=[
            pltpu.VMEM(queries.shape, BF16),
            pltpu.VMEM(queries.shape, BF16),
            pltpu.VMEM((parts, 2 * GROUP, rows), F32),
            pltpu.SemaphoreType.DMA((parts, 2, GROUP)),
            pltpu.SemaphoreType.DMA((2,)),
        ],
        specs=[HBM, HBM, HBM, VMEM],
    )
    (own,) = call(
        functools.partial(join, rows),
        (place, *pieces, token),
        [shape((parts * (2 * rows + EXTRA), HEAD_SIZE), BF16)],
    )
    query_pieces = exchange(query_pieces)
    windows = [own]
    for k in range(behind):
        windows.append(move(windows[-1], 1, low=k))

    kv_shape = (2 * span, HEAD_SIZE)
    stages = [0] + list(range(behind, 0, -1))
    dq, own_pieces, sent = None, None, None
    for k, offset in enumerate(stages):
        first, last = k == 0, k == len(stages) - 1
        ins = [place, *query_pieces, own, windows[offset]]
        if not first:
            ins.append(dq)
        if last:
            outs = [shape((HEAD_SIZE, width), BF16)] * parts
        else:
            outs = [shape((parts, HEAD_SIZE, width), F32)]
        outs = outs + [shape(kv_shape, BF16 if offset == behind > 0 else F32)]
        got = call(
            functools.partial(attend, rows, offset, reach, first, last),
            ins,
            outs,
            scratch=attend_scratch(rows),
            flops=10 * span * span * GROUP * HEAD_SIZE,
        )
        dq, term = (got[:parts] if last else got[0]), got[-1]
        piece_shapes = [shape((2 * rows, HEAD_SIZE), BF16)] * parts
        if offset == 0:
            own_pieces = call(functools.partial(cut_terms, rows, 1), (place, term), piece_shapes)
            own_pieces = exchange(own_pieces)
        elif offset == 1:
            terms = (term,) if sent is None else (sent, term)
            got = call(
                functools.partial(cut_terms, rows, len(terms)), (place, *terms), piece_shapes
            )
            sent = [move(piece, -1, s) for s, piece in enumerate(got)]
        elif sent is None:
            sent = move(term, -1, low=offset - 1)
        else:
            (term,) = call(add_terms, (place, sent, term), [shape(kv_shape, BF16)])
            sent = move(term, -1, low=offset - 1)

    dq_pieces = exchange(dq)
    query_grad, token = call(
        functools.partial(spread_queries, rows),
        (place, *dq_pieces),
        [shape((rows, parts * GROUP * HEAD_SIZE), BF16), TOKEN],
        scratch=[
            pltpu.VMEM((parts, rows, GROUP * HEAD_SIZE), BF16),
            pltpu.SemaphoreType.DMA((parts,)),
        ],
        out_specs=[HBM, VMEM],
    )
    pieces = own_pieces + (sent or [])
    key_grad, value_grad = call(
        functools.partial(spread_keys, rows, len(pieces) // parts),
        (place, *pieces, token),
        [shape((rows, parts * HEAD_SIZE), BF16)] * 2,
        scratch=[
            pltpu.VMEM((parts, 2 * rows, HEAD_SIZE), BF16),
            pltpu.SemaphoreType.DMA((parts, 2)),
        ],
        out_specs=[HBM, HBM],
    )
    return query_grad, key_grad, value_grad


def solution(mesh):
    axes = ("groups", "tok")
    return jax.shard_map(
        local,
        mesh=mesh,
        in_specs=(
            P(axes, None),
            P(axes, None),
            P(axes, None),
            P(axes, None),
            P(axes, None),
            P(None, axes),
            P(axes),
        ),
        out_specs=(P(axes, None), P(axes, None), P(axes, None)),
        check_vma=False,
    )
```

```python
import functools
import math

import jax
import jax.numpy as jnp
from jax import lax
from jax.experimental import pallas as pl
from jax.experimental.pallas import tpu as pltpu
from jax.sharding import PartitionSpec as P

WINDOW = 4096
QUERY_HEADS = 16
KEY_VALUE_HEADS = 4
HEAD_SIZE = 128
GROUP = QUERY_HEADS // KEY_VALUE_HEADS
SCALE = HEAD_SIZE ** (-0.5)
LOG2E = math.log2(math.e)
EXTRA = 8
F32 = jnp.float32
BF16 = jnp.bfloat16

VMEM = pl.BlockSpec(memory_space=pltpu.VMEM)
SMEM = pl.BlockSpec(memory_space=pltpu.SMEM)


def dot(a, b, dims):
    return lax.dot_general(a, b, (dims, ((), ())), preferred_element_type=F32)


HBM = pl.BlockSpec(memory_space=pltpu.MemorySpace.HBM)
TOKEN = jax.ShapeDtypeStruct((8, 128), F32)


def call(kernel, ins, outs, scratch=(), flops=0, specs=None, out_specs=None):
    specs = specs or [VMEM] * (len(ins) - 1)
    ins = [ins[0]] + [
        pltpu.with_memory_space_constraint(x, pltpu.MemorySpace.HBM) if spec is HBM else x
        for x, spec in zip(ins[1:], specs)
    ]
    size = sum(math.prod(o.shape) * o.dtype.itemsize for o in outs)
    size += sum(math.prod(x.shape) * x.dtype.itemsize for x in ins)
    return pl.pallas_call(
        kernel,
        out_shape=outs,
        in_specs=[SMEM] + specs,
        out_specs=out_specs or [VMEM] * len(outs),
        scratch_shapes=list(scratch),
        cost_estimate=pl.CostEstimate(flops=flops, bytes_accessed=size, transcendentals=0),
        compiler_params=pltpu.CompilerParams(vmem_limit_bytes=48 << 20),
    )(*ins)


def head_columns(g):
    return pl.ds(pl.multiple_of(g * HEAD_SIZE, HEAD_SIZE), HEAD_SIZE)


def pack_keys(rows, place, key_ref, value_ref, doc_ref, *rest):
    outs, (ids, doc_sem, sems) = rest[:-3], rest[-3:]
    first = pltpu.make_async_copy(doc_ref, ids, doc_sem)
    first.start()
    copies = []
    for s, out in enumerate(outs):
        cut = head_columns(place[1] ^ s)
        for k, source in enumerate((key_ref, value_ref)):
            target = out.at[k * rows : (k + 1) * rows, :]
            copies.append(pltpu.make_async_copy(source.at[:, cut], target, sems.at[s, k]))
    for copy in copies:
        copy.start()
    first.wait()
    docs = jnp.broadcast_to((ids[...] + 1).astype(F32), (EXTRA, rows)).astype(BF16)
    for out in outs:
        out[2 * rows :, 0:rows] = docs
    for copy in copies:
        copy.wait()


def pack_queries(rows, place, query_ref, grad_ref, output_ref, norm_ref, *rest):
    outs, (token, grads, outputs, stats, sems, more_sems) = rest[:-6], rest[-6:]
    first = pltpu.make_async_copy(grad_ref, grads, more_sems.at[0])
    second = pltpu.make_async_copy(output_ref, outputs, more_sems.at[1])
    first.start()
    second.start()
    copies = []
    for s, out in enumerate(outs):
        for h in range(GROUP):
            cut = head_columns((place[1] ^ s) * GROUP + h)
            for k, source in enumerate((query_ref, grad_ref)):
                at = (k * GROUP + h) * rows
                target = out.at[at : at + rows, :]
                copies.append(pltpu.make_async_copy(source.at[:, cut], target, sems.at[s, k, h]))
    for copy in copies:
        copy.start()
    first.wait()
    second.wait()
    lane = lax.broadcasted_iota(jnp.int32, (rows, HEAD_SIZE), 1)
    columns = jnp.zeros((rows, HEAD_SIZE), F32)
    for h in range(QUERY_HEADS):
        cut = slice(h * HEAD_SIZE, (h + 1) * HEAD_SIZE)
        product = grads[:, cut].astype(F32) * outputs[:, cut].astype(F32)
        columns = jnp.where(lane == h, jnp.sum(product, 1, keepdims=True), columns)
    delta = columns.T
    for g in range(KEY_VALUE_HEADS):
        stats[g, 0:GROUP, :] = norm_ref[g * GROUP : (g + 1) * GROUP, :]
        stats[g, GROUP : 2 * GROUP, :] = delta[g * GROUP : (g + 1) * GROUP, :]
    for s, out in enumerate(outs):
        left = stats[place[1] ^ s]
        for part in range(3):
            term = left.astype(BF16)
            at = 2 * GROUP * rows + part * EXTRA
            out[at : at + EXTRA, 0:rows] = term
            left = left - term.astype(F32)
    for copy in copies:
        copy.wait()
    token[...] = jnp.zeros_like(token)


def join(rows, place, *refs):
    parts = KEY_VALUE_HEADS
    pieces, out = refs[:parts], refs[-1]
    span = parts * rows
    for s, piece in enumerate(pieces):
        a = place[1] ^ s
        for k in range(2):
            at = pl.multiple_of(k * span + a * rows, rows)
            out[pl.ds(at, rows), :] = piece[k * rows : (k + 1) * rows, :]
        at = pl.multiple_of(2 * span + a * EXTRA, EXTRA)
        out[pl.ds(at, EXTRA), :] = piece[2 * rows :, :]


def attend_scratch(rows):
    parts = KEY_VALUE_HEADS
    return [
        pltpu.VMEM((parts, HEAD_SIZE, GROUP * rows), F32),
        pltpu.VMEM((2 * parts * rows, HEAD_SIZE), F32),
        pltpu.VMEM((HEAD_SIZE, parts * rows), BF16),
        pltpu.VMEM((parts * rows, rows), F32),
        pltpu.SMEM((2 * parts,), F32),
    ]


def attend(rows, offset, reach, first, last, place, *refs):
    parts = KEY_VALUE_HEADS
    queries, refs = refs[:parts], refs[parts:]
    own, key_ref, refs = refs[0], refs[1], refs[2:]
    if not first:
        dq_in, refs = refs[0], refs[1:]
    if last:
        dq_out, refs = refs[:parts], refs[parts:]
    else:
        dq_out, refs = refs[0], refs[1:]
    kv_out, dq, dkv, key_t, docs_t, docs_s = refs
    row, me = place[0], place[1]
    width = GROUP * rows
    span = parts * rows
    for a in range(parts):
        docs = own[2 * span + a * EXTRA : 2 * span + a * EXTRA + 1, 0:rows].astype(F32)
        docs_s[a] = jnp.min(docs)
    dq[...] = jnp.zeros_like(dq)
    dkv[...] = jnp.zeros_like(dkv)
    for b in range(parts):
        cut = slice(b * rows, (b + 1) * rows)
        key_t[:, cut] = key_ref[cut, :].T
        docs = key_ref[2 * span + b * EXTRA : 2 * span + b * EXTRA + 1, 0:rows].astype(F32)
        docs_t[cut, :] = jnp.broadcast_to(docs, (rows, rows)).T
        if (b + 1) % (parts // 2) == 0:
            docs_s[parts + b // (parts // 2)] = jnp.max(docs)
    half = span // 2
    for s in range(parts):
        a = me ^ s
        near = offset * span + a * rows
        low = (near - half + 1 < reach) & (row >= offset) & (docs_s[a] <= docs_s[parts])
        high = (near - span + 1 < reach) & (row >= offset) & (docs_s[a] <= docs_s[parts + 1])
        if offset == 0:
            high = high & (a * rows + rows > half)

        def block(start, stop, s=s, a=a, near=near):
            docs = own[pl.ds(pl.multiple_of(2 * span + a * EXTRA, EXTRA), EXTRA), :]
            docs = docs.astype(F32)[0:1, 0:rows]
            query = queries[s][0:width, :]
            grad = queries[s][width : 2 * width, :]
            stats = queries[s][2 * width :, :].astype(F32)
            stats = stats[0:EXTRA] + stats[EXTRA : 2 * EXTRA] + stats[2 * EXTRA :]
            gap = (
                near
                - start
                + lax.broadcasted_iota(jnp.int32, (stop - start, rows), 1)
                - lax.broadcasted_iota(jnp.int32, (stop - start, rows), 0)
            )
            mask = docs_t[start:stop, :] == docs
            if offset == 0:
                mask = mask & (gap >= 0)
            if (offset + 1) * span > WINDOW:
                mask = mask & (gap < WINDOW)
            scores = dot(key_ref[start:stop, :], query, ((1,), (1,)))
            dprob = dot(key_ref[span + start : span + stop, :], grad, ((1,), (1,)))
            probs, dscores = [], []
            for h in range(GROUP):
                cut = slice(h * rows, (h + 1) * rows)
                norm = stats[h : h + 1, :] * LOG2E
                delta = stats[GROUP + h : GROUP + h + 1, :]
                prob = jnp.exp2(scores[:, cut] * (SCALE * LOG2E) - norm)
                prob = jnp.where(mask, prob, 0.0)
                probs.append(prob.astype(BF16))
                dscores.append((prob * (dprob[:, cut] - delta) * SCALE).astype(BF16))
            prob = jnp.concatenate(probs, 1)
            dscore = jnp.concatenate(dscores, 1)
            dkv[start:stop, :] += dot(dscore, query, ((1,), (0,)))
            dkv[span + start : span + stop, :] += dot(prob, grad, ((1,), (0,)))
            dq[s] += dot(key_t[:, start:stop], dscore, ((1,), (0,)))

        pl.when(low & high)(functools.partial(block, 0, span))
        pl.when(high & ~low)(functools.partial(block, half, span))
        if offset == 0:
            pl.when(low & ~high)(functools.partial(block, 0, half))

    kv_out[...] = dkv[...].astype(kv_out.dtype)
    for s in range(parts):
        total = dq[s] if first else dq[s] + dq_in[s]
        if last:
            dq_out[s][...] = total.astype(BF16)
        else:
            dq_out[s] = total


def add_terms(place, arrived, term, out):
    out[...] = (arrived[...].astype(F32) + term[...]).astype(BF16)


def cut_terms(rows, count, place, *refs):
    parts = KEY_VALUE_HEADS
    terms, outs = refs[:count], refs[-parts:]
    for s, out in enumerate(outs):
        for k in range(2):
            at = pl.multiple_of((k * parts + (place[1] ^ s)) * rows, rows)
            total = sum(term[pl.ds(at, rows), :].astype(F32) for term in terms)
            out[k * rows : (k + 1) * rows, :] = total.astype(BF16)


def spread_queries(rows, place, *refs):
    pieces, (out, token, turned, sems) = refs[:-4], refs[-4:]
    width = GROUP * HEAD_SIZE
    copies = []
    for s, piece in enumerate(pieces):
        for h in range(GROUP):
            cut = slice(h * HEAD_SIZE, (h + 1) * HEAD_SIZE)
            turned[s, :, cut] = piece[:, h * rows : (h + 1) * rows].T
        cut = pl.ds(pl.multiple_of((place[1] ^ s) * width, width), width)
        copies.append(pltpu.make_async_copy(turned.at[s], out.at[:, cut], sems.at[s]))
        copies[-1].start()
    token[...] = jnp.zeros_like(token)
    for copy in copies:
        copy.wait()


def spread_keys(rows, sources, place, *refs):
    parts = KEY_VALUE_HEADS
    pieces, (key_out, value_out, total, sems) = refs[:-5], refs[-4:]
    copies = []
    for s in range(parts):
        term = pieces[s][...].astype(F32)
        for k in range(1, sources):
            term = term + pieces[k * parts + s][...].astype(F32)
        total[s] = term.astype(BF16)
        for k, out in enumerate((key_out, value_out)):
            source = total.at[s, k * rows : (k + 1) * rows, :]
            target = out.at[:, head_columns(place[1] ^ s)]
            copies.append(pltpu.make_async_copy(source, target, sems.at[s, k]))
            copies[-1].start()
    for copy in copies:
        copy.wait()


def local(
    queries, key_matrix, value_matrix, attention_output, output_gradient, log_sum_norm, doc_ids
):
    parts = KEY_VALUE_HEADS
    rows = queries.shape[0]
    count = lax.axis_size("tok")
    span = parts * rows
    reach = min(WINDOW, count * rows // 2)
    behind = min(-(-(reach - 1) // span), count // parts - 1)
    device = lax.axis_index("tok")
    place = jnp.stack([device // parts, device % parts]).astype(jnp.int32)
    width = GROUP * rows
    shape = jax.ShapeDtypeStruct

    def move(value, steps, s=0):
        pairs = [(t, ((t + steps * parts) % count) ^ s) for t in range(count)]
        return lax.ppermute(value, "tok", pairs)

    def exchange(pieces):
        return [pieces[0]] + [move(pieces[s], 0, s) for s in range(1, parts)]

    pieces = call(
        functools.partial(pack_keys, rows),
        (place, key_matrix, value_matrix, doc_ids.reshape(1, rows)),
        [shape((2 * rows + EXTRA, HEAD_SIZE), BF16)] * parts,
        scratch=[
            pltpu.VMEM((1, rows), jnp.int32),
            pltpu.SemaphoreType.DMA(()),
            pltpu.SemaphoreType.DMA((parts, 2)),
        ],
        specs=[HBM, HBM, HBM],
    )
    pieces = exchange(pieces)
    *query_pieces, token = call(
        functools.partial(pack_queries, rows),
        (place, queries, output_gradient, attention_output, log_sum_norm),
        [shape((2 * width + 3 * EXTRA, HEAD_SIZE), BF16)] * parts + [TOKEN],
        scratch=[
            pltpu.VMEM(queries.shape, BF16),
            pltpu.VMEM(queries.shape, BF16),
            pltpu.VMEM((parts, 2 * GROUP, rows), F32),
            pltpu.SemaphoreType.DMA((parts, 2, GROUP)),
            pltpu.SemaphoreType.DMA((2,)),
        ],
        specs=[HBM, HBM, HBM, VMEM],
    )
    (own,) = call(
        functools.partial(join, rows),
        (place, *pieces, token),
        [shape((parts * (2 * rows + EXTRA), HEAD_SIZE), BF16)],
    )
    query_pieces = exchange(query_pieces)
    windows = [own]
    for _ in range(behind):
        windows.append(move(windows[-1], 1))

    kv_shape = (2 * span, HEAD_SIZE)
    stages = [0] + list(range(behind, 0, -1))
    dq, own_pieces, sent = None, None, None
    for k, offset in enumerate(stages):
        first, last = k == 0, k == len(stages) - 1
        ins = [place, *query_pieces, own, windows[offset]]
        if not first:
            ins.append(dq)
        if last:
            outs = [shape((HEAD_SIZE, width), BF16)] * parts
        else:
            outs = [shape((parts, HEAD_SIZE, width), F32)]
        outs = outs + [shape(kv_shape, BF16 if offset == behind > 0 else F32)]
        got = call(
            functools.partial(attend, rows, offset, reach, first, last),
            ins,
            outs,
            scratch=attend_scratch(rows),
            flops=10 * span * span * GROUP * HEAD_SIZE,
        )
        dq, term = (got[:parts] if last else got[0]), got[-1]
        piece_shapes = [shape((2 * rows, HEAD_SIZE), BF16)] * parts
        if offset == 0:
            own_pieces = call(functools.partial(cut_terms, rows, 1), (place, term), piece_shapes)
            own_pieces = exchange(own_pieces)
        elif offset == 1:
            terms = (term,) if sent is None else (sent, term)
            got = call(
                functools.partial(cut_terms, rows, len(terms)), (place, *terms), piece_shapes
            )
            sent = [move(piece, -1, s) for s, piece in enumerate(got)]
        elif sent is None:
            sent = move(term, -1)
        else:
            (term,) = call(add_terms, (place, sent, term), [shape(kv_shape, BF16)])
            sent = move(term, -1)

    dq_pieces = exchange(dq)
    query_grad, token = call(
        functools.partial(spread_queries, rows),
        (place, *dq_pieces),
        [shape((rows, parts * GROUP * HEAD_SIZE), BF16), TOKEN],
        scratch=[
            pltpu.VMEM((parts, rows, GROUP * HEAD_SIZE), BF16),
            pltpu.SemaphoreType.DMA((parts,)),
        ],
        out_specs=[HBM, VMEM],
    )
    pieces = own_pieces + (sent or [])
    key_grad, value_grad = call(
        functools.partial(spread_keys, rows, len(pieces) // parts),
        (place, *pieces, token),
        [shape((rows, parts * HEAD_SIZE), BF16)] * 2,
        scratch=[
            pltpu.VMEM((parts, 2 * rows, HEAD_SIZE), BF16),
            pltpu.SemaphoreType.DMA((parts, 2)),
        ],
        out_specs=[HBM, HBM],
    )
    return query_grad, key_grad, value_grad


def solution(mesh):
    axes = ("groups", "tok")
    return jax.shard_map(
        local,
        mesh=mesh,
        in_specs=(
            P(axes, None),
            P(axes, None),
            P(axes, None),
            P(axes, None),
            P(axes, None),
            P(None, axes),
            P(axes),
        ),
        out_specs=(P(axes, None), P(axes, None), P(axes, None)),
        check_vma=False,
    )
```

```python
import functools
import math

import jax
import jax.numpy as jnp
from jax import lax
from jax.experimental import pallas as pl
from jax.experimental.pallas import tpu as pltpu
from jax.sharding import PartitionSpec as P

WINDOW = 4096
QUERY_HEADS = 16
KEY_VALUE_HEADS = 4
HEAD_SIZE = 128
GROUP = QUERY_HEADS // KEY_VALUE_HEADS
SCALE = HEAD_SIZE ** (-0.5)
LOG2E = math.log2(math.e)
EXTRA = 8
F32 = jnp.float32
BF16 = jnp.bfloat16

VMEM = pl.BlockSpec(memory_space=pltpu.VMEM)
SMEM = pl.BlockSpec(memory_space=pltpu.SMEM)


def dot(a, b, dims):
    return lax.dot_general(a, b, (dims, ((), ())), preferred_element_type=F32)


HBM = pl.BlockSpec(memory_space=pltpu.MemorySpace.HBM)
TOKEN = jax.ShapeDtypeStruct((8, 128), F32)


def call(kernel, ins, outs, scratch=(), flops=0, specs=None, out_specs=None):
    specs = specs or [VMEM] * (len(ins) - 1)
    ins = [ins[0]] + [
        pltpu.with_memory_space_constraint(x, pltpu.MemorySpace.HBM) if spec is HBM else x
        for x, spec in zip(ins[1:], specs)
    ]
    size = sum(math.prod(o.shape) * o.dtype.itemsize for o in outs)
    size += sum(math.prod(x.shape) * x.dtype.itemsize for x in ins)
    return pl.pallas_call(
        kernel,
        out_shape=outs,
        in_specs=[SMEM] + specs,
        out_specs=out_specs or [VMEM] * len(outs),
        scratch_shapes=list(scratch),
        cost_estimate=pl.CostEstimate(flops=flops, bytes_accessed=size, transcendentals=0),
        compiler_params=pltpu.CompilerParams(vmem_limit_bytes=48 << 20),
    )(*ins)


def head_columns(g):
    return pl.ds(pl.multiple_of(g * HEAD_SIZE, HEAD_SIZE), HEAD_SIZE)


def pack_keys(rows, place, key_ref, value_ref, doc_ref, *rest):
    outs, (ids, doc_sem, sems) = rest[:-3], rest[-3:]
    first = pltpu.make_async_copy(doc_ref, ids, doc_sem)
    first.start()
    copies = []
    for s, out in enumerate(outs):
        cut = head_columns(place[1] ^ s)
        for k, source in enumerate((key_ref, value_ref)):
            target = out.at[k * rows : (k + 1) * rows, :]
            copies.append(pltpu.make_async_copy(source.at[:, cut], target, sems.at[s, k]))
    for copy in copies:
        copy.start()
    first.wait()
    docs = jnp.broadcast_to((ids[...] + 1).astype(F32), (EXTRA, rows)).astype(BF16)
    for out in outs:
        out[2 * rows :, 0:rows] = docs
    for copy in copies:
        copy.wait()


def pack_queries(rows, place, query_ref, grad_ref, output_ref, norm_ref, doc_ref, *rest):
    outs, (token, grads, outputs, stats, sems, more_sems) = rest[:-6], rest[-6:]
    first = pltpu.make_async_copy(grad_ref, grads, more_sems.at[0])
    second = pltpu.make_async_copy(output_ref, outputs, more_sems.at[1])
    first.start()
    second.start()
    copies = []
    for s, out in enumerate(outs):
        for h in range(GROUP):
            cut = head_columns((place[1] ^ s) * GROUP + h)
            for k, source in enumerate((query_ref, grad_ref)):
                at = (k * GROUP + h) * rows
                target = out.at[at : at + rows, :]
                copies.append(pltpu.make_async_copy(source.at[:, cut], target, sems.at[s, k, h]))
    for copy in copies:
        copy.start()
    first.wait()
    second.wait()
    lane = lax.broadcasted_iota(jnp.int32, (rows, HEAD_SIZE), 1)
    columns = jnp.zeros((rows, HEAD_SIZE), F32)
    for h in range(QUERY_HEADS):
        cut = slice(h * HEAD_SIZE, (h + 1) * HEAD_SIZE)
        product = grads[:, cut].astype(F32) * outputs[:, cut].astype(F32)
        columns = jnp.where(lane == h, jnp.sum(product, 1, keepdims=True), columns)
    delta = columns.T
    for g in range(KEY_VALUE_HEADS):
        stats[g, 0:GROUP, :] = norm_ref[g * GROUP : (g + 1) * GROUP, :]
        stats[g, GROUP : 2 * GROUP, :] = delta[g * GROUP : (g + 1) * GROUP, :]
    docs = jnp.broadcast_to((doc_ref[...] + 1).astype(F32), (EXTRA, rows)).astype(BF16)
    for s, out in enumerate(outs):
        out[2 * GROUP * rows + 3 * EXTRA :, 0:rows] = docs
        left = stats[place[1] ^ s]
        for part in range(3):
            term = left.astype(BF16)
            at = 2 * GROUP * rows + part * EXTRA
            out[at : at + EXTRA, 0:rows] = term
            left = left - term.astype(F32)
    for copy in copies:
        copy.wait()
    token[...] = jnp.zeros_like(token)


def join(rows, place, *refs):
    parts = KEY_VALUE_HEADS
    pieces, out = refs[:parts], refs[-1]
    span = parts * rows
    for s, piece in enumerate(pieces):
        a = place[1] ^ s
        for k in range(2):
            at = pl.multiple_of(k * span + a * rows, rows)
            out[pl.ds(at, rows), :] = piece[k * rows : (k + 1) * rows, :]
        at = pl.multiple_of(2 * span + a * EXTRA, EXTRA)
        out[pl.ds(at, EXTRA), :] = piece[2 * rows :, :]


def attend_scratch(rows):
    parts = KEY_VALUE_HEADS
    return [
        pltpu.VMEM((2 * parts * rows, HEAD_SIZE), F32),
        pltpu.VMEM((HEAD_SIZE, parts * rows), BF16),
        pltpu.VMEM((parts * rows, rows), F32),
    ]


def attend(rows, offset, reach, first, last, place, *refs):
    parts = KEY_VALUE_HEADS
    queries, refs = refs[:parts], refs[parts:]
    key_ref, refs = refs[0], refs[1:]
    if not first:
        dq_in, refs = refs[0], refs[1:]
    if last:
        dq_out, refs = refs[:parts], refs[parts:]
    else:
        dq_out, refs = refs[0], refs[1:]
    kv_out, dkv, key_t, docs_t = refs
    row, me = place[0], place[1]
    width = GROUP * rows
    span = parts * rows

    def ids(ref, start, stop):
        return ref[2 * span + start * EXTRA : 2 * span + stop * EXTRA, 0:rows].astype(F32)

    ends = [jnp.max(ids(key_ref, k * parts // 2, (k + 1) * parts // 2)) for k in range(2)]
    dkv[...] = jnp.zeros_like(dkv)

    @pl.when(row >= offset)
    def _():
        for b in range(parts):
            cut = slice(b * rows, (b + 1) * rows)
            key_t[:, cut] = key_ref[cut, :].T
            docs_t[cut, :] = jnp.broadcast_to(ids(key_ref, b, b + 1)[0:1], (rows, rows)).T

    def add_query_grad(s, term=None):
        total = term if first else dq_in[s]
        if not first and term is not None:
            total = total + term
        if last:
            dq_out[s][...] = total.astype(BF16)
        else:
            dq_out[s] = total

    half = span // 2
    for s in range(parts):
        a = me ^ s
        near = offset * span + a * rows
        start = jnp.min(queries[s][2 * width + 3 * EXTRA :, 0:rows].astype(F32))
        low = (near - half + 1 < reach) & (row >= offset) & (start <= ends[0])
        high = (near - span + 1 < reach) & (row >= offset) & (start <= ends[1])
        if offset == 0:
            high = high & (a * rows + rows > half)

        def block(start, stop, s=s, a=a, near=near):
            docs = queries[s][2 * width + 3 * EXTRA :, 0:rows].astype(F32)[0:1]
            query = queries[s][0:width, :]
            grad = queries[s][width : 2 * width, :]
            stats = queries[s][2 * width : 2 * width + 3 * EXTRA, :].astype(F32)
            stats = stats[0:EXTRA] + stats[EXTRA : 2 * EXTRA] + stats[2 * EXTRA :]
            gap = (
                near
                - start
                + lax.broadcasted_iota(jnp.int32, (stop - start, rows), 1)
                - lax.broadcasted_iota(jnp.int32, (stop - start, rows), 0)
            )
            mask = docs_t[start:stop, :] == docs
            if offset == 0:
                mask = mask & (gap >= 0)
            if (offset + 1) * span > WINDOW:
                mask = mask & (gap < WINDOW)
            scores = dot(key_ref[start:stop, :], query, ((1,), (1,)))
            dprob = dot(key_ref[span + start : span + stop, :], grad, ((1,), (1,)))
            probs, dscores = [], []
            for h in range(GROUP):
                cut = slice(h * rows, (h + 1) * rows)
                norm = stats[h : h + 1, :] * LOG2E
                delta = stats[GROUP + h : GROUP + h + 1, :]
                prob = jnp.exp2(scores[:, cut] * (SCALE * LOG2E) - norm)
                prob = jnp.where(mask, prob, 0.0)
                probs.append(prob.astype(BF16))
                dscores.append((prob * (dprob[:, cut] - delta) * SCALE).astype(BF16))
            prob = jnp.concatenate(probs, 1)
            dscore = jnp.concatenate(dscores, 1)
            dkv[start:stop, :] += dot(dscore, query, ((1,), (0,)))
            dkv[span + start : span + stop, :] += dot(prob, grad, ((1,), (0,)))
            add_query_grad(s, dot(key_t[:, start:stop], dscore, ((1,), (0,))))

        pl.when(low & high)(functools.partial(block, 0, span))
        pl.when(high & ~low)(functools.partial(block, half, span))
        if offset == 0:
            pl.when(low & ~high)(functools.partial(block, 0, half))
        else:
            pl.when(~high)(functools.partial(add_query_grad, s))

    kv_out[...] = dkv[...].astype(kv_out.dtype)


def add_terms(place, arrived, term, out):
    out[...] = (arrived[...].astype(F32) + term[...]).astype(BF16)


def cut_terms(rows, count, place, *refs):
    parts = KEY_VALUE_HEADS
    terms, outs = refs[:count], refs[-parts:]
    for s, out in enumerate(outs):
        for k in range(2):
            at = pl.multiple_of((k * parts + (place[1] ^ s)) * rows, rows)
            total = sum(term[pl.ds(at, rows), :].astype(F32) for term in terms)
            out[k * rows : (k + 1) * rows, :] = total.astype(BF16)


def spread_queries(rows, place, *refs):
    pieces, (out, token, turned, sems) = refs[:-4], refs[-4:]
    width = GROUP * HEAD_SIZE
    copies = []
    for s, piece in enumerate(pieces):
        for h in range(GROUP):
            cut = slice(h * HEAD_SIZE, (h + 1) * HEAD_SIZE)
            turned[s, :, cut] = piece[:, h * rows : (h + 1) * rows].T
        cut = pl.ds(pl.multiple_of((place[1] ^ s) * width, width), width)
        copies.append(pltpu.make_async_copy(turned.at[s], out.at[:, cut], sems.at[s]))
        copies[-1].start()
    token[...] = jnp.zeros_like(token)
    for copy in copies:
        copy.wait()


def spread_keys(rows, sources, place, *refs):
    parts = KEY_VALUE_HEADS
    pieces, (key_out, value_out, total, sems) = refs[:-5], refs[-4:]
    copies = []
    for s in range(parts):
        term = pieces[s][...].astype(F32)
        for k in range(1, sources):
            term = term + pieces[k * parts + s][...].astype(F32)
        total[s] = term.astype(BF16)
        for k, out in enumerate((key_out, value_out)):
            source = total.at[s, k * rows : (k + 1) * rows, :]
            target = out.at[:, head_columns(place[1] ^ s)]
            copies.append(pltpu.make_async_copy(source, target, sems.at[s, k]))
            copies[-1].start()
    for copy in copies:
        copy.wait()


def local(
    queries, key_matrix, value_matrix, attention_output, output_gradient, log_sum_norm, doc_ids
):
    parts = KEY_VALUE_HEADS
    rows = queries.shape[0]
    count = lax.axis_size("tok")
    span = parts * rows
    reach = min(WINDOW, count * rows // 2)
    behind = min(-(-(reach - 1) // span), count // parts - 1)
    device = lax.axis_index("tok")
    place = jnp.stack([device // parts, device % parts]).astype(jnp.int32)
    width = GROUP * rows
    shape = jax.ShapeDtypeStruct

    def move(value, steps, s=0):
        pairs = [(t, ((t + steps * parts) % count) ^ s) for t in range(count)]
        return lax.ppermute(value, "tok", pairs)

    def lower(value, offset):
        pairs = [(t, t - parts) for t in range(offset * parts, count)]
        return lax.ppermute(value, "tok", pairs)

    def exchange(pieces):
        return [pieces[0]] + [move(pieces[s], 0, s) for s in range(1, parts)]

    pieces = call(
        functools.partial(pack_keys, rows),
        (place, key_matrix, value_matrix, doc_ids.reshape(1, rows)),
        [shape((2 * rows + EXTRA, HEAD_SIZE), BF16)] * parts,
        scratch=[
            pltpu.VMEM((1, rows), jnp.int32),
            pltpu.SemaphoreType.DMA(()),
            pltpu.SemaphoreType.DMA((parts, 2)),
        ],
        specs=[HBM, HBM, HBM],
    )
    pieces = exchange(pieces)
    *query_pieces, token = call(
        functools.partial(pack_queries, rows),
        (place, queries, output_gradient, attention_output, log_sum_norm, doc_ids.reshape(1, rows)),
        [shape((2 * width + 4 * EXTRA, HEAD_SIZE), BF16)] * parts + [TOKEN],
        scratch=[
            pltpu.VMEM(queries.shape, BF16),
            pltpu.VMEM(queries.shape, BF16),
            pltpu.VMEM((parts, 2 * GROUP, rows), F32),
            pltpu.SemaphoreType.DMA((parts, 2, GROUP)),
            pltpu.SemaphoreType.DMA((2,)),
        ],
        specs=[HBM, HBM, HBM, VMEM, VMEM],
    )
    (own,) = call(
        functools.partial(join, rows),
        (place, *pieces, token),
        [shape((parts * (2 * rows + EXTRA), HEAD_SIZE), BF16)],
    )
    query_pieces = exchange(query_pieces)
    windows = [own]
    for _ in range(behind):
        windows.append(move(windows[-1], 1))

    kv_shape = (2 * span, HEAD_SIZE)
    stages = [0] + list(range(behind, 0, -1))
    dq, own_pieces, sent = None, None, None
    for k, offset in enumerate(stages):
        first, last = k == 0, k == len(stages) - 1
        ins = [place, *query_pieces, windows[offset]]
        if not first:
            ins.append(dq)
        if last:
            outs = [shape((HEAD_SIZE, width), BF16)] * parts
        else:
            outs = [shape((parts, HEAD_SIZE, width), F32)]
        outs = outs + [shape(kv_shape, BF16 if offset == behind > 0 else F32)]
        got = call(
            functools.partial(attend, rows, offset, reach, first, last),
            ins,
            outs,
            scratch=attend_scratch(rows),
            flops=10 * span * span * GROUP * HEAD_SIZE,
        )
        dq, term = (got[:parts] if last else got[0]), got[-1]
        piece_shapes = [shape((2 * rows, HEAD_SIZE), BF16)] * parts
        if offset == 0:
            own_pieces = call(functools.partial(cut_terms, rows, 1), (place, term), piece_shapes)
            own_pieces = exchange(own_pieces)
        elif offset == 1:
            terms = (term,) if sent is None else (sent, term)
            got = call(
                functools.partial(cut_terms, rows, len(terms)), (place, *terms), piece_shapes
            )
            sent = [move(piece, -1, s) for s, piece in enumerate(got)]
        elif sent is None:
            sent = lower(term, offset)
        else:
            (term,) = call(add_terms, (place, sent, term), [shape(kv_shape, BF16)])
            sent = lower(term, offset)

    dq_pieces = exchange(dq)
    query_grad, token = call(
        functools.partial(spread_queries, rows),
        (place, *dq_pieces),
        [shape((rows, parts * GROUP * HEAD_SIZE), BF16), TOKEN],
        scratch=[
            pltpu.VMEM((parts, rows, GROUP * HEAD_SIZE), BF16),
            pltpu.SemaphoreType.DMA((parts,)),
        ],
        out_specs=[HBM, VMEM],
    )
    pieces = own_pieces + (sent or [])
    key_grad, value_grad = call(
        functools.partial(spread_keys, rows, len(pieces) // parts),
        (place, *pieces, token),
        [shape((rows, parts * HEAD_SIZE), BF16)] * 2,
        scratch=[
            pltpu.VMEM((parts, 2 * rows, HEAD_SIZE), BF16),
            pltpu.SemaphoreType.DMA((parts, 2)),
        ],
        out_specs=[HBM, HBM],
    )
    return query_grad, key_grad, value_grad


def solution(mesh):
    axes = ("groups", "tok")
    return jax.shard_map(
        local,
        mesh=mesh,
        in_specs=(
            P(axes, None),
            P(axes, None),
            P(axes, None),
            P(axes, None),
            P(axes, None),
            P(None, axes),
            P(axes),
        ),
        out_specs=(P(axes, None), P(axes, None), P(axes, None)),
        check_vma=False,
    )
```

```python
import functools
import math

import jax
import jax.numpy as jnp
from jax import lax
from jax.experimental import pallas as pl
from jax.experimental.pallas import tpu as pltpu
from jax.sharding import PartitionSpec as P

WINDOW = 4096
QUERY_HEADS = 16
KEY_VALUE_HEADS = 4
HEAD_SIZE = 128
GROUP = QUERY_HEADS // KEY_VALUE_HEADS
SCALE = HEAD_SIZE ** (-0.5)
LOG2E = math.log2(math.e)
EXTRA = 8
F32 = jnp.float32
BF16 = jnp.bfloat16

VMEM = pl.BlockSpec(memory_space=pltpu.VMEM)
SMEM = pl.BlockSpec(memory_space=pltpu.SMEM)


def dot(a, b, dims):
    return lax.dot_general(a, b, (dims, ((), ())), preferred_element_type=F32)


HBM = pl.BlockSpec(memory_space=pltpu.MemorySpace.HBM)
TOKEN = jax.ShapeDtypeStruct((8, 128), F32)


def call(kernel, ins, outs, scratch=(), flops=0, specs=None, out_specs=None):
    specs = specs or [VMEM] * (len(ins) - 1)
    ins = [ins[0]] + [
        pltpu.with_memory_space_constraint(x, pltpu.MemorySpace.HBM) if spec is HBM else x
        for x, spec in zip(ins[1:], specs)
    ]
    size = sum(math.prod(o.shape) * o.dtype.itemsize for o in outs)
    size += sum(math.prod(x.shape) * x.dtype.itemsize for x in ins)
    return pl.pallas_call(
        kernel,
        out_shape=outs,
        in_specs=[SMEM] + specs,
        out_specs=out_specs or [VMEM] * len(outs),
        scratch_shapes=list(scratch),
        cost_estimate=pl.CostEstimate(flops=flops, bytes_accessed=size, transcendentals=0),
        compiler_params=pltpu.CompilerParams(vmem_limit_bytes=48 << 20),
    )(*ins)


def head_columns(g):
    return pl.ds(pl.multiple_of(g * HEAD_SIZE, HEAD_SIZE), HEAD_SIZE)


def pack_keys(rows, place, key_ref, value_ref, doc_ref, grad_ref, output_ref, *rest):
    outs, (grads, outputs, ids, doc_sem, sems, more_sems) = rest[:-6], rest[-6:]
    first = pltpu.make_async_copy(doc_ref, ids, doc_sem)
    first.start()
    copies = []
    for s, out in enumerate(outs):
        cut = head_columns(place[1] ^ s)
        for k, source in enumerate((key_ref, value_ref)):
            target = out.at[k * rows : (k + 1) * rows, :]
            copies.append(pltpu.make_async_copy(source.at[:, cut], target, sems.at[s, k]))
    copies.append(pltpu.make_async_copy(grad_ref, grads, more_sems.at[0]))
    copies.append(pltpu.make_async_copy(output_ref, outputs, more_sems.at[1]))
    for copy in copies:
        copy.start()
    first.wait()
    docs = jnp.broadcast_to((ids[...] + 1).astype(F32), (EXTRA, rows)).astype(BF16)
    for out in outs:
        out[2 * rows :, 0:rows] = docs
    for copy in copies:
        copy.wait()


def pack_queries(rows, place, query_ref, grads, outputs, norm_ref, *rest):
    outs, (token, stats, sems) = rest[:-3], rest[-3:]
    copies = []
    for s, out in enumerate(outs):
        for h in range(GROUP):
            cut = head_columns((place[1] ^ s) * GROUP + h)
            target = out.at[h * rows : (h + 1) * rows, :]
            copies.append(pltpu.make_async_copy(query_ref.at[:, cut], target, sems.at[s, h]))
    for copy in copies:
        copy.start()
    for s, out in enumerate(outs):
        for h in range(GROUP):
            at = (GROUP + h) * rows
            out[at : at + rows, :] = grads[:, head_columns((place[1] ^ s) * GROUP + h)]
    lane = lax.broadcasted_iota(jnp.int32, (rows, HEAD_SIZE), 1)
    columns = jnp.zeros((rows, HEAD_SIZE), F32)
    for h in range(QUERY_HEADS):
        cut = slice(h * HEAD_SIZE, (h + 1) * HEAD_SIZE)
        product = grads[:, cut].astype(F32) * outputs[:, cut].astype(F32)
        columns = jnp.where(lane == h, jnp.sum(product, 1, keepdims=True), columns)
    delta = columns.T
    for g in range(KEY_VALUE_HEADS):
        stats[g, 0:GROUP, :] = norm_ref[g * GROUP : (g + 1) * GROUP, :]
        stats[g, GROUP : 2 * GROUP, :] = delta[g * GROUP : (g + 1) * GROUP, :]
    for s, out in enumerate(outs):
        left = stats[place[1] ^ s]
        for part in range(3):
            term = left.astype(BF16)
            at = 2 * GROUP * rows + part * EXTRA
            out[at : at + EXTRA, 0:rows] = term
            left = left - term.astype(F32)
    for copy in copies:
        copy.wait()
    token[...] = jnp.zeros_like(token)


def join(rows, place, *refs):
    parts = KEY_VALUE_HEADS
    pieces, out = refs[:parts], refs[-1]
    span = parts * rows
    for s, piece in enumerate(pieces):
        a = place[1] ^ s
        for k in range(2):
            at = pl.multiple_of(k * span + a * rows, rows)
            out[pl.ds(at, rows), :] = piece[k * rows : (k + 1) * rows, :]
        at = pl.multiple_of(2 * span + a * EXTRA, EXTRA)
        out[pl.ds(at, EXTRA), :] = piece[2 * rows :, :]


def attend_scratch(rows):
    parts = KEY_VALUE_HEADS
    return [
        pltpu.VMEM((parts, HEAD_SIZE, GROUP * rows), F32),
        pltpu.VMEM((2 * parts * rows, HEAD_SIZE), F32),
        pltpu.VMEM((HEAD_SIZE, parts * rows), BF16),
        pltpu.VMEM((parts * rows, rows), F32),
        pltpu.SMEM((2 * parts,), F32),
    ]


def attend(rows, offset, reach, first, last, place, *refs):
    parts = KEY_VALUE_HEADS
    queries, refs = refs[:parts], refs[parts:]
    own, key_ref, refs = refs[0], refs[1], refs[2:]
    if not first:
        dq_in, refs = refs[0], refs[1:]
    if last:
        dq_out, refs = refs[:parts], refs[parts:]
    else:
        dq_out, refs = refs[0], refs[1:]
    kv_out, dq, dkv, key_t, docs_t, docs_s = refs
    row, me = place[0], place[1]
    width = GROUP * rows
    span = parts * rows

    def work():
        for a in range(parts):
            docs = own[2 * span + a * EXTRA : 2 * span + a * EXTRA + 1, 0:rows].astype(F32)
            docs_s[a] = jnp.min(docs)
        dq[...] = jnp.zeros_like(dq)
        dkv[...] = jnp.zeros_like(dkv)
        for b in range(parts):
            cut = slice(b * rows, (b + 1) * rows)
            key_t[:, cut] = key_ref[cut, :].T
            docs = key_ref[2 * span + b * EXTRA : 2 * span + b * EXTRA + 1, 0:rows].astype(F32)
            docs_t[cut, :] = jnp.broadcast_to(docs, (rows, rows)).T
            if (b + 1) % (parts // 2) == 0:
                docs_s[parts + b // (parts // 2)] = jnp.max(docs)
        half = span // 2
        for s in range(parts):
            a = me ^ s
            near = offset * span + a * rows
            low = (near - half + 1 < reach) & (docs_s[a] <= docs_s[parts])
            high = (near - span + 1 < reach) & (docs_s[a] <= docs_s[parts + 1])
            if offset == 0:
                high = high & (a * rows + rows > half)

            def block(start, stop, s=s, a=a, near=near):
                docs = own[pl.ds(pl.multiple_of(2 * span + a * EXTRA, EXTRA), EXTRA), :]
                docs = docs.astype(F32)[0:1, 0:rows]
                query = queries[s][0:width, :]
                grad = queries[s][width : 2 * width, :]
                stats = queries[s][2 * width :, :].astype(F32)
                stats = stats[0:EXTRA] + stats[EXTRA : 2 * EXTRA] + stats[2 * EXTRA :]
                gap = (
                    near
                    - start
                    + lax.broadcasted_iota(jnp.int32, (stop - start, rows), 1)
                    - lax.broadcasted_iota(jnp.int32, (stop - start, rows), 0)
                )
                mask = docs_t[start:stop, :] == docs
                if offset == 0:
                    mask = mask & (gap >= 0)
                if (offset + 1) * span > WINDOW:
                    mask = mask & (gap < WINDOW)
                scores = dot(key_ref[start:stop, :], query, ((1,), (1,)))
                dprob = dot(key_ref[span + start : span + stop, :], grad, ((1,), (1,)))
                probs, dscores = [], []
                for h in range(GROUP):
                    cut = slice(h * rows, (h + 1) * rows)
                    norm = stats[h : h + 1, :] * LOG2E
                    delta = stats[GROUP + h : GROUP + h + 1, :]
                    prob = jnp.exp2(scores[:, cut] * (SCALE * LOG2E) - norm)
                    prob = jnp.where(mask, prob, 0.0)
                    probs.append(prob.astype(BF16))
                    dscores.append((prob * (dprob[:, cut] - delta) * SCALE).astype(BF16))
                prob = jnp.concatenate(probs, 1)
                dscore = jnp.concatenate(dscores, 1)
                dkv[start:stop, :] += dot(dscore, query, ((1,), (0,)))
                dkv[span + start : span + stop, :] += dot(prob, grad, ((1,), (0,)))
                dq[s] += dot(key_t[:, start:stop], dscore, ((1,), (0,)))

            pl.when(low & high)(functools.partial(block, 0, span))
            pl.when(high & ~low)(functools.partial(block, half, span))
            if offset == 0:
                pl.when(low & ~high)(functools.partial(block, 0, half))

        kv_out[...] = dkv[...].astype(kv_out.dtype)
        for s in range(parts):
            total = dq[s] if first else dq[s] + dq_in[s]
            if last:
                dq_out[s][...] = total.astype(BF16)
            else:
                dq_out[s] = total

    if first:
        work()
        return

    @pl.when(row < offset)
    def _():
        kv_out[...] = jnp.zeros_like(kv_out)
        for s in range(parts):
            if last:
                dq_out[s][...] = dq_in[s].astype(BF16)
            else:
                dq_out[s] = dq_in[s]

    pl.when(row >= offset)(work)


def add_terms(place, arrived, term, out):
    out[...] = (arrived[...].astype(F32) + term[...]).astype(BF16)


def cut_terms(rows, count, place, *refs):
    parts = KEY_VALUE_HEADS
    terms, outs = refs[:count], refs[-parts:]
    for s, out in enumerate(outs):
        for k in range(2):
            at = pl.multiple_of((k * parts + (place[1] ^ s)) * rows, rows)
            total = sum(term[pl.ds(at, rows), :].astype(F32) for term in terms)
            out[k * rows : (k + 1) * rows, :] = total.astype(BF16)


def spread_queries(rows, place, *refs):
    pieces, (out, token, turned, sems) = refs[:-4], refs[-4:]
    width = GROUP * HEAD_SIZE
    copies = []
    for s, piece in enumerate(pieces):
        for h in range(GROUP):
            cut = slice(h * HEAD_SIZE, (h + 1) * HEAD_SIZE)
            turned[s, :, cut] = piece[:, h * rows : (h + 1) * rows].T
        cut = pl.ds(pl.multiple_of((place[1] ^ s) * width, width), width)
        copies.append(pltpu.make_async_copy(turned.at[s], out.at[:, cut], sems.at[s]))
        copies[-1].start()
    token[...] = jnp.zeros_like(token)
    for copy in copies:
        copy.wait()


def spread_keys(rows, sources, place, *refs):
    parts = KEY_VALUE_HEADS
    pieces, (key_out, value_out, total, sems) = refs[:-5], refs[-4:]
    copies = []
    for s in range(parts):
        term = pieces[s][...].astype(F32)
        for k in range(1, sources):
            term = term + pieces[k * parts + s][...].astype(F32)
        total[s] = term.astype(BF16)
        for k, out in enumerate((key_out, value_out)):
            source = total.at[s, k * rows : (k + 1) * rows, :]
            target = out.at[:, head_columns(place[1] ^ s)]
            copies.append(pltpu.make_async_copy(source, target, sems.at[s, k]))
            copies[-1].start()
    for copy in copies:
        copy.wait()


def local(
    queries, key_matrix, value_matrix, attention_output, output_gradient, log_sum_norm, doc_ids
):
    parts = KEY_VALUE_HEADS
    rows = queries.shape[0]
    count = lax.axis_size("tok")
    span = parts * rows
    reach = min(WINDOW, count * rows // 2)
    behind = min(-(-(reach - 1) // span), count // parts - 1)
    device = lax.axis_index("tok")
    place = jnp.stack([device // parts, device % parts]).astype(jnp.int32)
    width = GROUP * rows
    shape = jax.ShapeDtypeStruct

    def move(value, steps, s=0):
        pairs = [(t, ((t + steps * parts) % count) ^ s) for t in range(count)]
        return lax.ppermute(value, "tok", pairs)

    def exchange(pieces):
        return [pieces[0]] + [move(pieces[s], 0, s) for s in range(1, parts)]

    *pieces, grads, outputs = call(
        functools.partial(pack_keys, rows),
        (place, key_matrix, value_matrix, doc_ids.reshape(1, rows), output_gradient, attention_output),
        [shape((2 * rows + EXTRA, HEAD_SIZE), BF16)] * parts + [shape(queries.shape, BF16)] * 2,
        scratch=[
            pltpu.VMEM((1, rows), jnp.int32),
            pltpu.SemaphoreType.DMA(()),
            pltpu.SemaphoreType.DMA((parts, 2)),
            pltpu.SemaphoreType.DMA((2,)),
        ],
        specs=[HBM] * 5,
    )
    pieces = exchange(pieces)
    *query_pieces, token = call(
        functools.partial(pack_queries, rows),
        (place, queries, grads, outputs, log_sum_norm),
        [shape((2 * width + 3 * EXTRA, HEAD_SIZE), BF16)] * parts + [TOKEN],
        scratch=[
            pltpu.VMEM((parts, 2 * GROUP, rows), F32),
            pltpu.SemaphoreType.DMA((parts, GROUP)),
        ],
        specs=[HBM, VMEM, VMEM, VMEM],
    )
    (own,) = call(
        functools.partial(join, rows),
        (place, *pieces, token),
        [shape((parts * (2 * rows + EXTRA), HEAD_SIZE), BF16)],
    )
    query_pieces = exchange(query_pieces)
    windows = [own]
    for _ in range(behind):
        windows.append(move(windows[-1], 1))

    kv_shape = (2 * span, HEAD_SIZE)
    stages = [0] + list(range(behind, 0, -1))
    dq, own_pieces, sent = None, None, None
    for k, offset in enumerate(stages):
        first, last = k == 0, k == len(stages) - 1
        ins = [place, *query_pieces, own, windows[offset]]
        if not first:
            ins.append(dq)
        if last:
            outs = [shape((HEAD_SIZE, width), BF16)] * parts
        else:
            outs = [shape((parts, HEAD_SIZE, width), F32)]
        outs = outs + [shape(kv_shape, BF16 if offset == behind > 0 else F32)]
        got = call(
            functools.partial(attend, rows, offset, reach, first, last),
            ins,
            outs,
            scratch=attend_scratch(rows),
            flops=10 * span * span * GROUP * HEAD_SIZE,
        )
        dq, term = (got[:parts] if last else got[0]), got[-1]
        piece_shapes = [shape((2 * rows, HEAD_SIZE), BF16)] * parts
        if offset == 0:
            own_pieces = call(functools.partial(cut_terms, rows, 1), (place, term), piece_shapes)
            own_pieces = exchange(own_pieces)
        elif offset == 1:
            terms = (term,) if sent is None else (sent, term)
            got = call(
                functools.partial(cut_terms, rows, len(terms)), (place, *terms), piece_shapes
            )
            sent = [move(piece, -1, s) for s, piece in enumerate(got)]
        elif sent is None:
            sent = move(term, -1)
        else:
            (term,) = call(add_terms, (place, sent, term), [shape(kv_shape, BF16)])
            sent = move(term, -1)

    dq_pieces = exchange(dq)
    query_grad, token = call(
        functools.partial(spread_queries, rows),
        (place, *dq_pieces),
        [shape((rows, parts * GROUP * HEAD_SIZE), BF16), TOKEN],
        scratch=[
            pltpu.VMEM((parts, rows, GROUP * HEAD_SIZE), BF16),
            pltpu.SemaphoreType.DMA((parts,)),
        ],
        out_specs=[HBM, VMEM],
    )
    pieces = own_pieces + (sent or [])
    key_grad, value_grad = call(
        functools.partial(spread_keys, rows, len(pieces) // parts),
        (place, *pieces, token),
        [shape((rows, parts * HEAD_SIZE), BF16)] * 2,
        scratch=[
            pltpu.VMEM((parts, 2 * rows, HEAD_SIZE), BF16),
            pltpu.SemaphoreType.DMA((parts, 2)),
        ],
        out_specs=[HBM, HBM],
    )
    return query_grad, key_grad, value_grad


def solution(mesh):
    axes = ("groups", "tok")
    return jax.shard_map(
        local,
        mesh=mesh,
        in_specs=(
            P(axes, None),
            P(axes, None),
            P(axes, None),
            P(axes, None),
            P(axes, None),
            P(None, axes),
            P(axes),
        ),
        out_specs=(P(axes, None), P(axes, None), P(axes, None)),
        check_vma=False,
    )
```

```python
import functools
import math

import jax
import jax.numpy as jnp
from jax import lax
from jax.experimental import pallas as pl
from jax.experimental.pallas import tpu as pltpu
from jax.sharding import PartitionSpec as P

WINDOW = 4096
QUERY_HEADS = 16
KEY_VALUE_HEADS = 4
HEAD_SIZE = 128
GROUP = QUERY_HEADS // KEY_VALUE_HEADS
SCALE = HEAD_SIZE ** (-0.5)
LOG2E = math.log2(math.e)
EXTRA = 8
F32 = jnp.float32
BF16 = jnp.bfloat16

VMEM = pl.BlockSpec(memory_space=pltpu.VMEM)
SMEM = pl.BlockSpec(memory_space=pltpu.SMEM)


def dot(a, b, dims):
    return lax.dot_general(a, b, (dims, ((), ())), preferred_element_type=F32)


HBM = pl.BlockSpec(memory_space=pltpu.MemorySpace.HBM)
TOKEN = jax.ShapeDtypeStruct((8, 128), F32)


def call(kernel, ins, outs, scratch=(), flops=0, specs=None, out_specs=None):
    specs = specs or [VMEM] * (len(ins) - 1)
    ins = [ins[0]] + [
        pltpu.with_memory_space_constraint(x, pltpu.MemorySpace.HBM) if spec is HBM else x
        for x, spec in zip(ins[1:], specs)
    ]
    size = sum(math.prod(o.shape) * o.dtype.itemsize for o in outs)
    size += sum(math.prod(x.shape) * x.dtype.itemsize for x in ins)
    return pl.pallas_call(
        kernel,
        out_shape=outs,
        in_specs=[SMEM] + specs,
        out_specs=out_specs or [VMEM] * len(outs),
        scratch_shapes=list(scratch),
        cost_estimate=pl.CostEstimate(flops=flops, bytes_accessed=size, transcendentals=0),
        compiler_params=pltpu.CompilerParams(vmem_limit_bytes=48 << 20),
    )(*ins)


def head_columns(g):
    return pl.ds(pl.multiple_of(g * HEAD_SIZE, HEAD_SIZE), HEAD_SIZE)


def pack_keys(rows, place, key_ref, value_ref, doc_ref, grad_ref, output_ref, *rest):
    outs, (grads, outputs, ids, doc_sem, sems, more_sems) = rest[:-6], rest[-6:]
    first = pltpu.make_async_copy(doc_ref, ids, doc_sem)
    first.start()
    copies = []
    for s, out in enumerate(outs):
        cut = head_columns(place[1] ^ s)
        for k, source in enumerate((key_ref, value_ref)):
            target = out.at[k * rows : (k + 1) * rows, :]
            copies.append(pltpu.make_async_copy(source.at[:, cut], target, sems.at[s, k]))
    copies.append(pltpu.make_async_copy(grad_ref, grads, more_sems.at[0]))
    copies.append(pltpu.make_async_copy(output_ref, outputs, more_sems.at[1]))
    for copy in copies:
        copy.start()
    first.wait()
    docs = jnp.broadcast_to((ids[...] + 1).astype(F32), (EXTRA, rows)).astype(BF16)
    for out in outs:
        out[2 * rows :, 0:rows] = docs
    for copy in copies:
        copy.wait()


def pack_queries(rows, place, query_ref, grads, outputs, norm_ref, *rest):
    outs, (token, stats, sems) = rest[:-3], rest[-3:]
    copies = []
    for s, out in enumerate(outs):
        for h in range(GROUP):
            cut = head_columns((place[1] ^ s) * GROUP + h)
            target = out.at[h * rows : (h + 1) * rows, :]
            copies.append(pltpu.make_async_copy(query_ref.at[:, cut], target, sems.at[s, h]))
    for copy in copies:
        copy.start()
    for s, out in enumerate(outs):
        for h in range(GROUP):
            at = (GROUP + h) * rows
            out[at : at + rows, :] = grads[:, head_columns((place[1] ^ s) * GROUP + h)]
    lane = lax.broadcasted_iota(jnp.int32, (rows, HEAD_SIZE), 1)
    columns = jnp.zeros((rows, HEAD_SIZE), F32)
    for h in range(QUERY_HEADS):
        cut = slice(h * HEAD_SIZE, (h + 1) * HEAD_SIZE)
        product = grads[:, cut].astype(F32) * outputs[:, cut].astype(F32)
        columns = jnp.where(lane == h, jnp.sum(product, 1, keepdims=True), columns)
    delta = columns.T
    for g in range(KEY_VALUE_HEADS):
        stats[g, 0:GROUP, :] = norm_ref[g * GROUP : (g + 1) * GROUP, :]
        stats[g, GROUP : 2 * GROUP, :] = delta[g * GROUP : (g + 1) * GROUP, :]
    for s, out in enumerate(outs):
        left = stats[place[1] ^ s]
        for part in range(3):
            term = left.astype(BF16)
            at = 2 * GROUP * rows + part * EXTRA
            out[at : at + EXTRA, 0:rows] = term
            left = left - term.astype(F32)
    for copy in copies:
        copy.wait()
    token[...] = jnp.zeros_like(token)


def join(rows, place, *refs):
    parts = KEY_VALUE_HEADS
    pieces, out = refs[:parts], refs[-1]
    span = parts * rows
    for s, piece in enumerate(pieces):
        a = place[1] ^ s
        for k in range(2):
            at = pl.multiple_of(k * span + a * rows, rows)
            out[pl.ds(at, rows), :] = piece[k * rows : (k + 1) * rows, :]
        at = pl.multiple_of(2 * span + a * EXTRA, EXTRA)
        out[pl.ds(at, EXTRA), :] = piece[2 * rows :, :]


def attend_scratch(rows):
    parts = KEY_VALUE_HEADS
    return [
        pltpu.VMEM((parts, HEAD_SIZE, GROUP * rows), F32),
        pltpu.VMEM((2 * parts * rows, HEAD_SIZE), F32),
        pltpu.VMEM((HEAD_SIZE, parts * rows), BF16),
        pltpu.VMEM((parts * rows, rows), F32),
        pltpu.SMEM((2 * parts,), F32),
    ]


def attend(rows, offset, reach, first, last, place, *refs):
    parts = KEY_VALUE_HEADS
    queries, refs = refs[:parts], refs[parts:]
    own, key_ref, refs = refs[0], refs[1], refs[2:]
    if not first:
        dq_in, refs = refs[0], refs[1:]
    if last:
        dq_out, refs = refs[:parts], refs[parts:]
    else:
        dq_out, refs = refs[0], refs[1:]
    kv_out, dq, dkv, key_t, docs_t, docs_s = refs
    row, me = place[0], place[1]
    width = GROUP * rows
    span = parts * rows

    def work():
        for a in range(parts):
            docs = own[2 * span + a * EXTRA : 2 * span + a * EXTRA + 1, 0:rows].astype(F32)
            docs_s[a] = jnp.min(docs)
        dq[...] = jnp.zeros_like(dq)
        dkv[...] = jnp.zeros_like(dkv)
        for b in range(parts):
            cut = slice(b * rows, (b + 1) * rows)
            key_t[:, cut] = key_ref[cut, :].T
            docs = key_ref[2 * span + b * EXTRA : 2 * span + b * EXTRA + 1, 0:rows].astype(F32)
            docs_t[cut, :] = jnp.broadcast_to(docs, (rows, rows)).T
            if (b + 1) % (parts // 2) == 0:
                docs_s[parts + b // (parts // 2)] = jnp.max(docs)
        half = span // 2
        for s in range(parts):
            a = me ^ s
            near = offset * span + a * rows
            low = (near - half + 1 < reach) & (docs_s[a] <= docs_s[parts])
            high = (near - span + 1 < reach) & (docs_s[a] <= docs_s[parts + 1])
            if offset == 0:
                high = high & (a * rows + rows > half)

            def block(start, stop, s=s, a=a, near=near):
                docs = own[pl.ds(pl.multiple_of(2 * span + a * EXTRA, EXTRA), EXTRA), :]
                docs = docs.astype(F32)[0:1, 0:rows]
                query = queries[s][0:width, :]
                grad = queries[s][width : 2 * width, :]
                stats = queries[s][2 * width :, :].astype(F32)
                stats = stats[0:EXTRA] + stats[EXTRA : 2 * EXTRA] + stats[2 * EXTRA :]
                gap = (
                    near
                    - start
                    + lax.broadcasted_iota(jnp.int32, (stop - start, rows), 1)
                    - lax.broadcasted_iota(jnp.int32, (stop - start, rows), 0)
                )
                mask = docs_t[start:stop, :] == docs
                if offset == 0:
                    mask = mask & (gap >= 0)
                if (offset + 1) * span > WINDOW:
                    mask = mask & (gap < WINDOW)
                scores = dot(key_ref[start:stop, :], query, ((1,), (1,)))
                dprob = dot(key_ref[span + start : span + stop, :], grad, ((1,), (1,)))
                probs, dscores = [], []
                for h in range(GROUP):
                    cut = slice(h * rows, (h + 1) * rows)
                    norm = stats[h : h + 1, :] * LOG2E
                    delta = stats[GROUP + h : GROUP + h + 1, :]
                    prob = jnp.exp2(scores[:, cut] * (SCALE * LOG2E) - norm)
                    prob = jnp.where(mask, prob, 0.0)
                    probs.append(prob.astype(BF16))
                    dscores.append((prob * (dprob[:, cut] - delta) * SCALE).astype(BF16))
                prob = jnp.concatenate(probs, 1)
                dscore = jnp.concatenate(dscores, 1)
                dkv[start:stop, :] += dot(dscore, query, ((1,), (0,)))
                dkv[span + start : span + stop, :] += dot(prob, grad, ((1,), (0,)))
                dq[s] += dot(key_t[:, start:stop], dscore, ((1,), (0,)))

            pl.when(low & high)(functools.partial(block, 0, span))
            pl.when(high & ~low)(functools.partial(block, half, span))
            if offset == 0:
                pl.when(low & ~high)(functools.partial(block, 0, half))

        kv_out[...] = dkv[...].astype(kv_out.dtype)
        for s in range(parts):
            total = dq[s] if first else dq[s] + dq_in[s]
            if last:
                dq_out[s][...] = total.astype(BF16)
            else:
                dq_out[s] = total

    if first:
        work()
        return

    @pl.when(row < offset)
    def _():
        kv_out[...] = jnp.zeros_like(kv_out)
        for s in range(parts):
            if last:
                dq_out[s][...] = dq_in[s].astype(BF16)
            else:
                dq_out[s] = dq_in[s]

    pl.when(row >= offset)(work)


def add_terms(place, arrived, term, out):
    out[...] = (arrived[...].astype(F32) + term[...]).astype(BF16)


def cut_terms(rows, count, place, *refs):
    parts = KEY_VALUE_HEADS
    terms, outs = refs[:count], refs[-parts:]
    for s, out in enumerate(outs):
        for k in range(2):
            at = pl.multiple_of((k * parts + (place[1] ^ s)) * rows, rows)
            total = sum(term[pl.ds(at, rows), :].astype(F32) for term in terms)
            out[k * rows : (k + 1) * rows, :] = total.astype(BF16)


def spread_queries(rows, place, *refs):
    pieces, (out, token, turned, sems) = refs[:-4], refs[-4:]
    width = GROUP * HEAD_SIZE
    copies = []
    for s, piece in enumerate(pieces):
        for h in range(GROUP):
            cut = slice(h * HEAD_SIZE, (h + 1) * HEAD_SIZE)
            turned[s, :, cut] = piece[:, h * rows : (h + 1) * rows].T
        cut = pl.ds(pl.multiple_of((place[1] ^ s) * width, width), width)
        copies.append(pltpu.make_async_copy(turned.at[s], out.at[:, cut], sems.at[s]))
        copies[-1].start()
    token[...] = jnp.zeros_like(token)
    for copy in copies:
        copy.wait()


def spread_keys(rows, sources, place, *refs):
    parts = KEY_VALUE_HEADS
    pieces, (key_out, value_out, total, sems) = refs[:-5], refs[-4:]
    copies = []
    for s in range(parts):
        term = pieces[s][...].astype(F32)
        for k in range(1, sources):
            term = term + pieces[k * parts + s][...].astype(F32)
        total[s] = term.astype(BF16)
        for k, out in enumerate((key_out, value_out)):
            source = total.at[s, k * rows : (k + 1) * rows, :]
            target = out.at[:, head_columns(place[1] ^ s)]
            copies.append(pltpu.make_async_copy(source, target, sems.at[s, k]))
            copies[-1].start()
    for copy in copies:
        copy.wait()


def local(
    queries, key_matrix, value_matrix, attention_output, output_gradient, log_sum_norm, doc_ids
):
    parts = KEY_VALUE_HEADS
    rows = queries.shape[0]
    count = lax.axis_size("tok")
    span = parts * rows
    reach = min(WINDOW, count * rows // 2)
    behind = min(-(-(reach - 1) // span), count // parts - 1)
    device = lax.axis_index("tok")
    place = jnp.stack([device // parts, device % parts]).astype(jnp.int32)
    width = GROUP * rows
    shape = jax.ShapeDtypeStruct

    def move(value, steps, s=0, low=0):
        def target(t):
            row, me = divmod(t, parts)
            if row < low:
                return t ^ 1
            if low <= row + steps < count // parts:
                return ((row + steps) * parts + me) ^ s
            row = low + (row - low + steps) % (count // parts - low)
            return row * parts + me

        return lax.ppermute(value, "tok", [(t, target(t)) for t in range(count)])

    def exchange(pieces):
        return [pieces[0]] + [move(pieces[s], 0, s) for s in range(1, parts)]

    *pieces, grads, outputs = call(
        functools.partial(pack_keys, rows),
        (place, key_matrix, value_matrix, doc_ids.reshape(1, rows), output_gradient, attention_output),
        [shape((2 * rows + EXTRA, HEAD_SIZE), BF16)] * parts + [shape(queries.shape, BF16)] * 2,
        scratch=[
            pltpu.VMEM((1, rows), jnp.int32),
            pltpu.SemaphoreType.DMA(()),
            pltpu.SemaphoreType.DMA((parts, 2)),
            pltpu.SemaphoreType.DMA((2,)),
        ],
        specs=[HBM] * 5,
    )
    pieces = exchange(pieces)
    *query_pieces, token = call(
        functools.partial(pack_queries, rows),
        (place, queries, grads, outputs, log_sum_norm),
        [shape((2 * width + 3 * EXTRA, HEAD_SIZE), BF16)] * parts + [TOKEN],
        scratch=[
            pltpu.VMEM((parts, 2 * GROUP, rows), F32),
            pltpu.SemaphoreType.DMA((parts, GROUP)),
        ],
        specs=[HBM, VMEM, VMEM, VMEM],
    )
    (own,) = call(
        functools.partial(join, rows),
        (place, *pieces, token),
        [shape((parts * (2 * rows + EXTRA), HEAD_SIZE), BF16)],
    )
    query_pieces = exchange(query_pieces)
    windows = [own]
    for k in range(behind):
        windows.append(move(windows[-1], 1, low=k))

    kv_shape = (2 * span, HEAD_SIZE)
    stages = [0] + list(range(behind, 0, -1))
    dq, own_pieces, sent = None, None, None
    for k, offset in enumerate(stages):
        first, last = k == 0, k == len(stages) - 1
        ins = [place, *query_pieces, own, windows[offset]]
        if not first:
            ins.append(dq)
        if last:
            outs = [shape((HEAD_SIZE, width), BF16)] * parts
        else:
            outs = [shape((parts, HEAD_SIZE, width), F32)]
        outs = outs + [shape(kv_shape, BF16 if offset == behind > 0 else F32)]
        got = call(
            functools.partial(attend, rows, offset, reach, first, last),
            ins,
            outs,
            scratch=attend_scratch(rows),
            flops=10 * span * span * GROUP * HEAD_SIZE,
        )
        dq, term = (got[:parts] if last else got[0]), got[-1]
        piece_shapes = [shape((2 * rows, HEAD_SIZE), BF16)] * parts
        if offset == 0:
            own_pieces = call(functools.partial(cut_terms, rows, 1), (place, term), piece_shapes)
            own_pieces = exchange(own_pieces)
        elif offset == 1:
            terms = (term,) if sent is None else (sent, term)
            got = call(
                functools.partial(cut_terms, rows, len(terms)), (place, *terms), piece_shapes
            )
            sent = [move(piece, -1, s) for s, piece in enumerate(got)]
        elif sent is None:
            sent = move(term, -1, low=offset - 1)
        else:
            (term,) = call(add_terms, (place, sent, term), [shape(kv_shape, BF16)])
            sent = move(term, -1, low=offset - 1)

    dq_pieces = exchange(dq)
    query_grad, token = call(
        functools.partial(spread_queries, rows),
        (place, *dq_pieces),
        [shape((rows, parts * GROUP * HEAD_SIZE), BF16), TOKEN],
        scratch=[
            pltpu.VMEM((parts, rows, GROUP * HEAD_SIZE), BF16),
            pltpu.SemaphoreType.DMA((parts,)),
        ],
        out_specs=[HBM, VMEM],
    )
    pieces = own_pieces + (sent or [])
    key_grad, value_grad = call(
        functools.partial(spread_keys, rows, len(pieces) // parts),
        (place, *pieces, token),
        [shape((rows, parts * HEAD_SIZE), BF16)] * 2,
        scratch=[
            pltpu.VMEM((parts, 2 * rows, HEAD_SIZE), BF16),
            pltpu.SemaphoreType.DMA((parts, 2)),
        ],
        out_specs=[HBM, HBM],
    )
    return query_grad, key_grad, value_grad


def solution(mesh):
    axes = ("groups", "tok")
    return jax.shard_map(
        local,
        mesh=mesh,
        in_specs=(
            P(axes, None),
            P(axes, None),
            P(axes, None),
            P(axes, None),
            P(axes, None),
            P(None, axes),
            P(axes),
        ),
        out_specs=(P(axes, None), P(axes, None), P(axes, None)),
        check_vma=False,
    )
```

```python
import functools
import math

import jax
import jax.numpy as jnp
from jax import lax
from jax.experimental import pallas as pl
from jax.experimental.pallas import tpu as pltpu
from jax.sharding import PartitionSpec as P

WINDOW = 4096
QUERY_HEADS = 16
KEY_VALUE_HEADS = 4
HEAD_SIZE = 128
GROUP = QUERY_HEADS // KEY_VALUE_HEADS
SCALE = HEAD_SIZE ** (-0.5)
LOG2E = math.log2(math.e)
EXTRA = 8
F32 = jnp.float32
BF16 = jnp.bfloat16

VMEM = pl.BlockSpec(memory_space=pltpu.VMEM)
SMEM = pl.BlockSpec(memory_space=pltpu.SMEM)


def dot(a, b, dims):
    return lax.dot_general(a, b, (dims, ((), ())), preferred_element_type=F32)


HBM = pl.BlockSpec(memory_space=pltpu.MemorySpace.HBM)
TOKEN = jax.ShapeDtypeStruct((8, 128), F32)


def call(kernel, ins, outs, scratch=(), flops=0, specs=None, out_specs=None):
    specs = specs or [VMEM] * (len(ins) - 1)
    ins = [ins[0]] + [
        pltpu.with_memory_space_constraint(x, pltpu.MemorySpace.HBM) if spec is HBM else x
        for x, spec in zip(ins[1:], specs)
    ]
    size = sum(math.prod(o.shape) * o.dtype.itemsize for o in outs)
    size += sum(math.prod(x.shape) * x.dtype.itemsize for x in ins)
    return pl.pallas_call(
        kernel,
        out_shape=outs,
        in_specs=[SMEM] + specs,
        out_specs=out_specs or [VMEM] * len(outs),
        scratch_shapes=list(scratch),
        cost_estimate=pl.CostEstimate(flops=flops, bytes_accessed=size, transcendentals=0),
        compiler_params=pltpu.CompilerParams(vmem_limit_bytes=48 << 20),
    )(*ins)


def head_columns(g):
    return pl.ds(pl.multiple_of(g * HEAD_SIZE, HEAD_SIZE), HEAD_SIZE)


def pack_keys(rows, place, key_ref, value_ref, doc_ref, grad_ref, output_ref, *rest):
    outs, (grads, outputs, ids, doc_sem, sems, more_sems) = rest[:-6], rest[-6:]
    first = pltpu.make_async_copy(doc_ref, ids, doc_sem)
    first.start()
    copies = []
    for s, out in enumerate(outs):
        cut = head_columns(place[1] ^ s)
        for k, source in enumerate((key_ref, value_ref)):
            target = out.at[k * rows : (k + 1) * rows, :]
            copies.append(pltpu.make_async_copy(source.at[:, cut], target, sems.at[s, k]))
    copies.append(pltpu.make_async_copy(grad_ref, grads, more_sems.at[0]))
    copies.append(pltpu.make_async_copy(output_ref, outputs, more_sems.at[1]))
    for copy in copies:
        copy.start()
    first.wait()
    docs = jnp.broadcast_to((ids[...] + 1).astype(F32), (EXTRA, rows)).astype(BF16)
    for out in outs:
        out[2 * rows :, 0:rows] = docs
    for copy in copies:
        copy.wait()


def pack_queries(rows, place, query_ref, grads, outputs, norm_ref, *rest):
    outs, (token, stats, sems) = rest[:-3], rest[-3:]
    copies = []
    for s, out in enumerate(outs):
        for h in range(GROUP):
            cut = head_columns((place[1] ^ s) * GROUP + h)
            target = out.at[h * rows : (h + 1) * rows, :]
            copies.append(pltpu.make_async_copy(query_ref.at[:, cut], target, sems.at[s, h]))
    for copy in copies:
        copy.start()
    for s, out in enumerate(outs):
        for h in range(GROUP):
            at = (GROUP + h) * rows
            out[at : at + rows, :] = grads[:, head_columns((place[1] ^ s) * GROUP + h)]
    lane = lax.broadcasted_iota(jnp.int32, (rows, HEAD_SIZE), 1)
    columns = jnp.zeros((rows, HEAD_SIZE), F32)
    for h in range(QUERY_HEADS):
        cut = slice(h * HEAD_SIZE, (h + 1) * HEAD_SIZE)
        product = grads[:, cut].astype(F32) * outputs[:, cut].astype(F32)
        columns = jnp.where(lane == h, jnp.sum(product, 1, keepdims=True), columns)
    delta = columns.T
    for g in range(KEY_VALUE_HEADS):
        stats[g, 0:GROUP, :] = norm_ref[g * GROUP : (g + 1) * GROUP, :]
        stats[g, GROUP : 2 * GROUP, :] = delta[g * GROUP : (g + 1) * GROUP, :]
    for s, out in enumerate(outs):
        left = stats[place[1] ^ s]
        for part in range(3):
            term = left.astype(BF16)
            at = 2 * GROUP * rows + part * EXTRA
            out[at : at + EXTRA, 0:rows] = term
            left = left - term.astype(F32)
    for copy in copies:
        copy.wait()
    token[...] = jnp.zeros_like(token)


def join(rows, place, *refs):
    parts = KEY_VALUE_HEADS
    pieces, out = refs[:parts], refs[-1]
    span = parts * rows
    for s, piece in enumerate(pieces):
        a = place[1] ^ s
        for k in range(2):
            at = pl.multiple_of(k * span + a * rows, rows)
            out[pl.ds(at, rows), :] = piece[k * rows : (k + 1) * rows, :]
        at = pl.multiple_of(2 * span + a * EXTRA, EXTRA)
        out[pl.ds(at, EXTRA), :] = piece[2 * rows :, :]


def attend_scratch(rows):
    parts = KEY_VALUE_HEADS
    return [
        pltpu.VMEM((parts, HEAD_SIZE, GROUP * rows), F32),
        pltpu.VMEM((2 * parts * rows, HEAD_SIZE), F32),
        pltpu.VMEM((HEAD_SIZE, parts * rows), BF16),
        pltpu.VMEM((parts * rows, rows), F32),
        pltpu.SMEM((2 * parts,), F32),
    ]


def attend(rows, offset, reach, first, last, place, *refs):
    parts = KEY_VALUE_HEADS
    queries, refs = refs[:parts], refs[parts:]
    own, key_ref, refs = refs[0], refs[1], refs[2:]
    if not first:
        dq_in, refs = refs[0], refs[1:]
    if last:
        dq_out, refs = refs[:parts], refs[parts:]
    else:
        dq_out, refs = refs[0], refs[1:]
    kv_out, dq, dkv, key_t, docs_t, docs_s = refs
    row, me = place[0], place[1]
    width = GROUP * rows
    span = parts * rows

    def work():
        for a in range(parts):
            docs = own[2 * span + a * EXTRA : 2 * span + a * EXTRA + 1, 0:rows].astype(F32)
            docs_s[a] = jnp.min(docs)
        dq[...] = jnp.zeros_like(dq)
        dkv[...] = jnp.zeros_like(dkv)
        for b in range(parts):
            cut = slice(b * rows, (b + 1) * rows)
            key_t[:, cut] = key_ref[cut, :].T
            docs = key_ref[2 * span + b * EXTRA : 2 * span + b * EXTRA + 1, 0:rows].astype(F32)
            docs_t[cut, :] = jnp.broadcast_to(docs, (rows, rows)).T
            if (b + 1) % (parts // 2) == 0:
                docs_s[parts + b // (parts // 2)] = jnp.max(docs)
        half = span // 2
        for s in range(parts):
            a = me ^ s
            near = offset * span + a * rows
            low = (near - half + 1 < reach) & (docs_s[a] <= docs_s[parts])
            high = (near - span + 1 < reach) & (docs_s[a] <= docs_s[parts + 1])
            if offset == 0:
                high = high & (a * rows + rows > half)

            def block(start, stop, s=s, a=a, near=near):
                docs = own[pl.ds(pl.multiple_of(2 * span + a * EXTRA, EXTRA), EXTRA), :]
                docs = docs.astype(F32)[0:1, 0:rows]
                query = queries[s][0:width, :]
                grad = queries[s][width : 2 * width, :]
                stats = queries[s][2 * width :, :].astype(F32)
                stats = stats[0:EXTRA] + stats[EXTRA : 2 * EXTRA] + stats[2 * EXTRA :]
                gap = (
                    near
                    - start
                    + lax.broadcasted_iota(jnp.int32, (stop - start, rows), 1)
                    - lax.broadcasted_iota(jnp.int32, (stop - start, rows), 0)
                )
                mask = docs_t[start:stop, :] == docs
                if offset == 0:
                    mask = mask & (gap >= 0)
                if (offset + 1) * span > WINDOW:
                    mask = mask & (gap < WINDOW)
                scores = dot(key_ref[start:stop, :], query, ((1,), (1,)))
                dprob = dot(key_ref[span + start : span + stop, :], grad, ((1,), (1,)))
                probs, dscores = [], []
                for h in range(GROUP):
                    cut = slice(h * rows, (h + 1) * rows)
                    norm = stats[h : h + 1, :] * LOG2E
                    delta = stats[GROUP + h : GROUP + h + 1, :]
                    prob = jnp.exp2(scores[:, cut] * (SCALE * LOG2E) - norm)
                    prob = jnp.where(mask, prob, 0.0)
                    probs.append(prob.astype(BF16))
                    dscores.append((prob * (dprob[:, cut] - delta) * SCALE).astype(BF16))
                prob = jnp.concatenate(probs, 1)
                dscore = jnp.concatenate(dscores, 1)
                dkv[start:stop, :] += dot(dscore, query, ((1,), (0,)))
                dkv[span + start : span + stop, :] += dot(prob, grad, ((1,), (0,)))
                dq[s] += dot(key_t[:, start:stop], dscore, ((1,), (0,)))

            pl.when(low & high)(functools.partial(block, 0, span))
            pl.when(high & ~low)(functools.partial(block, half, span))
            if offset == 0:
                pl.when(low & ~high)(functools.partial(block, 0, half))

        kv_out[...] = dkv[...].astype(kv_out.dtype)
        for s in range(parts):
            total = dq[s] if first else dq[s] + dq_in[s]
            if last:
                dq_out[s][...] = total.astype(BF16)
            else:
                dq_out[s] = total

    if first:
        work()
        return

    @pl.when(row < offset)
    def _():
        kv_out[...] = jnp.zeros_like(kv_out)
        for s in range(parts):
            if last:
                dq_out[s][...] = dq_in[s].astype(BF16)
            else:
                dq_out[s] = dq_in[s]

    pl.when(row >= offset)(work)


def add_terms(place, arrived, term, out):
    out[...] = (arrived[...].astype(F32) + term[...]).astype(BF16)


def cut_terms(rows, count, groups, place, *refs):
    parts = KEY_VALUE_HEADS
    terms, outs = refs[:count], refs[-len(groups) :]
    for group, out in zip(groups, outs):
        for n, s in enumerate(group):
            for k in range(2):
                at = pl.multiple_of((k * parts + (place[1] ^ s)) * rows, rows)
                total = sum(term[pl.ds(at, rows), :].astype(F32) for term in terms)
                start = (2 * n + k) * rows
                out[start : start + rows, :] = total.astype(BF16)


def spread_queries(rows, place, *refs):
    pieces, (out, token, turned, sems) = refs[:-4], refs[-4:]
    width = GROUP * HEAD_SIZE
    copies = []
    for s, piece in enumerate(pieces):
        for h in range(GROUP):
            cut = slice(h * HEAD_SIZE, (h + 1) * HEAD_SIZE)
            turned[s, :, cut] = piece[:, h * rows : (h + 1) * rows].T
        cut = pl.ds(pl.multiple_of((place[1] ^ s) * width, width), width)
        copies.append(pltpu.make_async_copy(turned.at[s], out.at[:, cut], sems.at[s]))
        copies[-1].start()
    token[...] = jnp.zeros_like(token)
    for copy in copies:
        copy.wait()


def spread_keys(rows, sources, place, *refs):
    parts = KEY_VALUE_HEADS
    pieces, (key_out, value_out, total, sems) = refs[:-5], refs[-4:]
    copies = []
    for s in range(parts):
        term = pieces[s][...].astype(F32)
        for k in range(1, sources):
            term = term + pieces[k * parts + s][0 : 2 * rows, :].astype(F32)
        total[s] = term.astype(BF16)
        for k, out in enumerate((key_out, value_out)):
            source = total.at[s, k * rows : (k + 1) * rows, :]
            target = out.at[:, head_columns(place[1] ^ s)]
            copies.append(pltpu.make_async_copy(source, target, sems.at[s, k]))
            copies[-1].start()
    for copy in copies:
        copy.wait()


def local(
    queries, key_matrix, value_matrix, attention_output, output_gradient, log_sum_norm, doc_ids
):
    parts = KEY_VALUE_HEADS
    rows = queries.shape[0]
    count = lax.axis_size("tok")
    span = parts * rows
    reach = min(WINDOW, count * rows // 2)
    behind = min(-(-(reach - 1) // span), count // parts - 1)
    device = lax.axis_index("tok")
    place = jnp.stack([device // parts, device % parts]).astype(jnp.int32)
    width = GROUP * rows
    shape = jax.ShapeDtypeStruct

    def move(value, steps, s=0, low=0):
        def target(t):
            row, me = divmod(t, parts)
            if row < low:
                return t ^ 1
            if low <= row + steps < count // parts:
                return ((row + steps) * parts + me) ^ s
            row = low + (row - low + steps) % (count // parts - low)
            return row * parts + me

        return lax.ppermute(value, "tok", [(t, target(t)) for t in range(count)])

    def exchange(pieces):
        return [pieces[0]] + [move(pieces[s], 0, s) for s in range(1, parts)]

    *pieces, grads, outputs = call(
        functools.partial(pack_keys, rows),
        (place, key_matrix, value_matrix, doc_ids.reshape(1, rows), output_gradient, attention_output),
        [shape((2 * rows + EXTRA, HEAD_SIZE), BF16)] * parts + [shape(queries.shape, BF16)] * 2,
        scratch=[
            pltpu.VMEM((1, rows), jnp.int32),
            pltpu.SemaphoreType.DMA(()),
            pltpu.SemaphoreType.DMA((parts, 2)),
            pltpu.SemaphoreType.DMA((2,)),
        ],
        specs=[HBM] * 5,
    )
    pieces = exchange(pieces)
    *query_pieces, token = call(
        functools.partial(pack_queries, rows),
        (place, queries, grads, outputs, log_sum_norm),
        [shape((2 * width + 3 * EXTRA, HEAD_SIZE), BF16)] * parts + [TOKEN],
        scratch=[
            pltpu.VMEM((parts, 2 * GROUP, rows), F32),
            pltpu.SemaphoreType.DMA((parts, GROUP)),
        ],
        specs=[HBM, VMEM, VMEM, VMEM],
    )
    (own,) = call(
        functools.partial(join, rows),
        (place, *pieces, token),
        [shape((parts * (2 * rows + EXTRA), HEAD_SIZE), BF16)],
    )
    query_pieces = exchange(query_pieces)
    windows = [own]
    for k in range(behind):
        windows.append(move(windows[-1], 1, low=k))

    kv_shape = (2 * span, HEAD_SIZE)
    stages = [0] + list(range(behind, 0, -1))
    dq, own_pieces, sent = None, None, None
    for k, offset in enumerate(stages):
        first, last = k == 0, k == len(stages) - 1
        ins = [place, *query_pieces, own, windows[offset]]
        if not first:
            ins.append(dq)
        if last:
            outs = [shape((HEAD_SIZE, width), BF16)] * parts
        else:
            outs = [shape((parts, HEAD_SIZE, width), F32)]
        outs = outs + [shape(kv_shape, BF16 if offset == behind > 0 else F32)]
        got = call(
            functools.partial(attend, rows, offset, reach, first, last),
            ins,
            outs,
            scratch=attend_scratch(rows),
            flops=10 * span * span * GROUP * HEAD_SIZE,
        )
        dq, term = (got[:parts] if last else got[0]), got[-1]
        piece_shapes = [shape((2 * rows, HEAD_SIZE), BF16)] * parts
        if offset == 0:
            own_pieces = call(
                functools.partial(cut_terms, rows, 1, [[s] for s in range(parts)]),
                (place, term),
                piece_shapes,
            )
            own_pieces = exchange(own_pieces)
        elif offset == 1:
            terms = (term,) if sent is None else (sent, term)
            groups = ((2, 3), (0,), (1,))
            got = call(
                functools.partial(cut_terms, rows, len(terms), groups),
                (place, *terms),
                [shape((2 * rows * len(group), HEAD_SIZE), BF16) for group in groups],
            )
            far, straight, beside = [move(piece, -1, group[0]) for piece, group in zip(got, groups)]
            sent = [straight, beside, far, move(far[2 * rows :], 0, 1)]
        elif sent is None:
            sent = move(term, -1, low=offset - 1)
        else:
            (term,) = call(add_terms, (place, sent, term), [shape(kv_shape, BF16)])
            sent = move(term, -1, low=offset - 1)

    dq_pieces = exchange(dq)
    query_grad, token = call(
        functools.partial(spread_queries, rows),
        (place, *dq_pieces),
        [shape((rows, parts * GROUP * HEAD_SIZE), BF16), TOKEN],
        scratch=[
            pltpu.VMEM((parts, rows, GROUP * HEAD_SIZE), BF16),
            pltpu.SemaphoreType.DMA((parts,)),
        ],
        out_specs=[HBM, VMEM],
    )
    pieces = own_pieces + (sent or [])
    key_grad, value_grad = call(
        functools.partial(spread_keys, rows, len(pieces) // parts),
        (place, *pieces, token),
        [shape((rows, parts * HEAD_SIZE), BF16)] * 2,
        scratch=[
            pltpu.VMEM((parts, 2 * rows, HEAD_SIZE), BF16),
            pltpu.SemaphoreType.DMA((parts, 2)),
        ],
        out_specs=[HBM, HBM],
    )
    return query_grad, key_grad, value_grad


def solution(mesh):
    axes = ("groups", "tok")
    return jax.shard_map(
        local,
        mesh=mesh,
        in_specs=(
            P(axes, None),
            P(axes, None),
            P(axes, None),
            P(axes, None),
            P(axes, None),
            P(None, axes),
            P(axes),
        ),
        out_specs=(P(axes, None), P(axes, None), P(axes, None)),
        check_vma=False,
    )
```

```python
import functools
import math

import jax
import jax.numpy as jnp
from jax import lax
from jax.experimental import pallas as pl
from jax.experimental.pallas import tpu as pltpu
from jax.sharding import PartitionSpec as P

WINDOW = 4096
QUERY_HEADS = 16
KEY_VALUE_HEADS = 4
HEAD_SIZE = 128
GROUP = QUERY_HEADS // KEY_VALUE_HEADS
SCALE = HEAD_SIZE ** (-0.5)
LOG2E = math.log2(math.e)
EXTRA = 8
F32 = jnp.float32
BF16 = jnp.bfloat16

VMEM = pl.BlockSpec(memory_space=pltpu.VMEM)
SMEM = pl.BlockSpec(memory_space=pltpu.SMEM)


def dot(a, b, dims):
    return lax.dot_general(a, b, (dims, ((), ())), preferred_element_type=F32)


HBM = pl.BlockSpec(memory_space=pltpu.MemorySpace.HBM)
TOKEN = jax.ShapeDtypeStruct((8, 128), F32)


def call(kernel, ins, outs, scratch=(), flops=0, specs=None, out_specs=None):
    specs = specs or [VMEM] * (len(ins) - 1)
    ins = [ins[0]] + [
        pltpu.with_memory_space_constraint(x, pltpu.MemorySpace.HBM) if spec is HBM else x
        for x, spec in zip(ins[1:], specs)
    ]
    size = sum(math.prod(o.shape) * o.dtype.itemsize for o in outs)
    size += sum(math.prod(x.shape) * x.dtype.itemsize for x in ins)
    return pl.pallas_call(
        kernel,
        out_shape=outs,
        in_specs=[SMEM] + specs,
        out_specs=out_specs or [VMEM] * len(outs),
        scratch_shapes=list(scratch),
        cost_estimate=pl.CostEstimate(flops=flops, bytes_accessed=size, transcendentals=0),
        compiler_params=pltpu.CompilerParams(vmem_limit_bytes=48 << 20),
    )(*ins)


def head_columns(g):
    return pl.ds(pl.multiple_of(g * HEAD_SIZE, HEAD_SIZE), HEAD_SIZE)


def pack_keys(rows, place, key_ref, value_ref, doc_ref, grad_ref, output_ref, *rest):
    outs, (grads, outputs, ids, doc_sem, sems, more_sems) = rest[:-6], rest[-6:]
    first = pltpu.make_async_copy(doc_ref, ids, doc_sem)
    first.start()
    copies = []
    for s, out in enumerate(outs):
        cut = head_columns(place[1] ^ s)
        for k, source in enumerate((key_ref, value_ref)):
            target = out.at[k * rows : (k + 1) * rows, :]
            copies.append(pltpu.make_async_copy(source.at[:, cut], target, sems.at[s, k]))
    copies.append(pltpu.make_async_copy(grad_ref, grads, more_sems.at[0]))
    copies.append(pltpu.make_async_copy(output_ref, outputs, more_sems.at[1]))
    for copy in copies:
        copy.start()
    first.wait()
    docs = jnp.broadcast_to((ids[...] + 1).astype(F32), (EXTRA, rows)).astype(BF16)
    for out in outs:
        out[2 * rows :, 0:rows] = docs
    for copy in copies:
        copy.wait()


def pack_queries(rows, place, query_ref, grads, outputs, norm_ref, *rest):
    outs, (token, stats, sems) = rest[:-3], rest[-3:]
    copies = []
    for s, out in enumerate(outs):
        for h in range(GROUP):
            cut = head_columns((place[1] ^ s) * GROUP + h)
            target = out.at[h * rows : (h + 1) * rows, :]
            copies.append(pltpu.make_async_copy(query_ref.at[:, cut], target, sems.at[s, h]))
    for copy in copies:
        copy.start()
    for s, out in enumerate(outs):
        for h in range(GROUP):
            at = (GROUP + h) * rows
            out[at : at + rows, :] = grads[:, head_columns((place[1] ^ s) * GROUP + h)]
    lane = lax.broadcasted_iota(jnp.int32, (rows, HEAD_SIZE), 1)
    columns = jnp.zeros((rows, HEAD_SIZE), F32)
    for h in range(QUERY_HEADS):
        cut = slice(h * HEAD_SIZE, (h + 1) * HEAD_SIZE)
        product = grads[:, cut].astype(F32) * outputs[:, cut].astype(F32)
        columns = jnp.where(lane == h, jnp.sum(product, 1, keepdims=True), columns)
    delta = columns.T
    for g in range(KEY_VALUE_HEADS):
        stats[g, 0:GROUP, :] = norm_ref[g * GROUP : (g + 1) * GROUP, :]
        stats[g, GROUP : 2 * GROUP, :] = delta[g * GROUP : (g + 1) * GROUP, :]
    for s, out in enumerate(outs):
        left = stats[place[1] ^ s]
        for part in range(3):
            term = left.astype(BF16)
            at = 2 * GROUP * rows + part * EXTRA
            out[at : at + EXTRA, 0:rows] = term
            left = left - term.astype(F32)
    for copy in copies:
        copy.wait()
    token[...] = jnp.zeros_like(token)


def join(rows, place, *refs):
    parts = KEY_VALUE_HEADS
    pieces, out = refs[:parts], refs[-1]
    span = parts * rows
    for s, piece in enumerate(pieces):
        a = place[1] ^ s
        for k in range(2):
            at = pl.multiple_of(k * span + a * rows, rows)
            out[pl.ds(at, rows), :] = piece[k * rows : (k + 1) * rows, :]
        at = pl.multiple_of(2 * span + a * EXTRA, EXTRA)
        out[pl.ds(at, EXTRA), :] = piece[2 * rows :, :]


def attend_scratch(rows):
    parts = KEY_VALUE_HEADS
    return [
        pltpu.VMEM((parts, HEAD_SIZE, GROUP * rows), F32),
        pltpu.VMEM((2 * parts * rows, HEAD_SIZE), F32),
        pltpu.VMEM((HEAD_SIZE, parts * rows), BF16),
        pltpu.VMEM((parts * rows, rows), F32),
        pltpu.SMEM((2 * parts,), F32),
    ]


def attend(rows, offset, reach, first, last, place, *refs):
    parts = KEY_VALUE_HEADS
    queries, refs = refs[:parts], refs[parts:]
    own, key_ref, refs = refs[0], refs[1], refs[2:]
    if not first:
        dq_in, refs = refs[0], refs[1:]
    if last:
        dq_out, refs = refs[:parts], refs[parts:]
    else:
        dq_out, refs = refs[0], refs[1:]
    (*kv_out, dq, dkv, key_t, docs_t, docs_s) = refs
    row, me = place[0], place[1]
    width = GROUP * rows
    span = parts * rows

    def work():
        for a in range(parts):
            docs = own[2 * span + a * EXTRA : 2 * span + a * EXTRA + 1, 0:rows].astype(F32)
            docs_s[a] = jnp.min(docs)
        dq[...] = jnp.zeros_like(dq)
        dkv[...] = jnp.zeros_like(dkv)
        for b in range(parts):
            cut = slice(b * rows, (b + 1) * rows)
            key_t[:, cut] = key_ref[cut, :].T
            docs = key_ref[2 * span + b * EXTRA : 2 * span + b * EXTRA + 1, 0:rows].astype(F32)
            docs_t[cut, :] = jnp.broadcast_to(docs, (rows, rows)).T
            if (b + 1) % (parts // 2) == 0:
                docs_s[parts + b // (parts // 2)] = jnp.max(docs)
        half = span // 2
        for s in range(parts):
            a = me ^ s
            near = offset * span + a * rows
            low = (near - half + 1 < reach) & (docs_s[a] <= docs_s[parts])
            high = (near - span + 1 < reach) & (docs_s[a] <= docs_s[parts + 1])
            if offset == 0:
                high = high & (a * rows + rows > half)

            def block(start, stop, s=s, a=a, near=near):
                docs = own[pl.ds(pl.multiple_of(2 * span + a * EXTRA, EXTRA), EXTRA), :]
                docs = docs.astype(F32)[0:1, 0:rows]
                query = queries[s][0:width, :]
                grad = queries[s][width : 2 * width, :]
                stats = queries[s][2 * width :, :].astype(F32)
                stats = stats[0:EXTRA] + stats[EXTRA : 2 * EXTRA] + stats[2 * EXTRA :]
                gap = (
                    near
                    - start
                    + lax.broadcasted_iota(jnp.int32, (stop - start, rows), 1)
                    - lax.broadcasted_iota(jnp.int32, (stop - start, rows), 0)
                )
                mask = docs_t[start:stop, :] == docs
                if offset == 0:
                    mask = mask & (gap >= 0)
                if (offset + 1) * span > WINDOW:
                    mask = mask & (gap < WINDOW)
                scores = dot(key_ref[start:stop, :], query, ((1,), (1,)))
                dprob = dot(key_ref[span + start : span + stop, :], grad, ((1,), (1,)))
                probs, dscores = [], []
                for h in range(GROUP):
                    cut = slice(h * rows, (h + 1) * rows)
                    norm = stats[h : h + 1, :] * LOG2E
                    delta = stats[GROUP + h : GROUP + h + 1, :]
                    prob = jnp.exp2(scores[:, cut] * (SCALE * LOG2E) - norm)
                    prob = jnp.where(mask, prob, 0.0)
                    probs.append(prob.astype(BF16))
                    dscores.append((prob * (dprob[:, cut] - delta) * SCALE).astype(BF16))
                prob = jnp.concatenate(probs, 1)
                dscore = jnp.concatenate(dscores, 1)
                dkv[start:stop, :] += dot(dscore, query, ((1,), (0,)))
                dkv[span + start : span + stop, :] += dot(prob, grad, ((1,), (0,)))
                dq[s] += dot(key_t[:, start:stop], dscore, ((1,), (0,)))

            pl.when(low & high)(functools.partial(block, 0, span))
            pl.when(high & ~low)(functools.partial(block, half, span))
            if offset == 0:
                pl.when(low & ~high)(functools.partial(block, 0, half))

        for k, out in enumerate(kv_out):
            out[...] = dkv[k * span : (k + 1) * span, :].astype(out.dtype)
        for s in range(parts):
            total = dq[s] if first else dq[s] + dq_in[s]
            if last:
                dq_out[s][...] = total.astype(BF16)
            else:
                dq_out[s] = total

    if first:
        work()
        return

    @pl.when(row < offset)
    def _():
        for out in kv_out:
            out[...] = jnp.zeros_like(out)
        for s in range(parts):
            if last:
                dq_out[s][...] = dq_in[s].astype(BF16)
            else:
                dq_out[s] = dq_in[s]

    pl.when(row >= offset)(work)


def add_terms(place, arrived, term, out):
    out[...] = (arrived[...].astype(F32) + term[...]).astype(BF16)


def cut_own(rows, place, key_ref, value_ref, *outs):
    for s, out in enumerate(outs):
        at = pl.multiple_of((place[1] ^ s) * rows, rows)
        for k, term in enumerate((key_ref, value_ref)):
            out[k * rows : (k + 1) * rows, :] = term[pl.ds(at, rows), :].astype(BF16)


def cut_terms(rows, count, groups, place, *refs):
    terms, outs = refs[:count], refs[-len(groups) :]
    for group, out in zip(groups, outs):
        for n, s in enumerate(group):
            at = pl.multiple_of((place[1] ^ s) * rows, rows)
            total = sum(term[pl.ds(at, rows), :].astype(F32) for term in terms)
            out[n * rows : (n + 1) * rows, :] = total.astype(BF16)


def spread_queries(rows, place, *refs):
    pieces, (out, token, turned, sems) = refs[:-4], refs[-4:]
    width = GROUP * HEAD_SIZE
    copies = []
    for s, piece in enumerate(pieces):
        for h in range(GROUP):
            cut = slice(h * HEAD_SIZE, (h + 1) * HEAD_SIZE)
            turned[s, :, cut] = piece[:, h * rows : (h + 1) * rows].T
        cut = pl.ds(pl.multiple_of((place[1] ^ s) * width, width), width)
        copies.append(pltpu.make_async_copy(turned.at[s], out.at[:, cut], sems.at[s]))
        copies[-1].start()
    token[...] = jnp.zeros_like(token)
    for copy in copies:
        copy.wait()


def spread_keys(rows, moved, place, *refs):
    parts = KEY_VALUE_HEADS
    pieces, (key_out, value_out, total, sems) = refs[:-5], refs[-4:]
    copies = []
    for s in range(parts):
        for k, out in enumerate((key_out, value_out)):
            cut = slice(k * rows, (k + 1) * rows)
            term = pieces[s][cut, :].astype(F32)
            if moved:
                term = term + pieces[(k + 1) * parts + s][0:rows, :].astype(F32)
            total[s, cut, :] = term.astype(BF16)
            target = out.at[:, head_columns(place[1] ^ s)]
            copies.append(pltpu.make_async_copy(total.at[s, cut, :], target, sems.at[s, k]))
            copies[-1].start()
    for copy in copies:
        copy.wait()


def local(
    queries, key_matrix, value_matrix, attention_output, output_gradient, log_sum_norm, doc_ids
):
    parts = KEY_VALUE_HEADS
    rows = queries.shape[0]
    count = lax.axis_size("tok")
    span = parts * rows
    reach = min(WINDOW, count * rows // 2)
    behind = min(-(-(reach - 1) // span), count // parts - 1)
    device = lax.axis_index("tok")
    place = jnp.stack([device // parts, device % parts]).astype(jnp.int32)
    width = GROUP * rows
    shape = jax.ShapeDtypeStruct

    def move(value, steps, s=0, low=0):
        def target(t):
            row, me = divmod(t, parts)
            if row < low:
                return t ^ 1
            if low <= row + steps < count // parts:
                return ((row + steps) * parts + me) ^ s
            row = low + (row - low + steps) % (count // parts - low)
            return row * parts + me

        return lax.ppermute(value, "tok", [(t, target(t)) for t in range(count)])

    def exchange(pieces):
        return [pieces[0]] + [move(pieces[s], 0, s) for s in range(1, parts)]

    *pieces, grads, outputs = call(
        functools.partial(pack_keys, rows),
        (place, key_matrix, value_matrix, doc_ids.reshape(1, rows), output_gradient, attention_output),
        [shape((2 * rows + EXTRA, HEAD_SIZE), BF16)] * parts + [shape(queries.shape, BF16)] * 2,
        scratch=[
            pltpu.VMEM((1, rows), jnp.int32),
            pltpu.SemaphoreType.DMA(()),
            pltpu.SemaphoreType.DMA((parts, 2)),
            pltpu.SemaphoreType.DMA((2,)),
        ],
        specs=[HBM] * 5,
    )
    pieces = exchange(pieces)
    *query_pieces, token = call(
        functools.partial(pack_queries, rows),
        (place, queries, grads, outputs, log_sum_norm),
        [shape((2 * width + 3 * EXTRA, HEAD_SIZE), BF16)] * parts + [TOKEN],
        scratch=[
            pltpu.VMEM((parts, 2 * GROUP, rows), F32),
            pltpu.SemaphoreType.DMA((parts, GROUP)),
        ],
        specs=[HBM, VMEM, VMEM, VMEM],
    )
    (own,) = call(
        functools.partial(join, rows),
        (place, *pieces, token),
        [shape((parts * (2 * rows + EXTRA), HEAD_SIZE), BF16)],
    )
    query_pieces = exchange(query_pieces)
    windows = [own]
    for k in range(behind):
        windows.append(move(windows[-1], 1, low=k))

    kv_shape = (span, HEAD_SIZE)
    stages = [0] + list(range(behind, 0, -1))
    dq, own_pieces, sent = None, None, None
    for k, offset in enumerate(stages):
        first, last = k == 0, k == len(stages) - 1
        ins = [place, *query_pieces, own, windows[offset]]
        if not first:
            ins.append(dq)
        if last:
            outs = [shape((HEAD_SIZE, width), BF16)] * parts
        else:
            outs = [shape((parts, HEAD_SIZE, width), F32)]
        outs = outs + [shape(kv_shape, BF16 if offset == behind > 0 else F32)] * 2
        got = call(
            functools.partial(attend, rows, offset, reach, first, last),
            ins,
            outs,
            scratch=attend_scratch(rows),
            flops=10 * span * span * GROUP * HEAD_SIZE,
        )
        dq, terms = (got[:parts] if last else got[0]), got[-2:]
        if offset == 0:
            own_pieces = call(
                functools.partial(cut_own, rows),
                (place, *terms),
                [shape((2 * rows, HEAD_SIZE), BF16)] * parts,
            )
            own_pieces = exchange(own_pieces)
            continue
        if sent is not None:
            terms = [(arrived, term) for arrived, term in zip(sent, terms)]
        else:
            terms = [(term,) for term in terms]
        sent = []
        for k, pair in enumerate(terms):
            if offset > 1:
                if len(pair) > 1:
                    pair = call(add_terms, (place, *pair), [shape(kv_shape, BF16)])
                sent.append(move(pair[0], -1, low=offset - 1))
                continue
            groups = ((2, 3), (0,), (1,))
            cut = call(
                functools.partial(cut_terms, rows, len(pair), groups),
                (place, *pair),
                [shape((rows * len(group), HEAD_SIZE), BF16) for group in groups],
            )
            far, straight, beside = [move(piece, -1, group[0]) for piece, group in zip(cut, groups)]
            sent += [straight, beside, far, move(far[rows:], 0, 1)]

    dq_pieces = exchange(dq)
    query_grad, token = call(
        functools.partial(spread_queries, rows),
        (place, *dq_pieces),
        [shape((rows, parts * GROUP * HEAD_SIZE), BF16), TOKEN],
        scratch=[
            pltpu.VMEM((parts, rows, GROUP * HEAD_SIZE), BF16),
            pltpu.SemaphoreType.DMA((parts,)),
        ],
        out_specs=[HBM, VMEM],
    )
    pieces = own_pieces + (sent or [])
    key_grad, value_grad = call(
        functools.partial(spread_keys, rows, sent is not None),
        (place, *pieces, token),
        [shape((rows, parts * HEAD_SIZE), BF16)] * 2,
        scratch=[
            pltpu.VMEM((parts, 2 * rows, HEAD_SIZE), BF16),
            pltpu.SemaphoreType.DMA((parts, 2)),
        ],
        out_specs=[HBM, HBM],
    )
    return query_grad, key_grad, value_grad


def solution(mesh):
    axes = ("groups", "tok")
    return jax.shard_map(
        local,
        mesh=mesh,
        in_specs=(
            P(axes, None),
            P(axes, None),
            P(axes, None),
            P(axes, None),
            P(axes, None),
            P(None, axes),
            P(axes),
        ),
        out_specs=(P(axes, None), P(axes, None), P(axes, None)),
        check_vma=False,
    )
```

```python
import functools
import math

import jax
import jax.numpy as jnp
from jax import lax
from jax.experimental import pallas as pl
from jax.experimental.pallas import tpu as pltpu
from jax.sharding import PartitionSpec as P

WINDOW = 4096
QUERY_HEADS = 16
KEY_VALUE_HEADS = 4
HEAD_SIZE = 128
GROUP = QUERY_HEADS // KEY_VALUE_HEADS
SCALE = HEAD_SIZE ** (-0.5)
LOG2E = math.log2(math.e)
EXTRA = 8
F32 = jnp.float32
BF16 = jnp.bfloat16

VMEM = pl.BlockSpec(memory_space=pltpu.VMEM)
SMEM = pl.BlockSpec(memory_space=pltpu.SMEM)


def dot(a, b, dims):
    return lax.dot_general(a, b, (dims, ((), ())), preferred_element_type=F32)


HBM = pl.BlockSpec(memory_space=pltpu.MemorySpace.HBM)
TOKEN = jax.ShapeDtypeStruct((8, 128), F32)


def call(kernel, ins, outs, scratch=(), flops=0, specs=None, out_specs=None):
    specs = specs or [VMEM] * (len(ins) - 1)
    ins = [ins[0]] + [
        pltpu.with_memory_space_constraint(x, pltpu.MemorySpace.HBM) if spec is HBM else x
        for x, spec in zip(ins[1:], specs)
    ]
    size = sum(math.prod(o.shape) * o.dtype.itemsize for o in outs)
    size += sum(math.prod(x.shape) * x.dtype.itemsize for x in ins)
    return pl.pallas_call(
        kernel,
        out_shape=outs,
        in_specs=[SMEM] + specs,
        out_specs=out_specs or [VMEM] * len(outs),
        scratch_shapes=list(scratch),
        cost_estimate=pl.CostEstimate(flops=flops, bytes_accessed=size, transcendentals=0),
        compiler_params=pltpu.CompilerParams(vmem_limit_bytes=48 << 20),
    )(*ins)


def head_columns(g):
    return pl.ds(pl.multiple_of(g * HEAD_SIZE, HEAD_SIZE), HEAD_SIZE)


def pack_keys(rows, place, key_ref, value_ref, doc_ref, grad_ref, output_ref, *rest):
    outs, (grads, outputs, ids, doc_sem, sems, more_sems) = rest[:-6], rest[-6:]
    first = pltpu.make_async_copy(doc_ref, ids, doc_sem)
    first.start()
    copies = []
    for s, out in enumerate(outs):
        cut = head_columns(place[1] ^ s)
        for k, source in enumerate((key_ref, value_ref)):
            target = out.at[k * rows : (k + 1) * rows, :]
            copies.append(pltpu.make_async_copy(source.at[:, cut], target, sems.at[s, k]))
    copies.append(pltpu.make_async_copy(grad_ref, grads, more_sems.at[0]))
    copies.append(pltpu.make_async_copy(output_ref, outputs, more_sems.at[1]))
    for copy in copies:
        copy.start()
    first.wait()
    docs = jnp.broadcast_to((ids[...] + 1).astype(F32), (EXTRA, rows)).astype(BF16)
    for out in outs:
        out[2 * rows :, 0:rows] = docs
    for copy in copies:
        copy.wait()


def pack_queries(rows, place, query_ref, grads, outputs, norm_ref, *rest):
    outs, (token, stats, sems) = rest[:-3], rest[-3:]
    copies = []
    for s, out in enumerate(outs):
        for h in range(GROUP):
            cut = head_columns((place[1] ^ s) * GROUP + h)
            target = out.at[h * rows : (h + 1) * rows, :]
            copies.append(pltpu.make_async_copy(query_ref.at[:, cut], target, sems.at[s, h]))
    for copy in copies:
        copy.start()
    for s, out in enumerate(outs):
        for h in range(GROUP):
            at = (GROUP + h) * rows
            out[at : at + rows, :] = grads[:, head_columns((place[1] ^ s) * GROUP + h)]
    lane = lax.broadcasted_iota(jnp.int32, (rows, HEAD_SIZE), 1)
    columns = jnp.zeros((rows, HEAD_SIZE), F32)
    for h in range(QUERY_HEADS):
        cut = slice(h * HEAD_SIZE, (h + 1) * HEAD_SIZE)
        product = grads[:, cut].astype(F32) * outputs[:, cut].astype(F32)
        columns = jnp.where(lane == h, jnp.sum(product, 1, keepdims=True), columns)
    delta = columns.T
    for g in range(KEY_VALUE_HEADS):
        stats[g, 0:GROUP, :] = norm_ref[g * GROUP : (g + 1) * GROUP, :]
        stats[g, GROUP : 2 * GROUP, :] = delta[g * GROUP : (g + 1) * GROUP, :]
    for s, out in enumerate(outs):
        left = stats[place[1] ^ s]
        for part in range(3):
            term = left.astype(BF16)
            at = 2 * GROUP * rows + part * EXTRA
            out[at : at + EXTRA, 0:rows] = term
            left = left - term.astype(F32)
    for copy in copies:
        copy.wait()
    token[...] = jnp.zeros_like(token)


def join(rows, place, *refs):
    parts = KEY_VALUE_HEADS
    pieces, out = refs[:parts], refs[-1]
    span = parts * rows
    for s, piece in enumerate(pieces):
        a = place[1] ^ s
        for k in range(2):
            at = pl.multiple_of(k * span + a * rows, rows)
            out[pl.ds(at, rows), :] = piece[k * rows : (k + 1) * rows, :]
        at = pl.multiple_of(2 * span + a * EXTRA, EXTRA)
        out[pl.ds(at, EXTRA), :] = piece[2 * rows :, :]


def attend_scratch(rows):
    parts = KEY_VALUE_HEADS
    return [
        pltpu.VMEM((parts, HEAD_SIZE, GROUP * rows), F32),
        pltpu.VMEM((2 * parts * rows, HEAD_SIZE), F32),
        pltpu.VMEM((HEAD_SIZE, parts * rows), BF16),
        pltpu.VMEM((parts * rows, rows), F32),
        pltpu.SMEM((2 * parts,), F32),
    ]


def attend(rows, offset, reach, first, last, place, *refs):
    parts = KEY_VALUE_HEADS
    queries, refs = refs[:parts], refs[parts:]
    own, key_ref, refs = refs[0], refs[1], refs[2:]
    if not first:
        dq_in, refs = refs[0], refs[1:]
    if last and not first:
        own_terms, refs = refs[0], refs[1:]
    if last:
        dq_out, refs = refs[:parts], refs[parts:]
    else:
        dq_out, refs = refs[0], refs[1:]
    kv_out, dq, dkv, key_t, docs_t, docs_s = refs
    row, me = place[0], place[1]
    width = GROUP * rows
    span = parts * rows

    def work():
        for a in range(parts):
            docs = own[2 * span + a * EXTRA : 2 * span + a * EXTRA + 1, 0:rows].astype(F32)
            docs_s[a] = jnp.min(docs)
        dq[...] = jnp.zeros_like(dq)
        dkv[...] = jnp.zeros_like(dkv)
        for b in range(parts):
            cut = slice(b * rows, (b + 1) * rows)
            key_t[:, cut] = key_ref[cut, :].T
            docs = key_ref[2 * span + b * EXTRA : 2 * span + b * EXTRA + 1, 0:rows].astype(F32)
            docs_t[cut, :] = jnp.broadcast_to(docs, (rows, rows)).T
            if (b + 1) % (parts // 2) == 0:
                docs_s[parts + b // (parts // 2)] = jnp.max(docs)
        half = span // 2
        for s in range(parts):
            a = me ^ s
            near = offset * span + a * rows
            low = (near - half + 1 < reach) & (docs_s[a] <= docs_s[parts])
            high = (near - span + 1 < reach) & (docs_s[a] <= docs_s[parts + 1])
            if offset == 0:
                high = high & (a * rows + rows > half)

            def block(start, stop, s=s, a=a, near=near):
                docs = own[pl.ds(pl.multiple_of(2 * span + a * EXTRA, EXTRA), EXTRA), :]
                docs = docs.astype(F32)[0:1, 0:rows]
                query = queries[s][0:width, :]
                grad = queries[s][width : 2 * width, :]
                stats = queries[s][2 * width :, :].astype(F32)
                stats = stats[0:EXTRA] + stats[EXTRA : 2 * EXTRA] + stats[2 * EXTRA :]
                gap = (
                    near
                    - start
                    + lax.broadcasted_iota(jnp.int32, (stop - start, rows), 1)
                    - lax.broadcasted_iota(jnp.int32, (stop - start, rows), 0)
                )
                mask = docs_t[start:stop, :] == docs
                if offset == 0:
                    mask = mask & (gap >= 0)
                if (offset + 1) * span > WINDOW:
                    mask = mask & (gap < WINDOW)
                scores = dot(key_ref[start:stop, :], query, ((1,), (1,)))
                dprob = dot(key_ref[span + start : span + stop, :], grad, ((1,), (1,)))
                probs, dscores = [], []
                for h in range(GROUP):
                    cut = slice(h * rows, (h + 1) * rows)
                    norm = stats[h : h + 1, :] * LOG2E
                    delta = stats[GROUP + h : GROUP + h + 1, :]
                    prob = jnp.exp2(scores[:, cut] * (SCALE * LOG2E) - norm)
                    prob = jnp.where(mask, prob, 0.0)
                    probs.append(prob.astype(BF16))
                    dscores.append((prob * (dprob[:, cut] - delta) * SCALE).astype(BF16))
                prob = jnp.concatenate(probs, 1)
                dscore = jnp.concatenate(dscores, 1)
                dkv[start:stop, :] += dot(dscore, query, ((1,), (0,)))
                dkv[span + start : span + stop, :] += dot(prob, grad, ((1,), (0,)))
                dq[s] += dot(key_t[:, start:stop], dscore, ((1,), (0,)))

            pl.when(low & high)(functools.partial(block, 0, span))
            pl.when(high & ~low)(functools.partial(block, half, span))
            if offset == 0:
                pl.when(low & ~high)(functools.partial(block, 0, half))

        kv_out[...] = dkv[...].astype(kv_out.dtype)
        for s in range(parts):
            total = dq[s] if first else dq[s] + dq_in[s]
            if last:
                close(s, total)
            else:
                dq_out[s] = total

    def close(s, total):
        out, a = dq_out[s], me ^ s
        for h in range(GROUP):
            at = slice(h * HEAD_SIZE, (h + 1) * HEAD_SIZE)
            out[at, :] = total[:, h * rows : (h + 1) * rows].astype(BF16)
        for k in range(2):
            at = GROUP * HEAD_SIZE + k * rows
            term = (kv_out if first else own_terms)[pl.ds(pl.multiple_of(k * span + a * rows, rows), rows), :]
            out[at : at + rows, :] = term.astype(BF16)

    if first:
        work()
        return

    @pl.when(row < offset)
    def _():
        kv_out[...] = jnp.zeros_like(kv_out)
        for s in range(parts):
            if last:
                close(s, dq_in[s])
            else:
                dq_out[s] = dq_in[s]

    pl.when(row >= offset)(work)


def add_terms(place, arrived, term, out):
    out[...] = (arrived[...].astype(F32) + term[...]).astype(BF16)


def cut_terms(rows, count, groups, place, *refs):
    parts = KEY_VALUE_HEADS
    terms, outs = refs[:count], refs[-len(groups) :]
    for group, out in zip(groups, outs):
        for n, s in enumerate(group):
            for k in range(2):
                at = pl.multiple_of((k * parts + (place[1] ^ s)) * rows, rows)
                total = sum(term[pl.ds(at, rows), :].astype(F32) for term in terms)
                start = (2 * n + k) * rows
                out[start : start + rows, :] = total.astype(BF16)


def spread_queries(place, *refs):
    pieces, (out, token, turned, sems) = refs[:-4], refs[-4:]
    width = GROUP * HEAD_SIZE
    copies = []
    for s, piece in enumerate(pieces):
        for h in range(GROUP):
            cut = slice(h * HEAD_SIZE, (h + 1) * HEAD_SIZE)
            turned[s, :, cut] = piece[cut, :].T
        cut = pl.ds(pl.multiple_of((place[1] ^ s) * width, width), width)
        copies.append(pltpu.make_async_copy(turned.at[s], out.at[:, cut], sems.at[s]))
        copies[-1].start()
    token[...] = jnp.zeros_like(token)
    for copy in copies:
        copy.wait()


def spread_keys(rows, sources, place, *refs):
    parts = KEY_VALUE_HEADS
    pieces, (key_out, value_out, total, sems) = refs[:-5], refs[-4:]
    copies = []
    for s in range(parts):
        term = pieces[s][GROUP * HEAD_SIZE :, :].astype(F32)
        for k in range(1, sources):
            term = term + pieces[k * parts + s][0 : 2 * rows, :].astype(F32)
        total[s] = term.astype(BF16)
        for k, out in enumerate((key_out, value_out)):
            source = total.at[s, k * rows : (k + 1) * rows, :]
            target = out.at[:, head_columns(place[1] ^ s)]
            copies.append(pltpu.make_async_copy(source, target, sems.at[s, k]))
            copies[-1].start()
    for copy in copies:
        copy.wait()


def local(
    queries, key_matrix, value_matrix, attention_output, output_gradient, log_sum_norm, doc_ids
):
    parts = KEY_VALUE_HEADS
    rows = queries.shape[0]
    count = lax.axis_size("tok")
    span = parts * rows
    reach = min(WINDOW, count * rows // 2)
    behind = min(-(-(reach - 1) // span), count // parts - 1)
    device = lax.axis_index("tok")
    place = jnp.stack([device // parts, device % parts]).astype(jnp.int32)
    width = GROUP * rows
    shape = jax.ShapeDtypeStruct

    def move(value, steps, s=0, low=0):
        def target(t):
            row, me = divmod(t, parts)
            if row < low:
                return t ^ 1
            if low <= row + steps < count // parts:
                return ((row + steps) * parts + me) ^ s
            row = low + (row - low + steps) % (count // parts - low)
            return row * parts + me

        return lax.ppermute(value, "tok", [(t, target(t)) for t in range(count)])

    def exchange(pieces):
        return [pieces[0]] + [move(pieces[s], 0, s) for s in range(1, parts)]

    *pieces, grads, outputs = call(
        functools.partial(pack_keys, rows),
        (place, key_matrix, value_matrix, doc_ids.reshape(1, rows), output_gradient, attention_output),
        [shape((2 * rows + EXTRA, HEAD_SIZE), BF16)] * parts + [shape(queries.shape, BF16)] * 2,
        scratch=[
            pltpu.VMEM((1, rows), jnp.int32),
            pltpu.SemaphoreType.DMA(()),
            pltpu.SemaphoreType.DMA((parts, 2)),
            pltpu.SemaphoreType.DMA((2,)),
        ],
        specs=[HBM] * 5,
    )
    pieces = exchange(pieces)
    *query_pieces, token = call(
        functools.partial(pack_queries, rows),
        (place, queries, grads, outputs, log_sum_norm),
        [shape((2 * width + 3 * EXTRA, HEAD_SIZE), BF16)] * parts + [TOKEN],
        scratch=[
            pltpu.VMEM((parts, 2 * GROUP, rows), F32),
            pltpu.SemaphoreType.DMA((parts, GROUP)),
        ],
        specs=[HBM, VMEM, VMEM, VMEM],
    )
    (own,) = call(
        functools.partial(join, rows),
        (place, *pieces, token),
        [shape((parts * (2 * rows + EXTRA), HEAD_SIZE), BF16)],
    )
    query_pieces = exchange(query_pieces)
    windows = [own]
    for k in range(behind):
        windows.append(move(windows[-1], 1, low=k))

    kv_shape = (2 * span, HEAD_SIZE)
    stages = [0] + list(range(behind, 0, -1))
    dq, own_terms, sent = None, None, None
    for k, offset in enumerate(stages):
        first, last = k == 0, k == len(stages) - 1
        ins = [place, *query_pieces, own, windows[offset]]
        if not first:
            ins.append(dq)
        if last and not first:
            ins.append(own_terms)
        if last:
            outs = [shape((GROUP * HEAD_SIZE + 2 * rows, rows), BF16)] * parts
        else:
            outs = [shape((parts, HEAD_SIZE, width), F32)]
        outs = outs + [shape(kv_shape, BF16 if offset == behind > 0 else F32)]
        got = call(
            functools.partial(attend, rows, offset, reach, first, last),
            ins,
            outs,
            scratch=attend_scratch(rows),
            flops=10 * span * span * GROUP * HEAD_SIZE,
        )
        dq, term = (got[:parts] if last else got[0]), got[-1]
        if offset == 0:
            own_terms = term
        elif offset == 1:
            terms = (term,) if sent is None else (sent, term)
            groups = ((2, 3), (0,), (1,))
            got = call(
                functools.partial(cut_terms, rows, len(terms), groups),
                (place, *terms),
                [shape((2 * rows * len(group), HEAD_SIZE), BF16) for group in groups],
            )
            far, straight, beside = [move(piece, -1, group[0]) for piece, group in zip(got, groups)]
            sent = [straight, beside, far, move(far[2 * rows :], 0, 1)]
        elif sent is None:
            sent = move(term, -1, low=offset - 1)
        else:
            (term,) = call(add_terms, (place, sent, term), [shape(kv_shape, BF16)])
            sent = move(term, -1, low=offset - 1)

    dq_pieces = exchange(dq)
    query_grad, token = call(
        spread_queries,
        (place, *dq_pieces),
        [shape((rows, parts * GROUP * HEAD_SIZE), BF16), TOKEN],
        scratch=[
            pltpu.VMEM((parts, rows, GROUP * HEAD_SIZE), BF16),
            pltpu.SemaphoreType.DMA((parts,)),
        ],
        out_specs=[HBM, VMEM],
    )
    pieces = dq_pieces + (sent or [])
    key_grad, value_grad = call(
        functools.partial(spread_keys, rows, len(pieces) // parts),
        (place, *pieces, token),
        [shape((rows, parts * HEAD_SIZE), BF16)] * 2,
        scratch=[
            pltpu.VMEM((parts, 2 * rows, HEAD_SIZE), BF16),
            pltpu.SemaphoreType.DMA((parts, 2)),
        ],
        out_specs=[HBM, HBM],
    )
    return query_grad, key_grad, value_grad


def solution(mesh):
    axes = ("groups", "tok")
    return jax.shard_map(
        local,
        mesh=mesh,
        in_specs=(
            P(axes, None),
            P(axes, None),
            P(axes, None),
            P(axes, None),
            P(axes, None),
            P(None, axes),
            P(axes),
        ),
        out_specs=(P(axes, None), P(axes, None), P(axes, None)),
        check_vma=False,
    )
```

```python
import functools
import math

import jax
import jax.numpy as jnp
from jax import lax
from jax.experimental import pallas as pl
from jax.experimental.pallas import tpu as pltpu
from jax.sharding import PartitionSpec as P

WINDOW = 4096
QUERY_HEADS = 16
KEY_VALUE_HEADS = 4
HEAD_SIZE = 128
GROUP = QUERY_HEADS // KEY_VALUE_HEADS
SCALE = HEAD_SIZE ** (-0.5)
LOG2E = math.log2(math.e)
EXTRA = 8
F32 = jnp.float32
BF16 = jnp.bfloat16

VMEM = pl.BlockSpec(memory_space=pltpu.VMEM)
SMEM = pl.BlockSpec(memory_space=pltpu.SMEM)


def dot(a, b, dims):
    return lax.dot_general(a, b, (dims, ((), ())), preferred_element_type=F32)


HBM = pl.BlockSpec(memory_space=pltpu.MemorySpace.HBM)
TOKEN = jax.ShapeDtypeStruct((8, 128), F32)


def call(kernel, ins, outs, scratch=(), flops=0, specs=None, out_specs=None):
    specs = specs or [VMEM] * (len(ins) - 1)
    ins = [ins[0]] + [
        pltpu.with_memory_space_constraint(x, pltpu.MemorySpace.HBM) if spec is HBM else x
        for x, spec in zip(ins[1:], specs)
    ]
    size = sum(math.prod(o.shape) * o.dtype.itemsize for o in outs)
    size += sum(math.prod(x.shape) * x.dtype.itemsize for x in ins)
    return pl.pallas_call(
        kernel,
        out_shape=outs,
        in_specs=[SMEM] + specs,
        out_specs=out_specs or [VMEM] * len(outs),
        scratch_shapes=list(scratch),
        cost_estimate=pl.CostEstimate(flops=flops, bytes_accessed=size, transcendentals=0),
        compiler_params=pltpu.CompilerParams(vmem_limit_bytes=48 << 20),
    )(*ins)


def head_columns(g):
    return pl.ds(pl.multiple_of(g * HEAD_SIZE, HEAD_SIZE), HEAD_SIZE)


def pack_keys(rows, place, key_ref, value_ref, doc_ref, grad_ref, output_ref, *rest):
    outs, (grads, outputs, ids, doc_sem, sems, more_sems) = rest[:-6], rest[-6:]
    first = pltpu.make_async_copy(doc_ref, ids, doc_sem)
    first.start()
    copies = []
    for s, out in enumerate(outs):
        cut = head_columns(place[1] ^ s)
        for k, source in enumerate((key_ref, value_ref)):
            target = out.at[k * rows : (k + 1) * rows, :]
            copies.append(pltpu.make_async_copy(source.at[:, cut], target, sems.at[s, k]))
    copies.append(pltpu.make_async_copy(grad_ref, grads, more_sems.at[0]))
    copies.append(pltpu.make_async_copy(output_ref, outputs, more_sems.at[1]))
    for copy in copies:
        copy.start()
    first.wait()
    docs = jnp.broadcast_to((ids[...] + 1).astype(F32), (EXTRA, rows)).astype(BF16)
    for out in outs:
        out[2 * rows :, 0:rows] = docs
    for copy in copies:
        copy.wait()


def pack_queries(rows, place, query_ref, grads, outputs, norm_ref, *rest):
    outs, (token, stats, sems) = rest[:-3], rest[-3:]
    copies = []
    for s, out in enumerate(outs):
        for h in range(GROUP):
            cut = head_columns((place[1] ^ s) * GROUP + h)
            target = out.at[h * rows : (h + 1) * rows, :]
            copies.append(pltpu.make_async_copy(query_ref.at[:, cut], target, sems.at[s, h]))
    for copy in copies:
        copy.start()
    for s, out in enumerate(outs):
        for h in range(GROUP):
            at = (GROUP + h) * rows
            out[at : at + rows, :] = grads[:, head_columns((place[1] ^ s) * GROUP + h)]
    lane = lax.broadcasted_iota(jnp.int32, (rows, HEAD_SIZE), 1)
    columns = jnp.zeros((rows, HEAD_SIZE), F32)
    for h in range(QUERY_HEADS):
        cut = slice(h * HEAD_SIZE, (h + 1) * HEAD_SIZE)
        product = grads[:, cut].astype(F32) * outputs[:, cut].astype(F32)
        columns = jnp.where(lane == h, jnp.sum(product, 1, keepdims=True), columns)
    delta = columns.T
    for g in range(KEY_VALUE_HEADS):
        stats[g, 0:GROUP, :] = norm_ref[g * GROUP : (g + 1) * GROUP, :]
        stats[g, GROUP : 2 * GROUP, :] = delta[g * GROUP : (g + 1) * GROUP, :]
    for s, out in enumerate(outs):
        left = stats[place[1] ^ s]
        for part in range(3):
            term = left.astype(BF16)
            at = 2 * GROUP * rows + part * EXTRA
            out[at : at + EXTRA, 0:rows] = term
            left = left - term.astype(F32)
    for copy in copies:
        copy.wait()
    token[...] = jnp.zeros_like(token)


def join(rows, place, *refs):
    parts = KEY_VALUE_HEADS
    pieces, out = refs[:parts], refs[-1]
    span = parts * rows
    for s, piece in enumerate(pieces):
        a = place[1] ^ s
        for k in range(2):
            at = pl.multiple_of(k * span + a * rows, rows)
            out[pl.ds(at, rows), :] = piece[k * rows : (k + 1) * rows, :]
        at = pl.multiple_of(2 * span + a * EXTRA, EXTRA)
        out[pl.ds(at, EXTRA), :] = piece[2 * rows :, :]


def attend_scratch(rows):
    parts = KEY_VALUE_HEADS
    return [
        pltpu.VMEM((parts, HEAD_SIZE, GROUP * rows), F32),
        pltpu.VMEM((2 * parts * rows, HEAD_SIZE), F32),
        pltpu.VMEM((HEAD_SIZE, parts * rows), BF16),
        pltpu.VMEM((parts * rows, rows), F32),
        pltpu.SMEM((2 * parts,), F32),
    ]


def attend(rows, offset, reach, earlier, last, place, *refs):
    parts = KEY_VALUE_HEADS
    queries, refs = refs[:parts], refs[parts:]
    own, key_ref, refs = refs[0], refs[1], refs[2:]
    first = earlier == 0
    if last:
        dq_in, refs = refs[:earlier], refs[earlier:]
    if last and not first:
        own_terms, refs = refs[0], refs[1:]
    if last:
        dq_out, refs = refs[:parts], refs[parts:]
    else:
        dq_out, refs = refs[0], refs[1:]
    kv_out, dq_sum, dkv, key_t, docs_t, docs_s = refs
    dq = dq_sum if last else dq_out
    row, me = place[0], place[1]
    width = GROUP * rows
    span = parts * rows

    def work():
        for a in range(parts):
            docs = own[2 * span + a * EXTRA : 2 * span + a * EXTRA + 1, 0:rows].astype(F32)
            docs_s[a] = jnp.min(docs)
        dq[...] = jnp.zeros_like(dq)
        dkv[...] = jnp.zeros_like(dkv)
        for b in range(parts):
            cut = slice(b * rows, (b + 1) * rows)
            key_t[:, cut] = key_ref[cut, :].T
            docs = key_ref[2 * span + b * EXTRA : 2 * span + b * EXTRA + 1, 0:rows].astype(F32)
            docs_t[cut, :] = jnp.broadcast_to(docs, (rows, rows)).T
            if (b + 1) % (parts // 2) == 0:
                docs_s[parts + b // (parts // 2)] = jnp.max(docs)
        half = span // 2
        for s in range(parts):
            a = me ^ s
            near = offset * span + a * rows
            low = (near - half + 1 < reach) & (docs_s[a] <= docs_s[parts])
            high = (near - span + 1 < reach) & (docs_s[a] <= docs_s[parts + 1])
            if offset == 0:
                high = high & (a * rows + rows > half)

            def block(start, stop, s=s, a=a, near=near):
                docs = own[pl.ds(pl.multiple_of(2 * span + a * EXTRA, EXTRA), EXTRA), :]
                docs = docs.astype(F32)[0:1, 0:rows]
                query = queries[s][0:width, :]
                grad = queries[s][width : 2 * width, :]
                stats = queries[s][2 * width :, :].astype(F32)
                stats = stats[0:EXTRA] + stats[EXTRA : 2 * EXTRA] + stats[2 * EXTRA :]
                gap = (
                    near
                    - start
                    + lax.broadcasted_iota(jnp.int32, (stop - start, rows), 1)
                    - lax.broadcasted_iota(jnp.int32, (stop - start, rows), 0)
                )
                mask = docs_t[start:stop, :] == docs
                if offset == 0:
                    mask = mask & (gap >= 0)
                if (offset + 1) * span > WINDOW:
                    mask = mask & (gap < WINDOW)
                scores = dot(key_ref[start:stop, :], query, ((1,), (1,)))
                dprob = dot(key_ref[span + start : span + stop, :], grad, ((1,), (1,)))
                probs, dscores = [], []
                for h in range(GROUP):
                    cut = slice(h * rows, (h + 1) * rows)
                    norm = stats[h : h + 1, :] * LOG2E
                    delta = stats[GROUP + h : GROUP + h + 1, :]
                    prob = jnp.exp2(scores[:, cut] * (SCALE * LOG2E) - norm)
                    prob = jnp.where(mask, prob, 0.0)
                    probs.append(prob.astype(BF16))
                    dscores.append((prob * (dprob[:, cut] - delta) * SCALE).astype(BF16))
                prob = jnp.concatenate(probs, 1)
                dscore = jnp.concatenate(dscores, 1)
                dkv[start:stop, :] += dot(dscore, query, ((1,), (0,)))
                dkv[span + start : span + stop, :] += dot(prob, grad, ((1,), (0,)))
                dq[s] += dot(key_t[:, start:stop], dscore, ((1,), (0,)))

            pl.when(low & high)(functools.partial(block, 0, span))
            pl.when(high & ~low)(functools.partial(block, half, span))
            if offset == 0:
                pl.when(low & ~high)(functools.partial(block, 0, half))

        kv_out[...] = dkv[...].astype(kv_out.dtype)
        if last:
            for s in range(parts):
                close(s, sum([part[s] for part in dq_in], dq[s]))

    def close(s, total):
        out, a = dq_out[s], me ^ s
        for h in range(GROUP):
            at = slice(h * HEAD_SIZE, (h + 1) * HEAD_SIZE)
            out[at, :] = total[:, h * rows : (h + 1) * rows].astype(BF16)
        for k in range(2):
            at = GROUP * HEAD_SIZE + k * rows
            term = (kv_out if first else own_terms)[pl.ds(pl.multiple_of(k * span + a * rows, rows), rows), :]
            out[at : at + rows, :] = term.astype(BF16)

    if first:
        work()
        return

    @pl.when(row < offset)
    def _():
        kv_out[...] = jnp.zeros_like(kv_out)
        if last:
            for s in range(parts):
                close(s, sum([part[s] for part in dq_in[1:]], dq_in[0][s]))
        else:
            dq_out[...] = jnp.zeros_like(dq_out)

    pl.when(row >= offset)(work)


def add_terms(place, arrived, term, out):
    out[...] = (arrived[...].astype(F32) + term[...]).astype(BF16)


def cut_terms(rows, count, groups, place, *refs):
    parts = KEY_VALUE_HEADS
    terms, outs = refs[:count], refs[-len(groups) :]
    for group, out in zip(groups, outs):
        for n, s in enumerate(group):
            for k in range(2):
                at = pl.multiple_of((k * parts + (place[1] ^ s)) * rows, rows)
                total = sum(term[pl.ds(at, rows), :].astype(F32) for term in terms)
                start = (2 * n + k) * rows
                out[start : start + rows, :] = total.astype(BF16)


def spread_queries(place, *refs):
    pieces, (out, token, turned, sems) = refs[:-4], refs[-4:]
    width = GROUP * HEAD_SIZE
    copies = []
    for s, piece in enumerate(pieces):
        for h in range(GROUP):
            cut = slice(h * HEAD_SIZE, (h + 1) * HEAD_SIZE)
            turned[s, :, cut] = piece[cut, :].T
        cut = pl.ds(pl.multiple_of((place[1] ^ s) * width, width), width)
        copies.append(pltpu.make_async_copy(turned.at[s], out.at[:, cut], sems.at[s]))
        copies[-1].start()
    token[...] = jnp.zeros_like(token)
    for copy in copies:
        copy.wait()


def spread_keys(rows, sources, place, *refs):
    parts = KEY_VALUE_HEADS
    pieces, (key_out, value_out, total, sems) = refs[:-5], refs[-4:]
    copies = []
    for s in range(parts):
        term = pieces[s][GROUP * HEAD_SIZE :, :].astype(F32)
        for k in range(1, sources):
            term = term + pieces[k * parts + s][0 : 2 * rows, :].astype(F32)
        total[s] = term.astype(BF16)
        for k, out in enumerate((key_out, value_out)):
            source = total.at[s, k * rows : (k + 1) * rows, :]
            target = out.at[:, head_columns(place[1] ^ s)]
            copies.append(pltpu.make_async_copy(source, target, sems.at[s, k]))
            copies[-1].start()
    for copy in copies:
        copy.wait()


def local(
    queries, key_matrix, value_matrix, attention_output, output_gradient, log_sum_norm, doc_ids
):
    parts = KEY_VALUE_HEADS
    rows = queries.shape[0]
    count = lax.axis_size("tok")
    span = parts * rows
    reach = min(WINDOW, count * rows // 2)
    behind = min(-(-(reach - 1) // span), count // parts - 1)
    device = lax.axis_index("tok")
    place = jnp.stack([device // parts, device % parts]).astype(jnp.int32)
    width = GROUP * rows
    shape = jax.ShapeDtypeStruct

    def move(value, steps, s=0, low=0):
        def target(t):
            row, me = divmod(t, parts)
            if row < low:
                return t ^ 1
            if low <= row + steps < count // parts:
                return ((row + steps) * parts + me) ^ s
            row = low + (row - low + steps) % (count // parts - low)
            return row * parts + me

        return lax.ppermute(value, "tok", [(t, target(t)) for t in range(count)])

    def exchange(pieces):
        return [pieces[0]] + [move(pieces[s], 0, s) for s in range(1, parts)]

    *pieces, grads, outputs = call(
        functools.partial(pack_keys, rows),
        (place, key_matrix, value_matrix, doc_ids.reshape(1, rows), output_gradient, attention_output),
        [shape((2 * rows + EXTRA, HEAD_SIZE), BF16)] * parts + [shape(queries.shape, BF16)] * 2,
        scratch=[
            pltpu.VMEM((1, rows), jnp.int32),
            pltpu.SemaphoreType.DMA(()),
            pltpu.SemaphoreType.DMA((parts, 2)),
            pltpu.SemaphoreType.DMA((2,)),
        ],
        specs=[HBM] * 5,
    )
    pieces = exchange(pieces)
    *query_pieces, token = call(
        functools.partial(pack_queries, rows),
        (place, queries, grads, outputs, log_sum_norm),
        [shape((2 * width + 3 * EXTRA, HEAD_SIZE), BF16)] * parts + [TOKEN],
        scratch=[
            pltpu.VMEM((parts, 2 * GROUP, rows), F32),
            pltpu.SemaphoreType.DMA((parts, GROUP)),
        ],
        specs=[HBM, VMEM, VMEM, VMEM],
    )
    (own,) = call(
        functools.partial(join, rows),
        (place, *pieces, token),
        [shape((parts * (2 * rows + EXTRA), HEAD_SIZE), BF16)],
    )
    query_pieces = exchange(query_pieces)
    windows = [own]
    for k in range(behind):
        windows.append(move(windows[-1], 1, low=k))

    kv_shape = (2 * span, HEAD_SIZE)
    stages = [0] + list(range(behind, 0, -1))
    dq_parts, own_terms, sent = [], None, None
    for k, offset in enumerate(stages):
        first, last = k == 0, k == len(stages) - 1
        ins = [place, *query_pieces, own, windows[offset]]
        if last and not first:
            ins += [*dq_parts, own_terms]
        if last:
            outs = [shape((GROUP * HEAD_SIZE + 2 * rows, rows), BF16)] * parts
        else:
            outs = [shape((parts, HEAD_SIZE, width), F32)]
        outs = outs + [shape(kv_shape, BF16 if offset == behind > 0 else F32)]
        got = call(
            functools.partial(attend, rows, offset, reach, k, last),
            ins,
            outs,
            scratch=attend_scratch(rows),
            flops=10 * span * span * GROUP * HEAD_SIZE,
        )
        term = got[-1]
        if last:
            dq = got[:parts]
        else:
            dq_parts.append(got[0])
        if offset == 0:
            own_terms = term
        elif offset == 1:
            terms = (term,) if sent is None else (sent, term)
            groups = ((2, 3), (0,), (1,))
            got = call(
                functools.partial(cut_terms, rows, len(terms), groups),
                (place, *terms),
                [shape((2 * rows * len(group), HEAD_SIZE), BF16) for group in groups],
            )
            far, straight, beside = [move(piece, -1, group[0]) for piece, group in zip(got, groups)]
            sent = [straight, beside, far, move(far[2 * rows :], 0, 1)]
        elif sent is None:
            sent = move(term, -1, low=offset - 1)
        else:
            (term,) = call(add_terms, (place, sent, term), [shape(kv_shape, BF16)])
            sent = move(term, -1, low=offset - 1)

    dq_pieces = exchange(dq)
    query_grad, token = call(
        spread_queries,
        (place, *dq_pieces),
        [shape((rows, parts * GROUP * HEAD_SIZE), BF16), TOKEN],
        scratch=[
            pltpu.VMEM((parts, rows, GROUP * HEAD_SIZE), BF16),
            pltpu.SemaphoreType.DMA((parts,)),
        ],
        out_specs=[HBM, VMEM],
    )
    pieces = dq_pieces + (sent or [])
    key_grad, value_grad = call(
        functools.partial(spread_keys, rows, len(pieces) // parts),
        (place, *pieces, token),
        [shape((rows, parts * HEAD_SIZE), BF16)] * 2,
        scratch=[
            pltpu.VMEM((parts, 2 * rows, HEAD_SIZE), BF16),
            pltpu.SemaphoreType.DMA((parts, 2)),
        ],
        out_specs=[HBM, HBM],
    )
    return query_grad, key_grad, value_grad


def solution(mesh):
    axes = ("groups", "tok")
    return jax.shard_map(
        local,
        mesh=mesh,
        in_specs=(
            P(axes, None),
            P(axes, None),
            P(axes, None),
            P(axes, None),
            P(axes, None),
            P(None, axes),
            P(axes),
        ),
        out_specs=(P(axes, None), P(axes, None), P(axes, None)),
        check_vma=False,
    )
```

```python
import functools
import math

import jax
import jax.numpy as jnp
from jax import lax
from jax.experimental import pallas as pl
from jax.experimental.pallas import tpu as pltpu
from jax.sharding import PartitionSpec as P

WINDOW = 4096
QUERY_HEADS = 16
KEY_VALUE_HEADS = 4
HEAD_SIZE = 128
GROUP = QUERY_HEADS // KEY_VALUE_HEADS
SCALE = HEAD_SIZE ** (-0.5)
LOG2E = math.log2(math.e)
EXTRA = 8
F32 = jnp.float32
BF16 = jnp.bfloat16

VMEM = pl.BlockSpec(memory_space=pltpu.VMEM)
SMEM = pl.BlockSpec(memory_space=pltpu.SMEM)


def dot(a, b, dims):
    return lax.dot_general(a, b, (dims, ((), ())), preferred_element_type=F32)


HBM = pl.BlockSpec(memory_space=pltpu.MemorySpace.HBM)
TOKEN = jax.ShapeDtypeStruct((8, 128), F32)


def call(kernel, ins, outs, scratch=(), flops=0, specs=None, out_specs=None):
    specs = specs or [VMEM] * (len(ins) - 1)
    ins = [ins[0]] + [
        pltpu.with_memory_space_constraint(x, pltpu.MemorySpace.HBM) if spec is HBM else x
        for x, spec in zip(ins[1:], specs)
    ]
    size = sum(math.prod(o.shape) * o.dtype.itemsize for o in outs)
    size += sum(math.prod(x.shape) * x.dtype.itemsize for x in ins)
    return pl.pallas_call(
        kernel,
        out_shape=outs,
        in_specs=[SMEM] + specs,
        out_specs=out_specs or [VMEM] * len(outs),
        scratch_shapes=list(scratch),
        cost_estimate=pl.CostEstimate(flops=flops, bytes_accessed=size, transcendentals=0),
        compiler_params=pltpu.CompilerParams(vmem_limit_bytes=48 << 20),
    )(*ins)


def head_columns(g):
    return pl.ds(pl.multiple_of(g * HEAD_SIZE, HEAD_SIZE), HEAD_SIZE)


def pack_keys(rows, place, key_ref, value_ref, doc_ref, query_ref, grad_ref, output_ref, *rest):
    outs, (queries, grads, outputs, ids, doc_sem, sems, more_sems) = rest[:-7], rest[-7:]
    first = pltpu.make_async_copy(doc_ref, ids, doc_sem)
    first.start()
    copies = []
    for s, out in enumerate(outs):
        cut = head_columns(place[1] ^ s)
        for k, source in enumerate((key_ref, value_ref)):
            target = out.at[k * rows : (k + 1) * rows, :]
            copies.append(pltpu.make_async_copy(source.at[:, cut], target, sems.at[s, k]))
    copies.append(pltpu.make_async_copy(grad_ref, grads, more_sems.at[0]))
    copies.append(pltpu.make_async_copy(output_ref, outputs, more_sems.at[1]))
    copies.append(pltpu.make_async_copy(query_ref, queries, more_sems.at[2]))
    for copy in copies:
        copy.start()
    first.wait()
    docs = jnp.broadcast_to((ids[...] + 1).astype(F32), (EXTRA, rows)).astype(BF16)
    for out in outs:
        out[2 * rows :, 0:rows] = docs
    for copy in copies:
        copy.wait()


def pack_queries(rows, place, query_ref, grads, outputs, norm_ref, *rest):
    outs, (token, stats) = rest[:-2], rest[-2:]
    for s, out in enumerate(outs):
        for h in range(GROUP):
            cut = head_columns((place[1] ^ s) * GROUP + h)
            for k, source in enumerate((query_ref, grads)):
                at = (k * GROUP + h) * rows
                out[at : at + rows, :] = source[:, cut]
    lane = lax.broadcasted_iota(jnp.int32, (rows, HEAD_SIZE), 1)
    columns = jnp.zeros((rows, HEAD_SIZE), F32)
    for h in range(QUERY_HEADS):
        cut = slice(h * HEAD_SIZE, (h + 1) * HEAD_SIZE)
        product = grads[:, cut].astype(F32) * outputs[:, cut].astype(F32)
        columns = jnp.where(lane == h, jnp.sum(product, 1, keepdims=True), columns)
    delta = columns.T
    for g in range(KEY_VALUE_HEADS):
        stats[g, 0:GROUP, :] = norm_ref[g * GROUP : (g + 1) * GROUP, :]
        stats[g, GROUP : 2 * GROUP, :] = delta[g * GROUP : (g + 1) * GROUP, :]
    for s, out in enumerate(outs):
        left = stats[place[1] ^ s]
        for part in range(3):
            term = left.astype(BF16)
            at = 2 * GROUP * rows + part * EXTRA
            out[at : at + EXTRA, 0:rows] = term
            left = left - term.astype(F32)
    token[...] = jnp.zeros_like(token)


def join(rows, place, *refs):
    parts = KEY_VALUE_HEADS
    pieces, out = refs[:parts], refs[-1]
    span = parts * rows
    for s, piece in enumerate(pieces):
        a = place[1] ^ s
        for k in range(2):
            at = pl.multiple_of(k * span + a * rows, rows)
            out[pl.ds(at, rows), :] = piece[k * rows : (k + 1) * rows, :]
        at = pl.multiple_of(2 * span + a * EXTRA, EXTRA)
        out[pl.ds(at, EXTRA), :] = piece[2 * rows :, :]


def attend_scratch(rows):
    parts = KEY_VALUE_HEADS
    return [
        pltpu.VMEM((parts, HEAD_SIZE, GROUP * rows), F32),
        pltpu.VMEM((2 * parts * rows, HEAD_SIZE), F32),
        pltpu.VMEM((HEAD_SIZE, parts * rows), BF16),
        pltpu.VMEM((parts * rows, rows), F32),
        pltpu.SMEM((2 * parts,), F32),
    ]


def attend(rows, offset, reach, earlier, last, place, *refs):
    parts = KEY_VALUE_HEADS
    queries, refs = refs[:parts], refs[parts:]
    own, key_ref, refs = refs[0], refs[1], refs[2:]
    first = earlier == 0
    if last:
        dq_in, refs = refs[:earlier], refs[earlier:]
    if last and not first:
        own_terms, refs = refs[0], refs[1:]
    if last:
        dq_out, refs = refs[:parts], refs[parts:]
    else:
        dq_out, refs = refs[0], refs[1:]
    kv_out, dq_sum, dkv, key_t, docs_t, docs_s = refs
    dq = dq_sum if last else dq_out
    row, me = place[0], place[1]
    width = GROUP * rows
    span = parts * rows

    def work():
        for a in range(parts):
            docs = own[2 * span + a * EXTRA : 2 * span + a * EXTRA + 1, 0:rows].astype(F32)
            docs_s[a] = jnp.min(docs)
        dq[...] = jnp.zeros_like(dq)
        dkv[...] = jnp.zeros_like(dkv)
        for b in range(parts):
            cut = slice(b * rows, (b + 1) * rows)
            key_t[:, cut] = key_ref[cut, :].T
            docs = key_ref[2 * span + b * EXTRA : 2 * span + b * EXTRA + 1, 0:rows].astype(F32)
            docs_t[cut, :] = jnp.broadcast_to(docs, (rows, rows)).T
            if (b + 1) % (parts // 2) == 0:
                docs_s[parts + b // (parts // 2)] = jnp.max(docs)
        half = span // 2
        for s in range(parts):
            a = me ^ s
            near = offset * span + a * rows
            low = (near - half + 1 < reach) & (docs_s[a] <= docs_s[parts])
            high = (near - span + 1 < reach) & (docs_s[a] <= docs_s[parts + 1])
            if offset == 0:
                high = high & (a * rows + rows > half)

            def block(start, stop, s=s, a=a, near=near):
                docs = own[pl.ds(pl.multiple_of(2 * span + a * EXTRA, EXTRA), EXTRA), :]
                docs = docs.astype(F32)[0:1, 0:rows]
                query = queries[s][0:width, :]
                grad = queries[s][width : 2 * width, :]
                stats = queries[s][2 * width :, :].astype(F32)
                stats = stats[0:EXTRA] + stats[EXTRA : 2 * EXTRA] + stats[2 * EXTRA :]
                gap = (
                    near
                    - start
                    + lax.broadcasted_iota(jnp.int32, (stop - start, rows), 1)
                    - lax.broadcasted_iota(jnp.int32, (stop - start, rows), 0)
                )
                mask = docs_t[start:stop, :] == docs
                if offset == 0:
                    mask = mask & (gap >= 0)
                if (offset + 1) * span > WINDOW:
                    mask = mask & (gap < WINDOW)
                scores = dot(key_ref[start:stop, :], query, ((1,), (1,)))
                dprob = dot(key_ref[span + start : span + stop, :], grad, ((1,), (1,)))
                probs, dscores = [], []
                for h in range(GROUP):
                    cut = slice(h * rows, (h + 1) * rows)
                    norm = stats[h : h + 1, :] * LOG2E
                    delta = stats[GROUP + h : GROUP + h + 1, :]
                    prob = jnp.exp2(scores[:, cut] * (SCALE * LOG2E) - norm)
                    prob = jnp.where(mask, prob, 0.0)
                    probs.append(prob.astype(BF16))
                    dscores.append((prob * (dprob[:, cut] - delta) * SCALE).astype(BF16))
                prob = jnp.concatenate(probs, 1)
                dscore = jnp.concatenate(dscores, 1)
                dkv[start:stop, :] += dot(dscore, query, ((1,), (0,)))
                dkv[span + start : span + stop, :] += dot(prob, grad, ((1,), (0,)))
                dq[s] += dot(key_t[:, start:stop], dscore, ((1,), (0,)))

            pl.when(low & high)(functools.partial(block, 0, span))
            pl.when(high & ~low)(functools.partial(block, half, span))
            if offset == 0:
                pl.when(low & ~high)(functools.partial(block, 0, half))

        kv_out[...] = dkv[...].astype(kv_out.dtype)
        if last:
            for s in range(parts):
                close(s, sum([part[s] for part in dq_in], dq[s]))

    def close(s, total):
        out, a = dq_out[s], me ^ s
        for h in range(GROUP):
            at = slice(h * HEAD_SIZE, (h + 1) * HEAD_SIZE)
            out[at, :] = total[:, h * rows : (h + 1) * rows].astype(BF16)
        for k in range(2):
            at = GROUP * HEAD_SIZE + k * rows
            term = (kv_out if first else own_terms)[pl.ds(pl.multiple_of(k * span + a * rows, rows), rows), :]
            out[at : at + rows, :] = term.astype(BF16)

    if first:
        work()
        return

    @pl.when(row < offset)
    def _():
        kv_out[...] = jnp.zeros_like(kv_out)
        if last:
            for s in range(parts):
                close(s, sum([part[s] for part in dq_in[1:]], dq_in[0][s]))
        else:
            dq_out[...] = jnp.zeros_like(dq_out)

    pl.when(row >= offset)(work)


def add_terms(place, arrived, term, out):
    out[...] = (arrived[...].astype(F32) + term[...]).astype(BF16)


def cut_terms(rows, count, groups, place, *refs):
    parts = KEY_VALUE_HEADS
    terms, outs = refs[:count], refs[-len(groups) :]
    for group, out in zip(groups, outs):
        for n, s in enumerate(group):
            for k in range(2):
                at = pl.multiple_of((k * parts + (place[1] ^ s)) * rows, rows)
                total = sum(term[pl.ds(at, rows), :].astype(F32) for term in terms)
                start = (2 * n + k) * rows
                out[start : start + rows, :] = total.astype(BF16)


def spread_queries(place, *refs):
    pieces, (out, token, turned, sems) = refs[:-4], refs[-4:]
    width = GROUP * HEAD_SIZE
    copies = []
    for s, piece in enumerate(pieces):
        for h in range(GROUP):
            cut = slice(h * HEAD_SIZE, (h + 1) * HEAD_SIZE)
            turned[s, :, cut] = piece[cut, :].T
        cut = pl.ds(pl.multiple_of((place[1] ^ s) * width, width), width)
        copies.append(pltpu.make_async_copy(turned.at[s], out.at[:, cut], sems.at[s]))
        copies[-1].start()
    token[...] = jnp.zeros_like(token)
    for copy in copies:
        copy.wait()


def spread_keys(rows, sources, place, *refs):
    parts = KEY_VALUE_HEADS
    pieces, (key_out, value_out, total, sems) = refs[:-5], refs[-4:]
    copies = []
    for s in range(parts):
        term = pieces[s][GROUP * HEAD_SIZE :, :].astype(F32)
        for k in range(1, sources):
            term = term + pieces[k * parts + s][0 : 2 * rows, :].astype(F32)
        total[s] = term.astype(BF16)
        for k, out in enumerate((key_out, value_out)):
            source = total.at[s, k * rows : (k + 1) * rows, :]
            target = out.at[:, head_columns(place[1] ^ s)]
            copies.append(pltpu.make_async_copy(source, target, sems.at[s, k]))
            copies[-1].start()
    for copy in copies:
        copy.wait()


def local(
    queries, key_matrix, value_matrix, attention_output, output_gradient, log_sum_norm, doc_ids
):
    parts = KEY_VALUE_HEADS
    rows = queries.shape[0]
    count = lax.axis_size("tok")
    span = parts * rows
    reach = min(WINDOW, count * rows // 2)
    behind = min(-(-(reach - 1) // span), count // parts - 1)
    device = lax.axis_index("tok")
    place = jnp.stack([device // parts, device % parts]).astype(jnp.int32)
    width = GROUP * rows
    shape = jax.ShapeDtypeStruct

    def move(value, steps, s=0, low=0):
        def target(t):
            row, me = divmod(t, parts)
            if row < low:
                return t ^ 1
            if low <= row + steps < count // parts:
                return ((row + steps) * parts + me) ^ s
            row = low + (row - low + steps) % (count // parts - low)
            return row * parts + me

        return lax.ppermute(value, "tok", [(t, target(t)) for t in range(count)])

    def exchange(pieces):
        return [pieces[0]] + [move(pieces[s], 0, s) for s in range(1, parts)]

    *pieces, held, grads, outputs = call(
        functools.partial(pack_keys, rows),
        (place, key_matrix, value_matrix, doc_ids.reshape(1, rows), queries, output_gradient, attention_output),
        [shape((2 * rows + EXTRA, HEAD_SIZE), BF16)] * parts + [shape(queries.shape, BF16)] * 3,
        scratch=[
            pltpu.VMEM((1, rows), jnp.int32),
            pltpu.SemaphoreType.DMA(()),
            pltpu.SemaphoreType.DMA((parts, 2)),
            pltpu.SemaphoreType.DMA((3,)),
        ],
        specs=[HBM] * 6,
    )
    pieces = exchange(pieces)
    *query_pieces, token = call(
        functools.partial(pack_queries, rows),
        (place, held, grads, outputs, log_sum_norm),
        [shape((2 * width + 3 * EXTRA, HEAD_SIZE), BF16)] * parts + [TOKEN],
        scratch=[
            pltpu.VMEM((parts, 2 * GROUP, rows), F32),
        ],
        specs=[VMEM, VMEM, VMEM, VMEM],
    )
    (own,) = call(
        functools.partial(join, rows),
        (place, *pieces, token),
        [shape((parts * (2 * rows + EXTRA), HEAD_SIZE), BF16)],
    )
    query_pieces = exchange(query_pieces)
    windows = [own]
    for k in range(behind):
        windows.append(move(windows[-1], 1, low=k))

    kv_shape = (2 * span, HEAD_SIZE)
    stages = [0] + list(range(behind, 0, -1))
    dq_parts, own_terms, sent = [], None, None
    for k, offset in enumerate(stages):
        first, last = k == 0, k == len(stages) - 1
        ins = [place, *query_pieces, own, windows[offset]]
        if last and not first:
            ins += [*dq_parts, own_terms]
        if last:
            outs = [shape((GROUP * HEAD_SIZE + 2 * rows, rows), BF16)] * parts
        else:
            outs = [shape((parts, HEAD_SIZE, width), F32)]
        outs = outs + [shape(kv_shape, BF16 if offset == behind > 0 else F32)]
        got = call(
            functools.partial(attend, rows, offset, reach, k, last),
            ins,
            outs,
            scratch=attend_scratch(rows),
            flops=10 * span * span * GROUP * HEAD_SIZE,
        )
        term = got[-1]
        if last:
            dq = got[:parts]
        else:
            dq_parts.append(got[0])
        if offset == 0:
            own_terms = term
        elif offset == 1:
            terms = (term,) if sent is None else (sent, term)
            groups = ((2, 3), (0,), (1,))
            got = call(
                functools.partial(cut_terms, rows, len(terms), groups),
                (place, *terms),
                [shape((2 * rows * len(group), HEAD_SIZE), BF16) for group in groups],
            )
            far, straight, beside = [move(piece, -1, group[0]) for piece, group in zip(got, groups)]
            sent = [straight, beside, far, move(far[2 * rows :], 0, 1)]
        elif sent is None:
            sent = move(term, -1, low=offset - 1)
        else:
            (term,) = call(add_terms, (place, sent, term), [shape(kv_shape, BF16)])
            sent = move(term, -1, low=offset - 1)

    dq_pieces = exchange(dq)
    query_grad, token = call(
        spread_queries,
        (place, *dq_pieces),
        [shape((rows, parts * GROUP * HEAD_SIZE), BF16), TOKEN],
        scratch=[
            pltpu.VMEM((parts, rows, GROUP * HEAD_SIZE), BF16),
            pltpu.SemaphoreType.DMA((parts,)),
        ],
        out_specs=[HBM, VMEM],
    )
    pieces = dq_pieces + (sent or [])
    key_grad, value_grad = call(
        functools.partial(spread_keys, rows, len(pieces) // parts),
        (place, *pieces, token),
        [shape((rows, parts * HEAD_SIZE), BF16)] * 2,
        scratch=[
            pltpu.VMEM((parts, 2 * rows, HEAD_SIZE), BF16),
            pltpu.SemaphoreType.DMA((parts, 2)),
        ],
        out_specs=[HBM, HBM],
    )
    return query_grad, key_grad, value_grad


def solution(mesh):
    axes = ("groups", "tok")
    return jax.shard_map(
        local,
        mesh=mesh,
        in_specs=(
            P(axes, None),
            P(axes, None),
            P(axes, None),
            P(axes, None),
            P(axes, None),
            P(None, axes),
            P(axes),
        ),
        out_specs=(P(axes, None), P(axes, None), P(axes, None)),
        check_vma=False,
    )
```
